128 devices in a mesh: ctx: 32 (over y_lo, z, x), tp: 4 (over y_hi, core).
Axes of the slice: x: 4, y: 4 (y_hi: 2, y_lo: 2; y = y_hi * 2 + y_lo), z: 4, core: 2. Of those that a mesh axis runs over, the one named last changes fastest.
Arguments:
- layer_input: float32 [4096, 1024], P('ctx'), may hold values from -6 to 6
- positions: int32 [4096], P('ctx'), may hold values from 0 to 4095, as said below
- attention_norm_gain: float32 [1024], replicated, may hold values from 0.5 to 1.5
- w_query: bfloat16 [1024, 2048], P(None, 'tp'), may hold values from -1 to 1
- key_projection: bfloat16 [1024, 1024], P(None, 'tp'), may hold values from -1 to 1
- value_projection: bfloat16 [1024, 1024], P(None, 'tp'), may hold values from -0.1875 to 0.1875
- query_norm: float32 [128], replicated, may hold values from 0.6 to 4.5
- key_norm_gain: float32 [128], replicated, may hold values from 0.6 to 4.5
- output_projection: bfloat16 [2048, 1024], P('tp'), may hold values from -2 to 2
- feedforward_norm_gain: float32 [1024], replicated, may hold values from 0.5 to 1.5
- w_gate: bfloat16 [1024, 3072], P(None, 'tp'), may hold values from -0.1875 to 0.1875
- w_up: bfloat16 [1024, 3072], P(None, 'tp'), may hold values from -0.1875 to 0.1875
- w_down: bfloat16 [3072, 1024], P('tp'), may hold values from -0.4375 to 0.4375
- output_cotangent: float32 [4096, 1024], P('ctx'), may hold values from -6 to 6
Outputs:
- hidden_out: float32 [4096, 1024], P('ctx')
- input_gradient: float32 [4096, 1024], P('ctx')
- attention_norm_gradient: float32 [1024], replicated
- grad_query: float32 [1024, 2048], P('ctx', 'tp')
- grad_key: float32 [1024, 1024], P('ctx', 'tp')
- grad_value: float32 [1024, 1024], P('ctx', 'tp')
- grad_query_norm: float32 [128], replicated
- grad_key_norm: float32 [128], replicated
- grad_output: float32 [2048, 1024], P('tp', 'ctx')
- feedforward_norm_gradient: float32 [1024], replicated
- grad_gate: float32 [1024, 3072], P('ctx', 'tp')
- grad_up: float32 [1024, 3072], P('ctx', 'tp')
- grad_down: float32 [3072, 1024], P('tp', 'ctx')
The draws below stay inside these ranges and needn't reach their ends.
Inputs may be any that keep to these rules, and one draw needn't show every extreme that they name: positions hold each of 0 to 4095 once; within each aligned block of 64 rows they rise by one from row to row.
All inputs are finite; a program needn't handle non-finite values.
Results may differ from the reference program's by a relative error of at most 0.038.
The reference program's roundings to bfloat16 on the way count: a program that leaves them out, or rounds other values in their place, can miss the bound.
Values may be sent and summed in bfloat16 or wider, within the bound.
A program may use at most 128 MiB of HBM per device.

```python
import math
import jax
import jax.numpy as jnp
from jax import lax

MODEL_WIDTH = 1024
QUERY_HEADS = 16
VALUE_HEADS_COUNT = 8
HEAD_SIZE = 128
FF = 3072
PBLK = 64
SEQUENCE_LENGTH = 4096


def draw_positions(key, part):
    blocks = SEQUENCE_LENGTH // PBLK
    block_order = jax.random.permutation(key, blocks).astype(jnp.int32)
    row_index = jnp.arange(SEQUENCE_LENGTH, dtype=jnp.int32)
    return block_order[row_index // PBLK] * PBLK + row_index % PBLK


def projection_pair(key):
    shared_terms = jax.random.fold_in(key, 7)
    query_sample = jax.random.normal(jax.random.fold_in(shared_terms, 1), (MODEL_WIDTH, QUERY_HEADS * HEAD_SIZE), jnp.float32)
    key_sample = jax.random.normal(jax.random.fold_in(shared_terms, 2), (MODEL_WIDTH, VALUE_HEADS_COUNT * HEAD_SIZE), jnp.float32)
    factor = 1.0 / math.sqrt(MODEL_WIDTH)
    return (jnp.clip(query_sample, -6.0, 6.0) * factor, jnp.clip(key_sample, -6.0, 6.0) * factor)


def draw_w_query(key, part):
    query_sample, key_sample = projection_pair(key)
    return query_sample.astype(jnp.bfloat16)


def draw_key_projection(key, part):
    query_sample, key_sample = projection_pair(key)
    return key_sample.astype(jnp.bfloat16)


def gain_between(key, lower, upper):
    spread = jax.random.uniform(key, (HEAD_SIZE,), jnp.float32, math.log(lower), math.log(upper))
    return jnp.exp(spread)


def draw_query_norm(key, part):
    return gain_between(jax.random.fold_in(key, 11), 0.6, 3.0)


def draw_key_norm_gain(key, part):
    return gain_between(jax.random.fold_in(key, 12), 0.6, 3.0)


def draw_layer_input(key, part):
    base = jax.random.normal(jax.random.fold_in(key, 13), (SEQUENCE_LENGTH, MODEL_WIDTH), jnp.float32)
    return jnp.clip(base, -6.0, 6.0)


def block_scale(rng, shape, pieces, low, largest):
    loudness = 1.0
    for dim, shards_of in pieces:
        draws = jax.random.uniform(jax.random.fold_in(jax.random.fold_in(rng, 6), dim), (shards_of,), jnp.float32, low / len(pieces), largest / len(pieces))
        loudness = loudness * jnp.repeat(jnp.exp(draws), shape[dim] // shards_of).reshape((-1,) + (1,) * (len(shape) - 1 - dim))
    return loudness


def centred(rng, dims, deviation, most, pieces=(), kind=jnp.bfloat16):
    loudness = block_scale(rng, dims, pieces, -0.22, 0.18) if pieces else 1.0
    drawn = jax.random.normal(rng, dims, jnp.float32) * deviation * loudness
    return jnp.minimum(jnp.maximum(drawn, -most), most).astype(kind)


def setup_inputs(seed: int = 0) -> dict:
    arg_keys = jax.random.split(jax.random.key(seed), 15)
    return {
        "layer_input": draw_layer_input(jax.random.fold_in(arg_keys[14], 71), 0),
        "positions": draw_positions(jax.random.fold_in(arg_keys[14], 71), 0),
        "attention_norm_gain": jnp.clip(1.0 + 0.1 * jax.random.normal(arg_keys[2], (MODEL_WIDTH,), jnp.float32), 0.5, 1.5),
        "w_query": draw_w_query(jax.random.fold_in(arg_keys[14], 71), 0),
        "key_projection": draw_key_projection(jax.random.fold_in(arg_keys[14], 71), 0),
        "value_projection": centred(arg_keys[5], (MODEL_WIDTH, VALUE_HEADS_COUNT * HEAD_SIZE), MODEL_WIDTH ** -0.5, 0.1875, ((1, 4),)),
        "query_norm": draw_query_norm(jax.random.fold_in(arg_keys[14], 71), 0),
        "key_norm_gain": draw_key_norm_gain(jax.random.fold_in(arg_keys[14], 71), 0),
        "output_projection": centred(arg_keys[8], (QUERY_HEADS * HEAD_SIZE, MODEL_WIDTH), (QUERY_HEADS * HEAD_SIZE // 256) ** -0.5, 2.0, ((0, 4),)),
        "feedforward_norm_gain": jnp.clip(1.0 + 0.1 * jax.random.normal(arg_keys[9], (MODEL_WIDTH,), jnp.float32), 0.5, 1.5),
        "w_gate": centred(arg_keys[10], (MODEL_WIDTH, FF), MODEL_WIDTH ** -0.5, 0.1875, ((1, 4),)),
        "w_up": centred(arg_keys[11], (MODEL_WIDTH, FF), MODEL_WIDTH ** -0.5, 0.1875, ((1, 4),)),
        "w_down": centred(arg_keys[12], (FF, MODEL_WIDTH), (FF // 16) ** -0.5, 0.4375, ((0, 4),)),
        "output_cotangent": centred(arg_keys[13], (SEQUENCE_LENGTH, MODEL_WIDTH), 1.0, 6.0, ((0, 32),), jnp.float32),
    }


EPSILON = 1e-06
ROPE_BASE = 1000000.0
MASKED = -1e+30

def rms_scale(values):
    return lax.rsqrt(lax.optimization_barrier(jnp.mean(values * values, axis=-1, keepdims=True)) + EPSILON)

def norm_backward(grad, normed, scale_rows):
    return scale_rows * (grad - normed * lax.optimization_barrier(jnp.mean(grad * normed, axis=-1, keepdims=True)))

def rope_tables(positions):
    half_dim = HEAD_SIZE // 2
    freqs = jnp.exp(-(2.0 * jnp.arange(half_dim, dtype=jnp.float32) / HEAD_SIZE) * math.log(ROPE_BASE))
    angles = positions.astype(jnp.float32)[:, None] * freqs[None, :]
    return (jnp.cos(angles)[:, None, :], jnp.sin(angles)[:, None, :])

def rotate_pairs(values, cosine, sine):
    half_dim = values.shape[-1] // 2
    first = values[..., :half_dim]
    second = values[..., half_dim:]
    return jnp.concatenate([first * cosine - second * sine, second * cosine + first * sine], axis=-1)

def rotate_back(grad, cosine, sine):
    half_dim = grad.shape[-1] // 2
    first = grad[..., :half_dim]
    second = grad[..., half_dim:]
    return jnp.concatenate([first * cosine + second * sine, second * cosine - first * sine], axis=-1)

def bround(values):
    return lax.optimization_barrier(values.astype(jnp.bfloat16)).astype(jnp.float32)

def reference(layer_input, positions, attention_norm_gain, w_query, key_projection, value_projection, query_norm, key_norm_gain, output_projection, feedforward_norm_gain, w_gate, w_up, w_down, output_cotangent):
    query_groups = QUERY_HEADS // VALUE_HEADS_COUNT
    inv_root = 1.0 / math.sqrt(HEAD_SIZE)
    block = math.gcd(SEQUENCE_LENGTH, 512)
    nblocks = SEQUENCE_LENGTH // block
    first_inverse_norm = rms_scale(layer_input)
    first_normalized = layer_input * first_inverse_norm
    first_normed = (first_normalized * attention_norm_gain).astype(jnp.bfloat16)
    queries = jnp.dot(first_normed, w_query, preferred_element_type=jnp.float32).reshape(SEQUENCE_LENGTH, QUERY_HEADS, HEAD_SIZE)
    unnormed_keys = jnp.dot(first_normed, key_projection, preferred_element_type=jnp.float32).reshape(SEQUENCE_LENGTH, VALUE_HEADS_COUNT, HEAD_SIZE)
    value_block = jnp.dot(first_normed, value_projection, preferred_element_type=jnp.float32).astype(jnp.bfloat16)
    r_query = rms_scale(queries)
    qhat = queries * r_query
    key_inverse_norm = rms_scale(unnormed_keys)
    normalized_keys = unnormed_keys * key_inverse_norm
    cosine, sine = rope_tables(positions)
    rotated_queries = rotate_pairs(qhat * query_norm, cosine, sine).astype(jnp.bfloat16)
    k_rot = rotate_pairs(normalized_keys * key_norm_gain, cosine, sine).astype(jnp.bfloat16)
    query_rows_full = rotated_queries.astype(jnp.float32).reshape(SEQUENCE_LENGTH, VALUE_HEADS_COUNT, query_groups, HEAD_SIZE)
    k_all = k_rot.astype(jnp.float32)
    value_rows_full = value_block.astype(jnp.float32).reshape(SEQUENCE_LENGTH, VALUE_HEADS_COUNT, HEAD_SIZE)

    def block_scores(block_index):
        offset = block_index * block
        q_blk = lax.dynamic_slice_in_dim(query_rows_full, offset, block, 0)
        pos_blk = lax.dynamic_slice_in_dim(positions, offset, block, 0)
        scores = jnp.einsum('tkgd,nkd->kgtn', q_blk, k_all) * inv_root
        causal = pos_blk[:, None] >= positions[None, :]
        return (q_blk, jnp.where(causal[None, None], scores, MASKED))

    def attend(block_index):
        q_blk, scores = block_scores(block_index)
        row_max = lax.optimization_barrier(jnp.max(scores, axis=-1))
        weights = jnp.exp(scores - row_max[..., None])
        row_sum = lax.optimization_barrier(jnp.sum(weights, axis=-1))
        mixed = jnp.einsum('kgtn,nkd->kgtd', bround(weights), value_rows_full) / row_sum[..., None]
        return (jnp.transpose(mixed, (2, 0, 1, 3)), row_max + jnp.log(row_sum))
    block_ids = jnp.arange(nblocks, dtype=jnp.int32)
    attention_blocks, log_sums = lax.map(attend, block_ids)
    attention_single = attention_blocks.reshape(SEQUENCE_LENGTH, VALUE_HEADS_COUNT, query_groups, HEAD_SIZE)
    att_b = attention_single.astype(jnp.bfloat16).reshape(SEQUENCE_LENGTH, QUERY_HEADS * HEAD_SIZE)
    middle_hidden = layer_input + jnp.dot(att_b, output_projection, preferred_element_type=jnp.float32)
    second_inverse_norm = rms_scale(middle_hidden)
    second_normalized = middle_hidden * second_inverse_norm
    second_normed = (second_normalized * feedforward_norm_gain).astype(jnp.bfloat16)
    gate = jnp.dot(second_normed, w_gate, preferred_element_type=jnp.float32)
    up_val = jnp.dot(second_normed, w_up, preferred_element_type=jnp.float32)
    sig_gate = jax.nn.sigmoid(gate)
    silu_gate = gate * sig_gate
    hid = (silu_gate * up_val).astype(jnp.bfloat16)
    hidden_out = middle_hidden + jnp.dot(hid, w_down, preferred_element_type=jnp.float32)
    grad_out_b = output_cotangent.astype(jnp.bfloat16)
    grad_down = jnp.dot(hid.T, grad_out_b, preferred_element_type=jnp.float32)
    d_hid = jnp.dot(grad_out_b, w_down.T, preferred_element_type=jnp.float32)
    d_gate = (d_hid * up_val * sig_gate * (1.0 + gate * (1.0 - sig_gate))).astype(jnp.bfloat16)
    d_up = (d_hid * silu_gate).astype(jnp.bfloat16)
    grad_gate = jnp.dot(second_normed.T, d_gate, preferred_element_type=jnp.float32)
    grad_up = jnp.dot(second_normed.T, d_up, preferred_element_type=jnp.float32)
    second_normed_gradient = jnp.dot(d_gate, w_gate.T, preferred_element_type=jnp.float32) + jnp.dot(d_up, w_up.T, preferred_element_type=jnp.float32)
    feedforward_norm_gradient = lax.optimization_barrier(jnp.sum(second_normed_gradient * second_normalized, axis=0))
    middle_gradient = output_cotangent + norm_backward(second_normed_gradient * feedforward_norm_gain, second_normalized, second_inverse_norm)
    middle_gradient_block = middle_gradient.astype(jnp.bfloat16)
    grad_output = jnp.dot(att_b.T, middle_gradient_block, preferred_element_type=jnp.float32)
    attention_gradient = jnp.dot(middle_gradient_block, output_projection.T, preferred_element_type=jnp.float32).reshape(SEQUENCE_LENGTH, VALUE_HEADS_COUNT, query_groups, HEAD_SIZE)
    delta = lax.optimization_barrier(jnp.sum(attention_gradient * attention_single, axis=-1))
    d_attn_b = bround(attention_gradient)

    def attend_back(carry, block_index):
        dk_acc, dv_acc = carry
        offset = block_index * block
        q_blk, scores = block_scores(block_index)
        lse = log_sums[block_index]
        do_blk = lax.dynamic_slice_in_dim(d_attn_b, offset, block, 0)
        delta_blk = jnp.transpose(lax.dynamic_slice_in_dim(delta, offset, block, 0), (1, 2, 0))
        probs = jnp.exp(scores - lse[..., None])
        d_prob = jnp.einsum('tkgd,nkd->kgtn', do_blk, value_rows_full)
        d_score = probs * (d_prob - delta_blk[..., None])
        ds_b = bround(d_score)
        prob_b = bround(probs)
        dq_blk = jnp.einsum('kgtn,nkd->tkgd', ds_b, k_all) * inv_root
        dk_acc = dk_acc + jnp.einsum('kgtn,tkgd->nkd', ds_b, q_blk) * inv_root
        dv_acc = dv_acc + jnp.einsum('kgtn,tkgd->nkd', prob_b, do_blk)
        return ((dk_acc, dv_acc), dq_blk)
    empty_key_value = jnp.zeros((SEQUENCE_LENGTH, VALUE_HEADS_COUNT, HEAD_SIZE), jnp.float32)
    (dk_sum, value_gradient_sum), dq_blocks = lax.scan(attend_back, (empty_key_value, empty_key_value), block_ids)
    d_qn = rotate_back(dq_blocks.reshape(SEQUENCE_LENGTH, QUERY_HEADS, HEAD_SIZE), cosine, sine)
    grad_query_norm = lax.optimization_barrier(jnp.sum(d_qn * qhat, axis=(0, 1)))
    dq_b = norm_backward(d_qn * query_norm, qhat, r_query).astype(jnp.bfloat16).reshape(SEQUENCE_LENGTH, QUERY_HEADS * HEAD_SIZE)
    normed_key_gradient = rotate_back(dk_sum, cosine, sine)
    grad_key_norm = lax.optimization_barrier(jnp.sum(normed_key_gradient * normalized_keys, axis=(0, 1)))
    key_gradient_block = norm_backward(normed_key_gradient * key_norm_gain, normalized_keys, key_inverse_norm).astype(jnp.bfloat16).reshape(SEQUENCE_LENGTH, VALUE_HEADS_COUNT * HEAD_SIZE)
    value_gradient_block = value_gradient_sum.astype(jnp.bfloat16).reshape(SEQUENCE_LENGTH, VALUE_HEADS_COUNT * HEAD_SIZE)
    grad_query = jnp.dot(first_normed.T, dq_b, preferred_element_type=jnp.float32)
    grad_key = jnp.dot(first_normed.T, key_gradient_block, preferred_element_type=jnp.float32)
    grad_value = jnp.dot(first_normed.T, value_gradient_block, preferred_element_type=jnp.float32)
    first_normed_gradient = jnp.dot(dq_b, w_query.T, preferred_element_type=jnp.float32)
    first_normed_gradient = first_normed_gradient + jnp.dot(key_gradient_block, key_projection.T, preferred_element_type=jnp.float32)
    first_normed_gradient = first_normed_gradient + jnp.dot(value_gradient_block, value_projection.T, preferred_element_type=jnp.float32)
    attention_norm_gradient = lax.optimization_barrier(jnp.sum(first_normed_gradient * first_normalized, axis=0))
    input_gradient = middle_gradient + norm_backward(first_normed_gradient * attention_norm_gain, first_normalized, first_inverse_norm)
    return (hidden_out, input_gradient, attention_norm_gradient, grad_query, grad_key, grad_value, grad_query_norm, grad_key_norm, grad_output, feedforward_norm_gradient, grad_gate, grad_up, grad_down)
```

```python
import math

import jax
import jax.numpy as jnp
from jax import lax
from jax.experimental import pallas as pl
from jax.experimental.pallas import tpu as pltpu
from jax.sharding import PartitionSpec as P

EPSILON = 1e-06
ROPE_BASE = 1000000.0
MASKED = -1e30


MESH = pl.DeviceIdType.MESH
SIZES = {"y": 2, "z": 4, "x": 4}
DIMS = ("y", "z", "x")


def place():
    me = lax.axis_index("ctx")
    return {"y": me // 16, "z": lax.rem(me // 4, 4), "x": lax.rem(me, 4)}, lax.axis_index("tp")


def shifted(coords, dim, step):
    moved = dict(coords)
    moved[dim] = lax.rem(coords[dim] + step + SIZES[dim], SIZES[dim])
    return moved


def device_at(coords, tp):
    return (coords["y"] * 16 + coords["z"] * 4 + coords["x"], tp)


def torus_peers(coords, tp):
    peers = [device_at(shifted(coords, "y", 1), tp)]
    for dim in ("z", "x"):
        peers.append(device_at(shifted(coords, dim, 1), tp))
        peers.append(device_at(shifted(coords, dim, -1), tp))
    return peers


def greet(peers):
    barrier = pltpu.get_barrier_semaphore()
    for peer in peers:
        pl.semaphore_signal(barrier, inc=1, device_id=peer, device_id_type=MESH)
    pl.semaphore_wait(barrier, len(peers))


class Copies:
    def __init__(self, send_sem, recv_sem):
        self.send_sem, self.recv_sem = send_sem, recv_sem
        self.count = 0
        self.started = []

    def make(self, source, target, device):
        slot = self.count
        self.count += 1
        return pltpu.make_async_remote_copy(
            src_ref=source,
            dst_ref=target,
            send_sem=self.send_sem.at[slot],
            recv_sem=self.recv_sem.at[slot],
            device_id=device,
            device_id_type=MESH,
        )

    def send(self, source, target, device):
        copy = self.make(source, target, device)
        copy.start()
        self.started.append(copy)
        return copy

    def drain(self):
        for copy in self.started:
            copy.wait_send()


def run_together(flows):
    live = list(flows)
    while live:
        left = []
        for flow in live:
            try:
                next(flow)
                left.append(flow)
            except StopIteration:
                pass
        live = left


def gather_flow(copies, coords, tp, ref, order, piece, halves):
    def region(held, where, part):
        index = tuple(slice(None) if dim in held else where[dim] for dim in DIMS)
        return ref.at[index + part]

    held = []
    for dim in order:
        right = device_at(shifted(coords, dim, 1), tp)
        mine = region(held, coords, piece)
        if SIZES[dim] == 2:
            copy = copies.send(mine, mine, right)
            yield
            copy.wait_recv()
        else:
            left = device_at(shifted(coords, dim, -1), tp)
            go_right = copies.send(mine, mine, right)
            go_left = copies.send(mine, mine, left)
            yield
            go_right.wait_recv()
            block = region(held, shifted(coords, dim, -1), halves[0])
            pass_right = copies.send(block, block, right)
            pass_left = None
            if halves[1] is not None:
                go_left.wait_recv()
                block = region(held, shifted(coords, dim, 1), halves[1])
                pass_left = copies.send(block, block, left)
            yield
            pass_right.wait_recv()
            if pass_left is None:
                go_left.wait_recv()
            else:
                pass_left.wait_recv()
        held.append(dim)


GATHER_PARTS = ((("y", "z", "x"), 0, 48), (("x", "y", "z"), 48, 48), (("z", "x", "y"), 96, 32))


def gather_kernel(kv_ref, pos_ref, out_ref, pos_out_ref, send_sem, recv_sem, local_sem):
    coords, tp = place()
    greet(torus_peers(coords, tp))
    own = (coords["y"], coords["z"], coords["x"])
    keep = pltpu.make_async_copy(kv_ref, out_ref.at[own], local_sem.at[0])
    keep_pos = pltpu.make_async_copy(pos_ref, pos_out_ref.at[own], local_sem.at[1])
    keep.start()
    keep_pos.start()
    keep.wait()
    keep_pos.wait()
    copies = Copies(send_sem, recv_sem)
    width = kv_ref.shape[1] // 2
    flows = []
    for order, first, count in GATHER_PARTS:
        rows = pl.ds(first, count)
        flows.append(
            gather_flow(
                copies,
                coords,
                tp,
                out_ref,
                order,
                (rows, slice(None)),
                ((rows, pl.ds(0, width)), (rows, pl.ds(width, width))),
            )
        )
    whole = (slice(None), slice(None))
    flows.append(
        gather_flow(copies, coords, tp, pos_out_ref, ("y", "z", "x"), whole, (whole, None))
    )
    run_together(flows)
    copies.drain()


def gather_all(kv_block, positions):
    rows, width = kv_block.shape
    vmem = pl.BlockSpec(memory_space=pltpu.VMEM)
    everything, all_pos = pl.pallas_call(
        gather_kernel,
        out_shape=(
            jax.ShapeDtypeStruct((2, 4, 4, rows, width), kv_block.dtype),
            jax.ShapeDtypeStruct((2, 4, 4, 1, rows), jnp.int32),
        ),
        in_specs=[vmem, vmem],
        out_specs=(vmem, vmem),
        scratch_shapes=[
            pltpu.SemaphoreType.DMA((40,)),
            pltpu.SemaphoreType.DMA((40,)),
            pltpu.SemaphoreType.DMA((2,)),
        ],
        compiler_params=pltpu.CompilerParams(
            collective_id=0, has_side_effects=True, vmem_limit_bytes=24 << 20
        ),
        name="gather_keys_values",
    )(kv_block, positions.reshape(1, rows))
    return everything.reshape(32 * rows, width), all_pos.reshape(32 * rows)


def leading_index(flat, dims):
    index = []
    for dim in reversed(dims):
        index.insert(0, lax.rem(flat, SIZES[dim]))
        flat = flat // SIZES[dim]
    return tuple(index)


def leading_shape(dims):
    return tuple(SIZES[dim] for dim in dims)


def over_leading(dims, step):
    count = math.prod(leading_shape(dims))
    if count == 1:
        step(())
        return

    def body(flat, carry):
        step(leading_index(flat, dims))
        return carry

    lax.fori_loop(0, count, body, 0)


def scatter_scratch(shape, order, axis):
    half = tuple(size // 2 if i == axis else size for i, size in enumerate(shape))
    buffers = []
    rest = list(DIMS)
    for dim in order:
        rest.remove(dim)
        lead = leading_shape(rest)
        if SIZES[dim] == 2:
            buffers.append(pltpu.VMEM(lead + shape, jnp.bfloat16))
        else:
            buffers.extend([pltpu.VMEM(lead + half, jnp.bfloat16)] * 8)
        if rest:
            buffers.append(pltpu.VMEM(lead + shape, jnp.bfloat16))
    return buffers


def scatter_flow(copies, coords, tp, source, result, buffers, order, axis):
    buffers = list(buffers)
    shape = source.shape[-2:]
    size = shape[axis] // 2
    halves = [
        tuple(pl.ds(h * size, size) if i == axis else slice(None) for i in range(2))
        for h in range(2)
    ]
    whole = (slice(None), slice(None))
    current = source
    dims = list(DIMS)

    for dim in order:
        rest = [d for d in dims if d != dim]
        spot = dims.index(dim)

        def at(where, lead, part, spot=spot, current=current):
            index = tuple(lead[:spot]) + (where[dim],) + tuple(lead[spot:])
            return current.at[index + part]

        everywhere = (slice(None),) * len(rest)
        right_coords = shifted(coords, dim, 1)
        right = device_at(right_coords, tp)
        f32 = jnp.float32
        if SIZES[dim] == 2:
            landed = buffers.pop(0)
            copy = copies.send(at(right_coords, everywhere, whole), landed, right)
            target = buffers.pop(0) if rest else result
            yield
            copy.wait_recv()

            def add(lead):
                total = at(coords, lead, whole)[...].astype(f32) + landed[lead + whole].astype(f32)
                target[lead + whole] = total.astype(target.dtype)

            over_leading(rest, add)
        else:
            left_coords = shifted(coords, dim, -1)
            far_coords = shifted(coords, dim, 2)
            left = device_at(left_coords, tp)
            pass_l, pass_r, near_l, near_r, sum_l, sum_r, out_r, out_l = buffers[:8]
            buffers = buffers[8:]
            target = buffers.pop(0) if rest else result
            relay_r = copies.send(at(far_coords, everywhere, halves[0]), pass_l, right)
            relay_l = copies.send(at(far_coords, everywhere, halves[1]), pass_r, left)
            direct_r = copies.send(at(right_coords, everywhere, halves[1]), near_l, right)
            direct_l = copies.send(at(left_coords, everywhere, halves[0]), near_r, left)
            yield
            relay_r.wait_recv()

            def merge_right(lead):
                total = at(right_coords, lead, halves[0])[...].astype(f32) + pass_l[
                    lead + whole
                ].astype(f32)
                out_r[lead + whole] = total.astype(out_r.dtype)

            over_leading(rest, merge_right)
            merged_r = copies.send(out_r, sum_l, right)
            relay_l.wait_recv()

            def merge_left(lead):
                total = at(left_coords, lead, halves[1])[...].astype(f32) + pass_r[
                    lead + whole
                ].astype(f32)
                out_l[lead + whole] = total.astype(out_l.dtype)

            over_leading(rest, merge_left)
            merged_l = copies.send(out_l, sum_r, left)
            yield
            direct_r.wait_recv()
            direct_l.wait_recv()
            merged_r.wait_recv()
            merged_l.wait_recv()

            def add(lead):
                for half, one, two in ((halves[0], sum_l, near_r), (halves[1], near_l, sum_r)):
                    total = (
                        at(coords, lead, half)[...].astype(f32)
                        + one[lead + whole].astype(f32)
                        + two[lead + whole].astype(f32)
                    )
                    target[lead + half] = total.astype(target.dtype)

            over_leading(rest, add)
        current = target
        dims = rest


def sum_everywhere_flow(copies, coords, tp, source, result, slots):
    current = source
    for stage, dim in enumerate(("x", "z")):
        ring = slots[stage]
        left = device_at(shifted(coords, dim, -1), tp)
        right = device_at(shifted(coords, dim, 1), tp)
        spot = coords[dim]
        ring[spot] = current[...]
        go_right = copies.send(current, ring.at[spot], right)
        go_left = copies.send(current, ring.at[spot], left)
        yield
        go_right.wait_recv()
        block = ring.at[shifted(coords, dim, -1)[dim]]
        passed = copies.send(block, block, right)
        yield
        go_left.wait_recv()
        passed.wait_recv()
        total = slots[5 + stage]
        total[...] = ring[0] + ring[1] + ring[2] + ring[3]
        current = total
    partners = (
        device_at(shifted(coords, "y", 1), tp),
        (lax.axis_index("ctx"), tp + 1 - 2 * lax.rem(tp, 2)),
        (lax.axis_index("ctx"), lax.rem(tp + 2, 4)),
    )
    for stage, partner in enumerate(partners):
        landed = slots[2 + stage]
        copy = copies.send(current, landed, partner)
        yield
        copy.wait_recv()
        total = slots[7 + stage] if stage < 2 else result
        total[...] = current[...] + landed[...]
        current = total


def sum_everywhere_scratch(shape):
    return [pltpu.VMEM((4,) + shape, jnp.float32)] * 2 + [pltpu.VMEM(shape, jnp.float32)] * 7


def reduce_scatter_all(arrays, orders, axes, out_dtype, collective_id, name, small=None):
    shapes = [array.shape[1:] for array in arrays]
    counts = [
        len(scatter_scratch(shape, order, axis))
        for shape, order, axis in zip(shapes, orders, axes)
    ]
    number = len(arrays)
    extra = 0 if small is None else 1

    def kernel(*refs):
        ins = refs[: number + extra]
        outs = refs[number + extra : 2 * (number + extra)]
        scratch = refs[2 * (number + extra) :]
        send_sem, recv_sem = scratch[:2]
        scratch = scratch[2:]
        coords, tp = place()
        peers = torus_peers(coords, tp)
        if extra:
            peers.append((lax.axis_index("ctx"), tp + 1 - 2 * lax.rem(tp, 2)))
            peers.append((lax.axis_index("ctx"), lax.rem(tp + 2, 4)))
        greet(peers)
        copies = Copies(send_sem, recv_sem)
        flows = []
        begin = 0
        for i in range(number):
            buffers = scratch[begin : begin + counts[i]]
            begin += counts[i]
            flows.append(
                scatter_flow(copies, coords, tp, ins[i], outs[i], buffers, orders[i], axes[i])
            )
        if extra:
            flows.append(
                sum_everywhere_flow(copies, coords, tp, ins[number], outs[number], scratch[begin:])
            )
        run_together(flows)
        copies.drain()

    vmem = pl.BlockSpec(memory_space=pltpu.VMEM)
    copies_needed = number * 13 + extra * 9
    scratch_shapes = [pltpu.SemaphoreType.DMA((copies_needed,))] * 2
    for shape, order, axis in zip(shapes, orders, axes):
        scratch_shapes.extend(scatter_scratch(shape, order, axis))
    out_shape = [jax.ShapeDtypeStruct(shape, out_dtype) for shape in shapes]
    operands = [array.reshape((2, 4, 4) + shape) for array, shape in zip(arrays, shapes)]
    if extra:
        scratch_shapes.extend(sum_everywhere_scratch(small.shape))
        out_shape.append(jax.ShapeDtypeStruct(small.shape, jnp.float32))
        operands.append(small)
    return pl.pallas_call(
        kernel,
        out_shape=tuple(out_shape),
        in_specs=[vmem] * len(operands),
        out_specs=(vmem,) * len(out_shape),
        scratch_shapes=scratch_shapes,
        compiler_params=pltpu.CompilerParams(
            collective_id=collective_id, has_side_effects=True, vmem_limit_bytes=60 << 20
        ),
        name=name,
    )(*operands)


def tp_sum_flow(copies, ins, out, landed, chip, far, partner_core, partner_far, core, first, count, rows):
    half = rows // 2
    mine = pl.ds(pl.multiple_of(core * half + first, 16), count)
    theirs = pl.ds(pl.multiple_of((1 - core) * half + first, 16), count)
    local = pl.ds(first, count)
    f32 = jnp.float32
    copy = copies.send(ins.at[theirs], landed.at[local], partner_core)
    yield
    copy.wait_recv()
    chip[local] = (ins[mine].astype(f32) + landed[local].astype(f32)).astype(chip.dtype)
    copy = copies.send(chip.at[local], far.at[local], partner_far)
    yield
    copy.wait_recv()
    out[mine] = (chip[local].astype(f32) + far[local].astype(f32)).astype(out.dtype)
    copy = copies.send(out.at[mine], out.at[mine], partner_core)
    yield
    copy.wait_recv()


def tp_sum(parts, collective_id, pieces=2):
    number = len(parts)
    rows, columns = parts[0].shape
    half = rows // 2

    def kernel(*refs):
        ins, outs = refs[:number], refs[number : 2 * number]
        send_sem, recv_sem = refs[2 * number : 2 * number + 2]
        scratch = refs[2 * number + 2 :]
        tp = lax.axis_index("tp")
        ctx = lax.axis_index("ctx")
        core = lax.rem(tp, 2)
        partner_core = (ctx, tp + 1 - 2 * core)
        partner_far = (ctx, lax.rem(tp + 2, 4))
        greet([partner_core, partner_far])
        copies = Copies(send_sem, recv_sem)
        flows = []
        count = half // pieces
        for i in range(number):
            landed, chip, far = scratch[3 * i : 3 * i + 3]
            for piece in range(pieces):
                flows.append(
                    tp_sum_flow(
                        copies, ins[i], outs[i], landed, chip, far, partner_core, partner_far,
                        core, piece * count, count, rows,
                    )
                )
        run_together(flows)
        copies.drain()

    vmem = pl.BlockSpec(memory_space=pltpu.VMEM)
    return pl.pallas_call(
        kernel,
        out_shape=tuple(jax.ShapeDtypeStruct(part.shape, part.dtype) for part in parts),
        in_specs=[vmem] * number,
        out_specs=(vmem,) * number,
        scratch_shapes=[pltpu.SemaphoreType.DMA((3 * pieces * number,))] * 2
        + [pltpu.VMEM((half, columns), jnp.bfloat16)] * (3 * number),
        compiler_params=pltpu.CompilerParams(
            collective_id=collective_id, has_side_effects=True, vmem_limit_bytes=24 << 20
        ),
        name="tp_sum",
    )(*parts)


def rms_scale(values):
    return lax.rsqrt(jnp.mean(values * values, axis=-1, keepdims=True) + EPSILON)


def norm_backward(grad, normed, scale_rows):
    return scale_rows * (grad - normed * jnp.mean(grad * normed, axis=-1, keepdims=True))


def rope_tables(positions, head_dim):
    half_dim = head_dim // 2
    freqs = jnp.exp(
        -(2.0 * jnp.arange(half_dim, dtype=jnp.float32) / head_dim) * math.log(ROPE_BASE)
    )
    angles = positions.astype(jnp.float32)[:, None] * freqs[None, :]
    return (jnp.cos(angles)[:, None, :], jnp.sin(angles)[:, None, :])


def rotate_pairs(values, cosine, sine):
    half_dim = values.shape[-1] // 2
    first = values[..., :half_dim]
    second = values[..., half_dim:]
    return jnp.concatenate(
        [first * cosine - second * sine, second * cosine + first * sine], axis=-1
    )


def rotate_back(grad, cosine, sine):
    half_dim = grad.shape[-1] // 2
    first = grad[..., :half_dim]
    second = grad[..., half_dim:]
    return jnp.concatenate(
        [first * cosine + second * sine, second * cosine - first * sine], axis=-1
    )


def scores_for(rotated_queries, key_piece, q_pos, key_pos, inv_root):
    count = key_piece.shape[0]
    key_heads = key_piece.reshape(count, rotated_queries.shape[1], rotated_queries.shape[3])
    scores = (
        jnp.einsum("tkgd,nkd->kgtn", rotated_queries, key_heads, preferred_element_type=jnp.float32)
        * inv_root
    )
    causal = q_pos[:, None] >= key_pos[None, :]
    return jnp.where(causal[None, None], scores, MASKED)


def in_blocks(step_fn, carry, pieces):
    count = pieces[0].shape[0]
    size = math.gcd(count, 1024)

    def inner_step(current, block_index):
        begin = block_index * size
        sub_pieces = (
            lax.dynamic_slice_in_dim(pieces[0], begin, size, 0),
            lax.dynamic_slice_in_dim(pieces[1], begin, size, 0),
        )
        return (step_fn(current, sub_pieces, begin), None)

    result, unused = lax.scan(inner_step, carry, jnp.arange(count // size, dtype=jnp.int32))
    return result


def body(
    layer_input,
    positions,
    attention_norm_gain,
    w_query,
    key_projection,
    value_projection,
    query_norm,
    key_norm_gain,
    output_projection,
    feedforward_norm_gain,
    w_gate,
    w_up,
    w_down,
    output_cotangent,
):
    rows = layer_input.shape[0]
    head_dim = query_norm.shape[0]
    heads_q = w_query.shape[1] // head_dim
    heads_kv = key_projection.shape[1] // head_dim
    query_groups = heads_q // heads_kv
    inv_root = 1.0 / math.sqrt(head_dim)
    total = rows * lax.axis_size("ctx")
    first_inverse_norm = rms_scale(layer_input)
    first_normalized = layer_input * first_inverse_norm
    first_normed = (first_normalized * attention_norm_gain).astype(jnp.bfloat16)
    queries = jnp.dot(first_normed, w_query, preferred_element_type=jnp.float32).reshape(
        rows, heads_q, head_dim
    )
    unnormed_keys = jnp.dot(
        first_normed, key_projection, preferred_element_type=jnp.float32
    ).reshape(rows, heads_kv, head_dim)
    value_block = jnp.dot(
        first_normed, value_projection, preferred_element_type=jnp.float32
    ).astype(jnp.bfloat16)
    r_query = rms_scale(queries)
    qhat = queries * r_query
    key_inverse_norm = rms_scale(unnormed_keys)
    normalized_keys = unnormed_keys * key_inverse_norm
    cosine, sine = rope_tables(positions, head_dim)
    rotated_queries = (
        rotate_pairs(qhat * query_norm, cosine, sine)
        .astype(jnp.bfloat16)
        .reshape(rows, heads_kv, query_groups, head_dim)
    )
    k_rot = (
        rotate_pairs(normalized_keys * key_norm_gain, cosine, sine)
        .astype(jnp.bfloat16)
        .reshape(rows, heads_kv * head_dim)
    )

    kv_all, all_pos = gather_all(jnp.concatenate([k_rot, value_block], axis=1), positions)
    keys_all, values_all = kv_all[:, : heads_kv * head_dim], kv_all[:, heads_kv * head_dim :]

    def forward_step(carry, pieces, offset):
        run_max, run_sum, accum = carry
        key_piece, value_piece = pieces
        count = key_piece.shape[0]
        key_pos = lax.dynamic_slice_in_dim(all_pos, offset, count, 0)
        scores = scores_for(rotated_queries, key_piece, positions, key_pos, inv_root)
        new_max = jnp.maximum(run_max, jnp.max(scores, axis=-1))
        factor = jnp.exp(run_max - new_max)
        weights = jnp.exp(scores - new_max[..., None])
        run_sum = run_sum * factor + jnp.sum(weights, axis=-1)
        value_heads = value_piece.reshape(count, heads_kv, head_dim)
        accum = accum * factor[..., None] + jnp.einsum(
            "kgtn,nkd->kgtd",
            weights.astype(jnp.bfloat16),
            value_heads,
            preferred_element_type=jnp.float32,
        )
        return (new_max, run_sum, accum)

    start_state = (
        jnp.full((heads_kv, query_groups, rows), MASKED, jnp.float32),
        jnp.zeros((heads_kv, query_groups, rows), jnp.float32),
        jnp.zeros((heads_kv, query_groups, rows, head_dim), jnp.float32),
    )
    state = in_blocks(
        forward_step,
        start_state,
        (keys_all, values_all),
    )
    run_max, run_sum, accum = state
    attention_single = jnp.transpose(accum / run_sum[..., None], (2, 0, 1, 3))
    log_sums = run_max + jnp.log(run_sum)
    att_b = attention_single.astype(jnp.bfloat16).reshape(rows, heads_q * head_dim)
    (attention_out,) = tp_sum(
        [jnp.dot(att_b, output_projection, preferred_element_type=jnp.float32).astype(jnp.bfloat16)],
        2,
    )
    middle_hidden = layer_input + attention_out.astype(jnp.float32)
    second_inverse_norm = rms_scale(middle_hidden)
    second_normalized = middle_hidden * second_inverse_norm
    second_normed = (second_normalized * feedforward_norm_gain).astype(jnp.bfloat16)
    gate = jnp.dot(second_normed, w_gate, preferred_element_type=jnp.float32)
    up_val = jnp.dot(second_normed, w_up, preferred_element_type=jnp.float32)
    sig_gate = jax.nn.sigmoid(gate)
    silu_gate = gate * sig_gate
    hid = (silu_gate * up_val).astype(jnp.bfloat16)
    ffn_part = jnp.dot(hid, w_down, preferred_element_type=jnp.float32).astype(jnp.bfloat16)
    grad_out_b = output_cotangent.astype(jnp.bfloat16)
    grad_down = jnp.dot(grad_out_b.T, hid, preferred_element_type=jnp.float32)
    d_hid = jnp.dot(grad_out_b, w_down.T, preferred_element_type=jnp.float32)
    d_gate = (d_hid * up_val * sig_gate * (1.0 + gate * (1.0 - sig_gate))).astype(jnp.bfloat16)
    d_up = (d_hid * silu_gate).astype(jnp.bfloat16)
    grad_gate = jnp.dot(second_normed.T, d_gate, preferred_element_type=jnp.float32)
    grad_up = jnp.dot(second_normed.T, d_up, preferred_element_type=jnp.float32)
    d_two_part = jnp.dot(d_gate, w_gate.T, preferred_element_type=jnp.float32) + jnp.dot(
        d_up, w_up.T, preferred_element_type=jnp.float32
    )
    ffn_out, second_normed_gradient = tp_sum([ffn_part, d_two_part.astype(jnp.bfloat16)], 3)
    hidden_out = middle_hidden + ffn_out.astype(jnp.float32)
    second_normed_gradient = second_normed_gradient.astype(jnp.float32)
    middle_gradient = output_cotangent + norm_backward(
        second_normed_gradient * feedforward_norm_gain, second_normalized, second_inverse_norm
    )
    middle_gradient_block = middle_gradient.astype(jnp.bfloat16)
    grad_output = jnp.dot(middle_gradient_block.T, att_b, preferred_element_type=jnp.float32)
    attention_gradient = jnp.dot(
        middle_gradient_block, output_projection.T, preferred_element_type=jnp.float32
    ).reshape(rows, heads_kv, query_groups, head_dim)
    delta = jnp.transpose(jnp.sum(attention_gradient * attention_single, axis=-1), (1, 2, 0))
    d_attn_b = attention_gradient.astype(jnp.bfloat16)

    def backward_step(carry, pieces, offset):
        dq_acc, dkv_full = carry
        key_piece, value_piece = pieces
        count = key_piece.shape[0]
        key_pos = lax.dynamic_slice_in_dim(all_pos, offset, count, 0)
        scores = scores_for(rotated_queries, key_piece, positions, key_pos, inv_root)
        probs = jnp.exp(scores - log_sums[..., None])
        key_heads = key_piece.reshape(count, heads_kv, head_dim)
        value_heads = value_piece.reshape(count, heads_kv, head_dim)
        d_prob = jnp.einsum(
            "tkgd,nkd->kgtn", d_attn_b, value_heads, preferred_element_type=jnp.float32
        )
        ds_b = (probs * (d_prob - delta[..., None])).astype(jnp.bfloat16)
        prob_b = probs.astype(jnp.bfloat16)
        dq_acc = (
            dq_acc
            + jnp.einsum("kgtn,nkd->tkgd", ds_b, key_heads, preferred_element_type=jnp.float32)
            * inv_root
        )
        d_keys = (
            jnp.einsum("kgtn,tkgd->nkd", ds_b, rotated_queries, preferred_element_type=jnp.float32)
            * inv_root
        )
        d_vals = jnp.einsum("kgtn,tkgd->nkd", prob_b, d_attn_b, preferred_element_type=jnp.float32)
        term = jnp.concatenate(
            [
                d_keys.reshape(count, heads_kv * head_dim),
                d_vals.reshape(count, heads_kv * head_dim),
            ],
            axis=1,
        )
        current = lax.dynamic_slice_in_dim(dkv_full, offset, count, 0)
        dkv_full = lax.dynamic_update_slice_in_dim(dkv_full, current + term, offset, 0)
        return (dq_acc, dkv_full)

    back_init = (
        jnp.zeros((rows, heads_kv, query_groups, head_dim), jnp.float32),
        jnp.zeros((total, 2 * heads_kv * head_dim), jnp.float32),
    )
    back_state = in_blocks(
        backward_step,
        back_init,
        (keys_all, values_all),
    )
    dq_acc, dkv_full = back_state
    dkv_bf16 = dkv_full.astype(jnp.bfloat16).reshape(32, rows, 2 * heads_kv * head_dim)
    (dkv_a, dkv_b, dkv_c) = reduce_scatter_all(
        [dkv_bf16[:, :48], dkv_bf16[:, 48:96], dkv_bf16[:, 96:]],
        [("x", "z", "y"), ("z", "y", "x"), ("y", "x", "z")],
        [1, 1, 1],
        jnp.float32,
        1,
        "scatter_key_value_gradients",
    )
    dkv_local = jnp.concatenate([dkv_a, dkv_b, dkv_c], axis=0)
    kv_width = heads_kv * head_dim
    d_qn = rotate_back(dq_acc.reshape(rows, heads_q, head_dim), cosine, sine)
    part_query_norm = jnp.sum(d_qn * qhat, axis=(0, 1))
    dq_b = (
        norm_backward(d_qn * query_norm, qhat, r_query)
        .astype(jnp.bfloat16)
        .reshape(rows, heads_q * head_dim)
    )
    normed_key_gradient = rotate_back(
        dkv_local[:, :kv_width].reshape(rows, heads_kv, head_dim), cosine, sine
    )
    part_key_norm = jnp.sum(normed_key_gradient * normalized_keys, axis=(0, 1))
    key_gradient_block = (
        norm_backward(normed_key_gradient * key_norm_gain, normalized_keys, key_inverse_norm)
        .astype(jnp.bfloat16)
        .reshape(rows, kv_width)
    )
    value_gradient_block = dkv_local[:, kv_width:].astype(jnp.bfloat16)
    part_wq = jnp.dot(first_normed.T, dq_b, preferred_element_type=jnp.float32)
    part_wk = jnp.dot(first_normed.T, key_gradient_block, preferred_element_type=jnp.float32)
    part_wv = jnp.dot(first_normed.T, value_gradient_block, preferred_element_type=jnp.float32)
    d_one_part = jnp.dot(dq_b, w_query.T, preferred_element_type=jnp.float32)
    d_one_part = d_one_part + jnp.dot(
        key_gradient_block, key_projection.T, preferred_element_type=jnp.float32
    )
    d_one_part = d_one_part + jnp.dot(
        value_gradient_block, value_projection.T, preferred_element_type=jnp.float32
    )
    (first_normed_gradient,) = tp_sum([d_one_part.astype(jnp.bfloat16)], 4)
    first_normed_gradient = first_normed_gradient.astype(jnp.float32)
    input_gradient = middle_gradient + norm_backward(
        first_normed_gradient * attention_norm_gain, first_normalized, first_inverse_norm
    )
    group_share = rows // lax.axis_size("tp")
    leading_row = lax.axis_index("tp") * group_share
    part_attn_norm = jnp.sum(
        lax.dynamic_slice_in_dim(first_normed_gradient, leading_row, group_share, 0)
        * lax.dynamic_slice_in_dim(first_normalized, leading_row, group_share, 0),
        axis=0,
    )
    part_ffn_norm = jnp.sum(
        lax.dynamic_slice_in_dim(second_normed_gradient, leading_row, group_share, 0)
        * lax.dynamic_slice_in_dim(second_normalized, leading_row, group_share, 0),
        axis=0,
    )
    small = jnp.concatenate(
        [part_attn_norm, part_ffn_norm, part_query_norm, part_key_norm, jnp.zeros((768,), jnp.float32)]
    ).reshape(24, 128)
    xzy, zyx, yxz = ("x", "z", "y"), ("z", "y", "x"), ("y", "x", "z")
    (
        grad_query, grad_key, grad_value, grad_gate_s, grad_up_s, grad_output_s, grad_down_s, small_sum,
    ) = reduce_scatter_all(
        [
            part.astype(jnp.bfloat16).reshape(32, 32, part.shape[1])
            for part in (part_wq, part_wk, part_wv, grad_gate, grad_up, grad_output, grad_down)
        ],
        [xzy, yxz, yxz, zyx, xzy, zyx, yxz],
        [0] * 7,
        jnp.float32,
        5,
        "scatter_weight_gradients",
        small,
    )
    grad_output_s = grad_output_s.T
    grad_down_s = grad_down_s.T
    small_sum = small_sum.reshape(-1)
    attention_norm_gradient = small_sum[:1024]
    feedforward_norm_gradient = small_sum[1024:2048]
    grad_query_norm = small_sum[2048:2176]
    grad_key_norm = small_sum[2176:2304]
    return (
        hidden_out,
        input_gradient,
        attention_norm_gradient,
        grad_query,
        grad_key,
        grad_value,
        grad_query_norm,
        grad_key_norm,
        grad_output_s,
        feedforward_norm_gradient,
        grad_gate_s,
        grad_up_s,
        grad_down_s,
    )


def solution(mesh):
    return jax.shard_map(
        body,
        mesh=mesh,
        in_specs=(
            P("ctx", None),
            P("ctx"),
            P(),
            P(None, "tp"),
            P(None, "tp"),
            P(None, "tp"),
            P(),
            P(),
            P("tp", None),
            P(),
            P(None, "tp"),
            P(None, "tp"),
            P("tp", None),
            P("ctx", None),
        ),
        out_specs=(
            P("ctx", None),
            P("ctx", None),
            P(),
            P("ctx", "tp"),
            P("ctx", "tp"),
            P("ctx", "tp"),
            P(),
            P(),
            P("tp", "ctx"),
            P(),
            P("ctx", "tp"),
            P("ctx", "tp"),
            P("tp", "ctx"),
        ),
        check_vma=False,
    )
```

```python
import functools
import math

import jax
import jax.numpy as jnp
from jax import lax
from jax.experimental import pallas as pl
from jax.experimental.pallas import tpu as pltpu
from jax.sharding import PartitionSpec as P

EPSILON = 1e-06
ROPE_BASE = 1000000.0
MASKED = -1e30


MESH = pl.DeviceIdType.MESH
SIZES = {"y": 2, "z": 4, "x": 4}
DIMS = ("y", "z", "x")


def place():
    me = lax.axis_index("ctx")
    return {"y": me // 16, "z": lax.rem(me // 4, 4), "x": lax.rem(me, 4)}, lax.axis_index("tp")


def shifted(coords, dim, step):
    moved = dict(coords)
    moved[dim] = lax.rem(coords[dim] + step + SIZES[dim], SIZES[dim])
    return moved


def device_at(coords, tp):
    return (coords["y"] * 16 + coords["z"] * 4 + coords["x"], tp)


def torus_peers(coords, tp):
    peers = [device_at(shifted(coords, "y", 1), tp)]
    for dim in ("z", "x"):
        peers.append(device_at(shifted(coords, dim, 1), tp))
        peers.append(device_at(shifted(coords, dim, -1), tp))
    return peers


def greet(peers):
    barrier = pltpu.get_barrier_semaphore()
    for peer in peers:
        pl.semaphore_signal(barrier, inc=1, device_id=peer, device_id_type=MESH)
    pl.semaphore_wait(barrier, len(peers))


class Copies:
    def __init__(self, send_sem, recv_sem):
        self.send_sem, self.recv_sem = send_sem, recv_sem
        self.count = 0
        self.started = []

    def make(self, source, target, device):
        slot = self.count
        self.count += 1
        return pltpu.make_async_remote_copy(
            src_ref=source,
            dst_ref=target,
            send_sem=self.send_sem.at[slot],
            recv_sem=self.recv_sem.at[slot],
            device_id=device,
            device_id_type=MESH,
        )

    def send(self, source, target, device):
        copy = self.make(source, target, device)
        copy.start()
        self.started.append(copy)
        return copy

    def drain(self):
        for copy in self.started:
            copy.wait_send()


def run_together(flows):
    live = list(flows)
    while live:
        left = []
        for flow in live:
            try:
                next(flow)
                left.append(flow)
            except StopIteration:
                pass
        live = left


def gather_flow(copies, coords, tp, ref, order, piece, halves):
    def region(held, where, part):
        index = tuple(slice(None) if dim in held else where[dim] for dim in DIMS)
        return ref.at[index + part]

    held = []
    for dim in order:
        right = device_at(shifted(coords, dim, 1), tp)
        mine = region(held, coords, piece)
        if SIZES[dim] == 2:
            copy = copies.send(mine, mine, right)
            yield
            copy.wait_recv()
        else:
            left = device_at(shifted(coords, dim, -1), tp)
            go_right = copies.send(mine, mine, right)
            go_left = copies.send(mine, mine, left)
            yield
            go_right.wait_recv()
            block = region(held, shifted(coords, dim, -1), halves[0])
            pass_right = copies.send(block, block, right)
            pass_left = None
            if halves[1] is not None:
                go_left.wait_recv()
                block = region(held, shifted(coords, dim, 1), halves[1])
                pass_left = copies.send(block, block, left)
            yield
            pass_right.wait_recv()
            if pass_left is None:
                go_left.wait_recv()
            else:
                pass_left.wait_recv()
        held.append(dim)


GATHER_PARTS = ((("y", "z", "x"), 0, 48), (("x", "y", "z"), 48, 48), (("z", "x", "y"), 96, 32))


def gather_kernel(kv_ref, pos_ref, out_ref, pos_out_ref, send_sem, recv_sem, local_sem):
    coords, tp = place()
    greet(torus_peers(coords, tp))
    own = (coords["y"], coords["z"], coords["x"])
    keep = pltpu.make_async_copy(kv_ref, out_ref.at[own], local_sem.at[0])
    keep_pos = pltpu.make_async_copy(pos_ref, pos_out_ref.at[own], local_sem.at[1])
    keep.start()
    keep_pos.start()
    keep.wait()
    keep_pos.wait()
    copies = Copies(send_sem, recv_sem)
    width = kv_ref.shape[1] // 2
    flows = []
    for order, first, count in GATHER_PARTS:
        rows = pl.ds(first, count)
        flows.append(
            gather_flow(
                copies,
                coords,
                tp,
                out_ref,
                order,
                (rows, slice(None)),
                ((rows, pl.ds(0, width)), (rows, pl.ds(width, width))),
            )
        )
    whole = (slice(None), slice(None))
    flows.append(
        gather_flow(copies, coords, tp, pos_out_ref, ("y", "z", "x"), whole, (whole, None))
    )
    run_together(flows)
    copies.drain()


def gather_all(kv_block, positions):
    rows, width = kv_block.shape
    vmem = pl.BlockSpec(memory_space=pltpu.VMEM)
    everything, all_pos = pl.pallas_call(
        gather_kernel,
        out_shape=(
            jax.ShapeDtypeStruct((2, 4, 4, rows, width), kv_block.dtype),
            jax.ShapeDtypeStruct((2, 4, 4, 1, rows), jnp.int32),
        ),
        in_specs=[vmem, vmem],
        out_specs=(vmem, vmem),
        scratch_shapes=[
            pltpu.SemaphoreType.DMA((40,)),
            pltpu.SemaphoreType.DMA((40,)),
            pltpu.SemaphoreType.DMA((2,)),
        ],
        compiler_params=pltpu.CompilerParams(
            collective_id=0, has_side_effects=True, vmem_limit_bytes=24 << 20
        ),
        name="gather_keys_values",
    )(kv_block, positions.reshape(1, rows))
    return everything.reshape(32, rows, width), all_pos.reshape(32 * rows)


def leading_index(flat, dims):
    index = []
    for dim in reversed(dims):
        index.insert(0, lax.rem(flat, SIZES[dim]))
        flat = flat // SIZES[dim]
    return tuple(index)


def leading_shape(dims):
    return tuple(SIZES[dim] for dim in dims)


def over_leading(dims, step):
    count = math.prod(leading_shape(dims))
    if count == 1:
        step(())
        return

    def body(flat, carry):
        step(leading_index(flat, dims))
        return carry

    lax.fori_loop(0, count, body, 0)


def scatter_scratch(shape, order, axis):
    half = tuple(size // 2 if i == axis else size for i, size in enumerate(shape))
    buffers = []
    rest = list(DIMS)
    for dim in order:
        rest.remove(dim)
        lead = leading_shape(rest)
        if SIZES[dim] == 2:
            buffers.append(pltpu.VMEM(lead + shape, jnp.bfloat16))
        else:
            buffers.extend([pltpu.VMEM(lead + half, jnp.bfloat16)] * 8)
        if rest:
            buffers.append(pltpu.VMEM(lead + shape, jnp.bfloat16))
    return buffers


def scatter_flow(copies, coords, tp, source, result, buffers, order, axis):
    buffers = list(buffers)
    shape = source.shape[-2:]
    size = shape[axis] // 2
    halves = [
        tuple(pl.ds(h * size, size) if i == axis else slice(None) for i in range(2))
        for h in range(2)
    ]
    whole = (slice(None), slice(None))
    current = source
    dims = list(DIMS)

    for dim in order:
        rest = [d for d in dims if d != dim]
        spot = dims.index(dim)

        def at(where, lead, part, spot=spot, current=current):
            index = tuple(lead[:spot]) + (where[dim],) + tuple(lead[spot:])
            return current.at[index + part]

        everywhere = (slice(None),) * len(rest)
        right_coords = shifted(coords, dim, 1)
        right = device_at(right_coords, tp)
        f32 = jnp.float32
        if SIZES[dim] == 2:
            landed = buffers.pop(0)
            copy = copies.send(at(right_coords, everywhere, whole), landed, right)
            target = buffers.pop(0) if rest else result
            yield
            copy.wait_recv()

            def add(lead):
                total = at(coords, lead, whole)[...].astype(f32) + landed[lead + whole].astype(f32)
                target[lead + whole] = total.astype(target.dtype)

            over_leading(rest, add)
        else:
            left_coords = shifted(coords, dim, -1)
            far_coords = shifted(coords, dim, 2)
            left = device_at(left_coords, tp)
            pass_l, pass_r, near_l, near_r, sum_l, sum_r, out_r, out_l = buffers[:8]
            buffers = buffers[8:]
            target = buffers.pop(0) if rest else result
            relay_r = copies.send(at(far_coords, everywhere, halves[0]), pass_l, right)
            relay_l = copies.send(at(far_coords, everywhere, halves[1]), pass_r, left)
            direct_r = copies.send(at(right_coords, everywhere, halves[1]), near_l, right)
            direct_l = copies.send(at(left_coords, everywhere, halves[0]), near_r, left)
            yield
            relay_r.wait_recv()

            def merge_right(lead):
                total = at(right_coords, lead, halves[0])[...].astype(f32) + pass_l[
                    lead + whole
                ].astype(f32)
                out_r[lead + whole] = total.astype(out_r.dtype)

            over_leading(rest, merge_right)
            merged_r = copies.send(out_r, sum_l, right)
            relay_l.wait_recv()

            def merge_left(lead):
                total = at(left_coords, lead, halves[1])[...].astype(f32) + pass_r[
                    lead + whole
                ].astype(f32)
                out_l[lead + whole] = total.astype(out_l.dtype)

            over_leading(rest, merge_left)
            merged_l = copies.send(out_l, sum_r, left)
            yield
            direct_r.wait_recv()
            direct_l.wait_recv()
            merged_r.wait_recv()
            merged_l.wait_recv()

            def add(lead):
                for half, one, two in ((halves[0], sum_l, near_r), (halves[1], near_l, sum_r)):
                    total = (
                        at(coords, lead, half)[...].astype(f32)
                        + one[lead + whole].astype(f32)
                        + two[lead + whole].astype(f32)
                    )
                    target[lead + half] = total.astype(target.dtype)

            over_leading(rest, add)
        current = target
        dims = rest


def sum_everywhere_flow(copies, coords, tp, source, result, slots):
    current = source
    for stage, dim in enumerate(("x", "z")):
        ring = slots[stage]
        left = device_at(shifted(coords, dim, -1), tp)
        right = device_at(shifted(coords, dim, 1), tp)
        spot = coords[dim]
        ring[spot] = current[...]
        go_right = copies.send(current, ring.at[spot], right)
        go_left = copies.send(current, ring.at[spot], left)
        yield
        go_right.wait_recv()
        block = ring.at[shifted(coords, dim, -1)[dim]]
        passed = copies.send(block, block, right)
        yield
        go_left.wait_recv()
        passed.wait_recv()
        total = slots[5 + stage]
        total[...] = ring[0] + ring[1] + ring[2] + ring[3]
        current = total
    partners = (
        device_at(shifted(coords, "y", 1), tp),
        (lax.axis_index("ctx"), tp + 1 - 2 * lax.rem(tp, 2)),
        (lax.axis_index("ctx"), lax.rem(tp + 2, 4)),
    )
    for stage, partner in enumerate(partners):
        landed = slots[2 + stage]
        copy = copies.send(current, landed, partner)
        yield
        copy.wait_recv()
        total = slots[7 + stage] if stage < 2 else result
        total[...] = current[...] + landed[...]
        current = total


def sum_everywhere_scratch(shape):
    return [pltpu.VMEM((4,) + shape, jnp.float32)] * 2 + [pltpu.VMEM(shape, jnp.float32)] * 7


def reduce_scatter_all(arrays, orders, axes, out_dtype, collective_id, name, small=None):
    shapes = [array.shape[1:] for array in arrays]
    counts = [
        len(scatter_scratch(shape, order, axis))
        for shape, order, axis in zip(shapes, orders, axes)
    ]
    number = len(arrays)
    extra = 0 if small is None else 1

    def kernel(*refs):
        ins = refs[: number + extra]
        outs = refs[number + extra : 2 * (number + extra)]
        scratch = refs[2 * (number + extra) :]
        send_sem, recv_sem = scratch[:2]
        scratch = scratch[2:]
        coords, tp = place()
        peers = torus_peers(coords, tp)
        if extra:
            peers.append((lax.axis_index("ctx"), tp + 1 - 2 * lax.rem(tp, 2)))
            peers.append((lax.axis_index("ctx"), lax.rem(tp + 2, 4)))
        greet(peers)
        copies = Copies(send_sem, recv_sem)
        flows = []
        begin = 0
        for i in range(number):
            buffers = scratch[begin : begin + counts[i]]
            begin += counts[i]
            flows.append(
                scatter_flow(copies, coords, tp, ins[i], outs[i], buffers, orders[i], axes[i])
            )
        if extra:
            flows.append(
                sum_everywhere_flow(copies, coords, tp, ins[number], outs[number], scratch[begin:])
            )
        run_together(flows)
        copies.drain()

    vmem = pl.BlockSpec(memory_space=pltpu.VMEM)
    copies_needed = number * 13 + extra * 9
    scratch_shapes = [pltpu.SemaphoreType.DMA((copies_needed,))] * 2
    for shape, order, axis in zip(shapes, orders, axes):
        scratch_shapes.extend(scatter_scratch(shape, order, axis))
    out_shape = [jax.ShapeDtypeStruct(shape, out_dtype) for shape in shapes]
    operands = [array.reshape((2, 4, 4) + shape) for array, shape in zip(arrays, shapes)]
    if extra:
        scratch_shapes.extend(sum_everywhere_scratch(small.shape))
        out_shape.append(jax.ShapeDtypeStruct(small.shape, jnp.float32))
        operands.append(small)
    return pl.pallas_call(
        kernel,
        out_shape=tuple(out_shape),
        in_specs=[vmem] * len(operands),
        out_specs=(vmem,) * len(out_shape),
        scratch_shapes=scratch_shapes,
        compiler_params=pltpu.CompilerParams(
            collective_id=collective_id, has_side_effects=True, vmem_limit_bytes=60 << 20
        ),
        name=name,
    )(*operands)


def tp_sum_flow(copies, ins, out, landed, chip, far, partner_core, partner_far, core, first, count, rows):
    half = rows // 2
    mine = pl.ds(pl.multiple_of(core * half + first, 16), count)
    theirs = pl.ds(pl.multiple_of((1 - core) * half + first, 16), count)
    local = pl.ds(first, count)
    f32 = jnp.float32
    copy = copies.send(ins.at[theirs], landed.at[local], partner_core)
    yield
    copy.wait_recv()
    chip[local] = (ins[mine].astype(f32) + landed[local].astype(f32)).astype(chip.dtype)
    copy = copies.send(chip.at[local], far.at[local], partner_far)
    yield
    copy.wait_recv()
    out[mine] = (chip[local].astype(f32) + far[local].astype(f32)).astype(out.dtype)
    copy = copies.send(out.at[mine], out.at[mine], partner_core)
    yield
    copy.wait_recv()


def tp_sum(parts, collective_id, pieces=2):
    number = len(parts)
    rows, columns = parts[0].shape
    half = rows // 2

    def kernel(*refs):
        ins, outs = refs[:number], refs[number : 2 * number]
        send_sem, recv_sem = refs[2 * number : 2 * number + 2]
        scratch = refs[2 * number + 2 :]
        tp = lax.axis_index("tp")
        ctx = lax.axis_index("ctx")
        core = lax.rem(tp, 2)
        partner_core = (ctx, tp + 1 - 2 * core)
        partner_far = (ctx, lax.rem(tp + 2, 4))
        greet([partner_core, partner_far])
        copies = Copies(send_sem, recv_sem)
        flows = []
        count = half // pieces
        for i in range(number):
            landed, chip, far = scratch[3 * i : 3 * i + 3]
            for piece in range(pieces):
                flows.append(
                    tp_sum_flow(
                        copies, ins[i], outs[i], landed, chip, far, partner_core, partner_far,
                        core, piece * count, count, rows,
                    )
                )
        run_together(flows)
        copies.drain()

    vmem = pl.BlockSpec(memory_space=pltpu.VMEM)
    return pl.pallas_call(
        kernel,
        out_shape=tuple(jax.ShapeDtypeStruct(part.shape, part.dtype) for part in parts),
        in_specs=[vmem] * number,
        out_specs=(vmem,) * number,
        scratch_shapes=[pltpu.SemaphoreType.DMA((3 * pieces * number,))] * 2
        + [pltpu.VMEM((half, columns), jnp.bfloat16)] * (3 * number),
        compiler_params=pltpu.CompilerParams(
            collective_id=collective_id, has_side_effects=True, vmem_limit_bytes=24 << 20
        ),
        name="tp_sum",
    )(*parts)


CHUNK = 4


def stacked(ref, head, groups, width):
    return jnp.concatenate(
        [ref[:, (head * groups + g) * width : (head * groups + g + 1) * width] for g in range(groups)],
        axis=0,
    )


def transposed_dot(left, right):
    return lax.dot_general(
        left, right, (((1,), (1,)), ((), ())), preferred_element_type=jnp.float32
    )


def masked_scores(keys, queries, starts_ref, first_block, q_pos, inv_root):
    scores = transposed_dot(keys, queries) * inv_root
    step = lax.broadcasted_iota(jnp.int32, (64, queries.shape[0]), 0)
    pieces = []
    for b in range(keys.shape[0] // 64):
        ahead = q_pos - starts_ref[first_block + b]
        pieces.append(jnp.where(ahead >= step, scores[b * 64 : (b + 1) * 64], MASKED))
    return jnp.concatenate(pieces, axis=0)


def attention_forward_kernel(
    starts_ref, q_ref, kv_ref, q_pos_ref, out_ref, lse_ref, scores_ref, *, heads_kv, groups
):
    width = 128
    rows = q_ref.shape[0]
    keys_per = CHUNK * rows
    steps = kv_ref.shape[0] // CHUNK
    inv_root = 1.0 / math.sqrt(width)
    q_pos = q_pos_ref[...]
    for head in range(heads_kv):
        queries = stacked(q_ref, head, groups, width)

        def score_step(i, top, head=head, queries=queries):
            keys = kv_ref[pl.ds(i * CHUNK, CHUNK), :, head * width : (head + 1) * width]
            scores = masked_scores(
                keys.reshape(keys_per, width), queries, starts_ref, i * (keys_per // 64), q_pos, inv_root
            )
            scores_ref[pl.ds(pl.multiple_of(i * keys_per, keys_per), keys_per), :] = scores
            return jnp.maximum(top, jnp.max(scores, axis=0, keepdims=True))

        top = lax.fori_loop(
            0, steps, score_step, jnp.full((1, groups * rows), MASKED, jnp.float32)
        )

        def weight_step(i, carry, head=head, top=top):
            total, mixed = carry
            base = (heads_kv + head) * width
            values = kv_ref[pl.ds(i * CHUNK, CHUNK), :, base : base + width]
            scores = scores_ref[pl.ds(pl.multiple_of(i * keys_per, keys_per), keys_per), :]
            weights = jnp.exp(scores - top)
            total = total + jnp.sum(weights, axis=0, keepdims=True)
            mixed = mixed + lax.dot_general(
                values.reshape(keys_per, width),
                weights.astype(jnp.bfloat16),
                (((0,), (0,)), ((), ())),
                preferred_element_type=jnp.float32,
            )
            return total, mixed

        total, mixed = lax.fori_loop(
            0,
            steps,
            weight_step,
            (
                jnp.zeros((1, groups * rows), jnp.float32),
                jnp.zeros((width, groups * rows), jnp.float32),
            ),
        )
        mixed = mixed / total
        lse_ref[head] = top + jnp.log(total)
        for g in range(groups):
            first = (head * groups + g) * width
            out_ref[:, first : first + width] = mixed[:, g * rows : (g + 1) * rows].T


def attention_forward(starts, queries, kv_all, q_pos, heads_kv, groups):
    rows, total = queries.shape
    vmem = pl.BlockSpec(memory_space=pltpu.VMEM)
    smem = pl.BlockSpec(memory_space=pltpu.SMEM)
    keys = kv_all.shape[0] * kv_all.shape[1]
    return pl.pallas_call(
        functools.partial(attention_forward_kernel, heads_kv=heads_kv, groups=groups),
        out_shape=(
            jax.ShapeDtypeStruct((rows, total), jnp.float32),
            jax.ShapeDtypeStruct((heads_kv, 1, groups * rows), jnp.float32),
        ),
        in_specs=[smem, vmem, vmem, vmem],
        out_specs=(vmem, vmem),
        scratch_shapes=[pltpu.VMEM((keys, groups * rows), jnp.float32)],
        compiler_params=pltpu.CompilerParams(vmem_limit_bytes=32 << 20),
        name="attention_forward",
    )(starts, queries, kv_all, q_pos)


def backward_steps(refs, dkv_ref, dq_acc_ref, heads_kv, groups, begin, end):
    starts_ref, q_ref, kv_ref, q_pos_ref, grad_ref, lse_ref, delta_ref = refs
    width = 128
    rows = q_ref.shape[0]
    keys_per = CHUNK * rows
    inv_root = 1.0 / math.sqrt(width)

    def step(i, carry):
        q_pos = q_pos_ref[...]
        for head in range(heads_kv):
            queries = stacked(q_ref, head, groups, width)
            grads = stacked(grad_ref, head, groups, width)
            chunk = pl.ds(i * CHUNK, CHUNK)
            base = (heads_kv + head) * width
            keys = kv_ref[chunk, :, head * width : (head + 1) * width].reshape(keys_per, width)
            values = kv_ref[chunk, :, base : base + width].reshape(keys_per, width)
            scores = masked_scores(keys, queries, starts_ref, i * (keys_per // 64), q_pos, inv_root)
            probs = jnp.exp(scores - lse_ref[head])
            d_prob = transposed_dot(values, grads)
            d_scores = (probs * (d_prob - delta_ref[head])).astype(jnp.bfloat16)
            d_keys = jnp.dot(d_scores, queries, preferred_element_type=jnp.float32) * inv_root
            d_values = jnp.dot(
                probs.astype(jnp.bfloat16), grads, preferred_element_type=jnp.float32
            )
            where = (i // 4, lax.rem(i, 4))
            shape = (CHUNK, rows, width)
            dkv_ref[where + (slice(None), slice(None), slice(head * width, (head + 1) * width))] = (
                d_keys.astype(jnp.bfloat16).reshape(shape)
            )
            dkv_ref[where + (slice(None), slice(None), slice(base, base + width))] = (
                d_values.astype(jnp.bfloat16).reshape(shape)
            )
            dq_acc_ref[head] += lax.dot_general(
                keys, d_scores, (((0,), (0,)), ((), ())), preferred_element_type=jnp.float32
            )
        return carry

    lax.fori_loop(begin, end, step, 0)


def attention_backward(
    starts, queries, kv_all, q_pos, grads, lse, delta, weights, orders, heads_kv, groups, collective_id
):
    rows, total = queries.shape
    width = 128
    number = len(weights)
    shapes = [weight.shape[1:] for weight in weights]
    kv_width = kv_all.shape[2]
    row_parts = ((("x", "z", "y"), 0, 48), (("z", "y", "x"), 48, 48), (("y", "x", "z"), 96, 32))
    weight_scratch = [scatter_scratch(shape, order, 0) for shape, order in zip(shapes, orders)]
    kv_scratch = [scatter_scratch((count, kv_width), order, 1) for order, first, count in row_parts]

    def kernel(*refs):
        ins, refs = refs[:7], refs[7:]
        weight_refs, refs = refs[:number], refs[number:]
        dq_ref, dkv_out_ref = refs[:2]
        weight_outs, refs = refs[2 : 2 + number], refs[2 + number :]
        send_sem, recv_sem, dkv_ref, dq_acc_ref = refs[:4]
        scratch = refs[4:]
        coords, tp = place()
        greet(torus_peers(coords, tp))
        copies = Copies(send_sem, recv_sem)
        early = []
        begin = 0
        for i in range(number):
            buffers = scratch[begin : begin + len(weight_scratch[i])]
            begin += len(weight_scratch[i])
            early.append(
                scatter_flow(copies, coords, tp, weight_refs[i], weight_outs[i], buffers, orders[i], 0)
            )
        late = []
        for (order, first, count), needed in zip(row_parts, kv_scratch):
            buffers = scratch[begin : begin + len(needed)]
            begin += len(needed)
            own_rows = pl.ds(first, count)
            late.append(
                scatter_flow(
                    copies,
                    coords,
                    tp,
                    dkv_ref.at[:, :, :, own_rows, :],
                    dkv_out_ref.at[own_rows, :],
                    buffers,
                    order,
                    1,
                )
            )
        steps = kv_all.shape[0] // CHUNK
        dq_acc_ref[...] = jnp.zeros_like(dq_acc_ref)
        for flow in early:
            next(flow)
        cut = steps // 2
        backward_steps(ins, dkv_ref, dq_acc_ref, heads_kv, groups, 0, cut)
        for flow in early:
            next(flow)
        backward_steps(ins, dkv_ref, dq_acc_ref, heads_kv, groups, cut, steps)
        for flow in late:
            next(flow)
        inv_root = 1.0 / math.sqrt(width)
        for head in range(heads_kv):
            for g in range(groups):
                first = (head * groups + g) * width
                dq_ref[:, first : first + width] = (
                    dq_acc_ref[head, :, g * rows : (g + 1) * rows].T * inv_root
                )
        run_together(late + early)
        copies.drain()

    vmem = pl.BlockSpec(memory_space=pltpu.VMEM)
    smem = pl.BlockSpec(memory_space=pltpu.SMEM)
    scratch_shapes = [
        pltpu.SemaphoreType.DMA((13 * (number + 3),)),
        pltpu.SemaphoreType.DMA((13 * (number + 3),)),
        pltpu.VMEM((2, 4, 4, rows, kv_width), jnp.bfloat16),
        pltpu.VMEM((heads_kv, width, groups * rows), jnp.float32),
    ]
    for needed in weight_scratch + kv_scratch:
        scratch_shapes.extend(needed)
    results = pl.pallas_call(
        kernel,
        out_shape=(
            jax.ShapeDtypeStruct((rows, total), jnp.float32),
            jax.ShapeDtypeStruct((rows, kv_width), jnp.float32),
        )
        + tuple(jax.ShapeDtypeStruct(shape, jnp.float32) for shape in shapes),
        in_specs=[smem] + [vmem] * (6 + number),
        out_specs=(vmem,) * (2 + number),
        scratch_shapes=scratch_shapes,
        compiler_params=pltpu.CompilerParams(
            collective_id=collective_id, has_side_effects=True, vmem_limit_bytes=60 << 20
        ),
        name="attention_backward",
    )(
        starts,
        queries,
        kv_all,
        q_pos,
        grads,
        lse,
        delta,
        *[weight.reshape((2, 4, 4) + shape) for weight, shape in zip(weights, shapes)],
    )
    return results[0], results[1], results[2:]


def write_results_kernel(*refs):
    number = len(refs) // 2
    for source, target in zip(refs[:number], refs[number:]):
        if source.shape == target.shape:
            target[...] = source[...]
        else:
            target[...] = source[...].T


def write_results(arrays, flipped):
    vmem = pl.BlockSpec(memory_space=pltpu.VMEM)
    return pl.pallas_call(
        write_results_kernel,
        out_shape=tuple(
            jax.ShapeDtypeStruct(a.shape[::-1] if flip else a.shape, a.dtype)
            for a, flip in zip(arrays, flipped)
        ),
        in_specs=[vmem] * len(arrays),
        out_specs=(vmem,) * len(arrays),
        compiler_params=pltpu.CompilerParams(vmem_limit_bytes=24 << 20),
        name="write_results",
    )(*arrays)


def rms_scale(values):
    return lax.rsqrt(jnp.mean(values * values, axis=-1, keepdims=True) + EPSILON)


def norm_backward(grad, normed, scale_rows):
    return scale_rows * (grad - normed * jnp.mean(grad * normed, axis=-1, keepdims=True))


def rope_tables(positions, head_dim):
    half_dim = head_dim // 2
    freqs = jnp.exp(
        -(2.0 * jnp.arange(half_dim, dtype=jnp.float32) / head_dim) * math.log(ROPE_BASE)
    )
    angles = positions.astype(jnp.float32)[:, None] * freqs[None, :]
    return (jnp.cos(angles)[:, None, :], jnp.sin(angles)[:, None, :])


def rotate_pairs(values, cosine, sine):
    half_dim = values.shape[-1] // 2
    first = values[..., :half_dim]
    second = values[..., half_dim:]
    return jnp.concatenate(
        [first * cosine - second * sine, second * cosine + first * sine], axis=-1
    )


def rotate_back(grad, cosine, sine):
    half_dim = grad.shape[-1] // 2
    first = grad[..., :half_dim]
    second = grad[..., half_dim:]
    return jnp.concatenate(
        [first * cosine + second * sine, second * cosine - first * sine], axis=-1
    )


def body(
    layer_input,
    positions,
    attention_norm_gain,
    w_query,
    key_projection,
    value_projection,
    query_norm,
    key_norm_gain,
    output_projection,
    feedforward_norm_gain,
    w_gate,
    w_up,
    w_down,
    output_cotangent,
):
    rows = layer_input.shape[0]
    head_dim = query_norm.shape[0]
    heads_q = w_query.shape[1] // head_dim
    heads_kv = key_projection.shape[1] // head_dim
    query_groups = heads_q // heads_kv
    first_inverse_norm = rms_scale(layer_input)
    first_normalized = layer_input * first_inverse_norm
    first_normed = (first_normalized * attention_norm_gain).astype(jnp.bfloat16)
    queries = jnp.dot(first_normed, w_query, preferred_element_type=jnp.float32).reshape(
        rows, heads_q, head_dim
    )
    unnormed_keys = jnp.dot(
        first_normed, key_projection, preferred_element_type=jnp.float32
    ).reshape(rows, heads_kv, head_dim)
    value_block = jnp.dot(
        first_normed, value_projection, preferred_element_type=jnp.float32
    ).astype(jnp.bfloat16)
    r_query = rms_scale(queries)
    qhat = queries * r_query
    key_inverse_norm = rms_scale(unnormed_keys)
    normalized_keys = unnormed_keys * key_inverse_norm
    cosine, sine = rope_tables(positions, head_dim)
    rotated_queries = (
        rotate_pairs(qhat * query_norm, cosine, sine)
        .astype(jnp.bfloat16)
        .reshape(rows, heads_kv, query_groups, head_dim)
    )
    k_rot = (
        rotate_pairs(normalized_keys * key_norm_gain, cosine, sine)
        .astype(jnp.bfloat16)
        .reshape(rows, heads_kv * head_dim)
    )

    kv_all, all_pos = gather_all(jnp.concatenate([k_rot, value_block], axis=1), positions)
    starts = all_pos.reshape(-1, 64)[:, 0]
    q_pos = jnp.tile(positions, query_groups).reshape(1, query_groups * rows)
    rotated_queries = rotated_queries.reshape(rows, heads_q * head_dim)
    attention_single, log_sums = attention_forward(
        starts, rotated_queries, kv_all, q_pos, heads_kv, query_groups
    )
    att_b = attention_single.astype(jnp.bfloat16)
    attention_single = attention_single.reshape(rows, heads_kv, query_groups, head_dim)
    (attention_out,) = tp_sum(
        [jnp.dot(att_b, output_projection, preferred_element_type=jnp.float32).astype(jnp.bfloat16)],
        2,
    )
    middle_hidden = layer_input + attention_out.astype(jnp.float32)
    second_inverse_norm = rms_scale(middle_hidden)
    second_normalized = middle_hidden * second_inverse_norm
    second_normed = (second_normalized * feedforward_norm_gain).astype(jnp.bfloat16)
    gate = jnp.dot(second_normed, w_gate, preferred_element_type=jnp.float32)
    up_val = jnp.dot(second_normed, w_up, preferred_element_type=jnp.float32)
    sig_gate = jax.nn.sigmoid(gate)
    silu_gate = gate * sig_gate
    hid = (silu_gate * up_val).astype(jnp.bfloat16)
    ffn_part = jnp.dot(hid, w_down, preferred_element_type=jnp.float32).astype(jnp.bfloat16)
    grad_out_b = output_cotangent.astype(jnp.bfloat16)
    grad_down = jnp.dot(grad_out_b.T, hid, preferred_element_type=jnp.float32)
    d_hid = jnp.dot(grad_out_b, w_down.T, preferred_element_type=jnp.float32)
    d_gate = (d_hid * up_val * sig_gate * (1.0 + gate * (1.0 - sig_gate))).astype(jnp.bfloat16)
    d_up = (d_hid * silu_gate).astype(jnp.bfloat16)
    grad_gate = jnp.dot(second_normed.T, d_gate, preferred_element_type=jnp.float32)
    grad_up = jnp.dot(second_normed.T, d_up, preferred_element_type=jnp.float32)
    d_two_part = jnp.dot(d_gate, w_gate.T, preferred_element_type=jnp.float32) + jnp.dot(
        d_up, w_up.T, preferred_element_type=jnp.float32
    )
    ffn_out, second_normed_gradient = tp_sum([ffn_part, d_two_part.astype(jnp.bfloat16)], 3)
    hidden_out = middle_hidden + ffn_out.astype(jnp.float32)
    second_normed_gradient = second_normed_gradient.astype(jnp.float32)
    middle_gradient = output_cotangent + norm_backward(
        second_normed_gradient * feedforward_norm_gain, second_normalized, second_inverse_norm
    )
    middle_gradient_block = middle_gradient.astype(jnp.bfloat16)
    grad_output = jnp.dot(middle_gradient_block.T, att_b, preferred_element_type=jnp.float32)
    attention_gradient = jnp.dot(
        middle_gradient_block, output_projection.T, preferred_element_type=jnp.float32
    ).reshape(rows, heads_kv, query_groups, head_dim)
    delta = jnp.transpose(jnp.sum(attention_gradient * attention_single, axis=-1), (1, 2, 0))
    d_attn_b = attention_gradient.astype(jnp.bfloat16)

    xzy, zyx, yxz = ("x", "z", "y"), ("z", "y", "x"), ("y", "x", "z")
    early_weights = [
        part.astype(jnp.bfloat16).reshape(32, 32, part.shape[1])
        for part in (grad_gate, grad_up, grad_output, grad_down)
    ]
    dq_acc, dkv_local, (grad_gate_s, grad_up_s, grad_output_s, grad_down_s) = attention_backward(
        starts,
        rotated_queries,
        kv_all,
        q_pos,
        d_attn_b.reshape(rows, heads_q * head_dim),
        log_sums,
        delta.reshape(heads_kv, 1, query_groups * rows),
        early_weights,
        [zyx, xzy, yxz, yxz],
        heads_kv,
        query_groups,
        1,
    )
    kv_width = heads_kv * head_dim
    d_qn = rotate_back(dq_acc.reshape(rows, heads_q, head_dim), cosine, sine)
    part_query_norm = jnp.sum(d_qn * qhat, axis=(0, 1))
    dq_b = (
        norm_backward(d_qn * query_norm, qhat, r_query)
        .astype(jnp.bfloat16)
        .reshape(rows, heads_q * head_dim)
    )
    normed_key_gradient = rotate_back(
        dkv_local[:, :kv_width].reshape(rows, heads_kv, head_dim), cosine, sine
    )
    part_key_norm = jnp.sum(normed_key_gradient * normalized_keys, axis=(0, 1))
    key_gradient_block = (
        norm_backward(normed_key_gradient * key_norm_gain, normalized_keys, key_inverse_norm)
        .astype(jnp.bfloat16)
        .reshape(rows, kv_width)
    )
    value_gradient_block = dkv_local[:, kv_width:].astype(jnp.bfloat16)
    part_wq = jnp.dot(first_normed.T, dq_b, preferred_element_type=jnp.float32)
    part_wk = jnp.dot(first_normed.T, key_gradient_block, preferred_element_type=jnp.float32)
    part_wv = jnp.dot(first_normed.T, value_gradient_block, preferred_element_type=jnp.float32)
    d_one_part = jnp.dot(dq_b, w_query.T, preferred_element_type=jnp.float32)
    d_one_part = d_one_part + jnp.dot(
        key_gradient_block, key_projection.T, preferred_element_type=jnp.float32
    )
    d_one_part = d_one_part + jnp.dot(
        value_gradient_block, value_projection.T, preferred_element_type=jnp.float32
    )
    (first_normed_gradient,) = tp_sum([d_one_part.astype(jnp.bfloat16)], 4)
    first_normed_gradient = first_normed_gradient.astype(jnp.float32)
    input_gradient = middle_gradient + norm_backward(
        first_normed_gradient * attention_norm_gain, first_normalized, first_inverse_norm
    )
    group_share = rows // lax.axis_size("tp")
    leading_row = lax.axis_index("tp") * group_share
    part_attn_norm = jnp.sum(
        lax.dynamic_slice_in_dim(first_normed_gradient, leading_row, group_share, 0)
        * lax.dynamic_slice_in_dim(first_normalized, leading_row, group_share, 0),
        axis=0,
    )
    part_ffn_norm = jnp.sum(
        lax.dynamic_slice_in_dim(second_normed_gradient, leading_row, group_share, 0)
        * lax.dynamic_slice_in_dim(second_normalized, leading_row, group_share, 0),
        axis=0,
    )
    small = jnp.concatenate(
        [part_attn_norm, part_ffn_norm, part_query_norm, part_key_norm, jnp.zeros((768,), jnp.float32)]
    ).reshape(24, 128)
    grad_query, grad_key, grad_value, small_sum = reduce_scatter_all(
        [
            part.astype(jnp.bfloat16).reshape(32, 32, part.shape[1])
            for part in (part_wq, part_wk, part_wv)
        ],
        [xzy, zyx, yxz],
        [0] * 3,
        jnp.float32,
        5,
        "scatter_weight_gradients",
        small,
    )
    (
        grad_query, grad_key, grad_value, grad_gate_s, grad_up_s, grad_output_s, grad_down_s, small_sum,
    ) = write_results(
        [grad_query, grad_key, grad_value, grad_gate_s, grad_up_s, grad_output_s, grad_down_s, small_sum],
        [False, False, False, False, False, True, True, False],
    )
    small_sum = small_sum.reshape(-1)
    attention_norm_gradient = small_sum[:1024]
    feedforward_norm_gradient = small_sum[1024:2048]
    grad_query_norm = small_sum[2048:2176]
    grad_key_norm = small_sum[2176:2304]
    return (
        hidden_out,
        input_gradient,
        attention_norm_gradient,
        grad_query,
        grad_key,
        grad_value,
        grad_query_norm,
        grad_key_norm,
        grad_output_s,
        feedforward_norm_gradient,
        grad_gate_s,
        grad_up_s,
        grad_down_s,
    )


def solution(mesh):
    return jax.shard_map(
        body,
        mesh=mesh,
        in_specs=(
            P("ctx", None),
            P("ctx"),
            P(),
            P(None, "tp"),
            P(None, "tp"),
            P(None, "tp"),
            P(),
            P(),
            P("tp", None),
            P(),
            P(None, "tp"),
            P(None, "tp"),
            P("tp", None),
            P("ctx", None),
        ),
        out_specs=(
            P("ctx", None),
            P("ctx", None),
            P(),
            P("ctx", "tp"),
            P("ctx", "tp"),
            P("ctx", "tp"),
            P(),
            P(),
            P("tp", "ctx"),
            P(),
            P("ctx", "tp"),
            P("ctx", "tp"),
            P("tp", "ctx"),
        ),
        check_vma=False,
    )
```

```python
import math
import types

import jax
import jax.numpy as jnp
from jax import lax
from jax.experimental import pallas as pl
from jax.experimental.pallas import tpu as pltpu
from jax.sharding import PartitionSpec as P

EPSILON = 1e-06
ROPE_BASE = 1000000.0
MASKED = -1e30


MESH = pl.DeviceIdType.MESH
SIZES = {"y": 2, "z": 4, "x": 4}
DIMS = ("y", "z", "x")


def place():
    me = lax.axis_index("ctx")
    return {"y": me // 16, "z": lax.rem(me // 4, 4), "x": lax.rem(me, 4)}, lax.axis_index("tp")


def shifted(coords, dim, step):
    moved = dict(coords)
    moved[dim] = lax.rem(coords[dim] + step + SIZES[dim], SIZES[dim])
    return moved


def device_at(coords, tp):
    return (coords["y"] * 16 + coords["z"] * 4 + coords["x"], tp)


def torus_peers(coords, tp):
    peers = [device_at(shifted(coords, "y", 1), tp)]
    for dim in ("z", "x"):
        peers.append(device_at(shifted(coords, dim, 1), tp))
        peers.append(device_at(shifted(coords, dim, -1), tp))
    return peers


def greet(peers):
    barrier = pltpu.get_barrier_semaphore()
    for peer in peers:
        pl.semaphore_signal(barrier, inc=1, device_id=peer, device_id_type=MESH)
    pl.semaphore_wait(barrier, len(peers))


class Copies:
    def __init__(self, send_sem, recv_sem):
        self.send_sem, self.recv_sem = send_sem, recv_sem
        self.count = 0
        self.started = []

    def make(self, source, target, device):
        slot = self.count
        self.count += 1
        return pltpu.make_async_remote_copy(
            src_ref=source,
            dst_ref=target,
            send_sem=self.send_sem.at[slot],
            recv_sem=self.recv_sem.at[slot],
            device_id=device,
            device_id_type=MESH,
        )

    def send(self, source, target, device):
        copy = self.make(source, target, device)
        copy.start()
        self.started.append(copy)
        return copy

    def drain(self):
        for copy in self.started:
            copy.wait_send()


def run_together(flows):
    live = list(flows)
    while live:
        left = []
        for flow in live:
            try:
                next(flow)
                left.append(flow)
            except StopIteration:
                pass
        live = left


def gather_flow(copies, coords, tp, ref, order, piece, halves):
    def region(held, where, part):
        index = tuple(slice(None) if dim in held else where[dim] for dim in DIMS)
        return ref.at[index + part]

    held = []
    for dim in order:
        right = device_at(shifted(coords, dim, 1), tp)
        mine = region(held, coords, piece)
        if SIZES[dim] == 2:
            copy = copies.send(mine, mine, right)
            yield
            copy.wait_recv()
        else:
            left = device_at(shifted(coords, dim, -1), tp)
            go_right = copies.send(mine, mine, right)
            go_left = copies.send(mine, mine, left)
            yield
            go_right.wait_recv()
            block = region(held, shifted(coords, dim, -1), halves[0])
            pass_right = copies.send(block, block, right)
            pass_left = None
            if halves[1] is not None:
                go_left.wait_recv()
                block = region(held, shifted(coords, dim, 1), halves[1])
                pass_left = copies.send(block, block, left)
            yield
            pass_right.wait_recv()
            if pass_left is None:
                go_left.wait_recv()
            else:
                pass_left.wait_recv()
        held.append(dim)


def leading_index(flat, dims):
    index = []
    for dim in reversed(dims):
        index.insert(0, lax.rem(flat, SIZES[dim]))
        flat = flat // SIZES[dim]
    return tuple(index)


def leading_shape(dims):
    return tuple(SIZES[dim] for dim in dims)


def over_leading(dims, step):
    count = math.prod(leading_shape(dims))
    if count == 1:
        step(())
        return

    def body(flat, carry):
        step(leading_index(flat, dims))
        return carry

    lax.fori_loop(0, count, body, 0)


def scatter_scratch(shape, order, axis):
    half = tuple(size // 2 if i == axis else size for i, size in enumerate(shape))
    buffers = []
    rest = list(DIMS)
    for dim in order:
        rest.remove(dim)
        lead = leading_shape(rest)
        if SIZES[dim] == 2:
            buffers.append(pltpu.VMEM(lead + shape, jnp.bfloat16))
        else:
            buffers.extend([pltpu.VMEM(lead + half, jnp.bfloat16)] * 8)
        if rest:
            buffers.append(pltpu.VMEM(lead + shape, jnp.bfloat16))
    return buffers


def scatter_flow(copies, coords, tp, source, result, buffers, order, axis):
    buffers = list(buffers)
    shape = source.shape[-2:]
    size = shape[axis] // 2
    halves = [
        tuple(pl.ds(h * size, size) if i == axis else slice(None) for i in range(2))
        for h in range(2)
    ]
    whole = (slice(None), slice(None))
    current = source
    dims = list(DIMS)

    for dim in order:
        rest = [d for d in dims if d != dim]
        spot = dims.index(dim)

        def at(where, lead, part, spot=spot, current=current):
            index = tuple(lead[:spot]) + (where[dim],) + tuple(lead[spot:])
            return current.at[index + part]

        everywhere = (slice(None),) * len(rest)
        right_coords = shifted(coords, dim, 1)
        right = device_at(right_coords, tp)
        f32 = jnp.float32
        if SIZES[dim] == 2:
            landed = buffers.pop(0)
            copy = copies.send(at(right_coords, everywhere, whole), landed, right)
            target = buffers.pop(0) if rest else result
            yield
            copy.wait_recv()

            def add(lead):
                total = at(coords, lead, whole)[...].astype(f32) + landed[lead + whole].astype(f32)
                target[lead + whole] = total.astype(target.dtype)

            over_leading(rest, add)
        else:
            left_coords = shifted(coords, dim, -1)
            far_coords = shifted(coords, dim, 2)
            left = device_at(left_coords, tp)
            pass_l, pass_r, near_l, near_r, sum_l, sum_r, out_r, out_l = buffers[:8]
            buffers = buffers[8:]
            target = buffers.pop(0) if rest else result
            relay_r = copies.send(at(far_coords, everywhere, halves[0]), pass_l, right)
            relay_l = copies.send(at(far_coords, everywhere, halves[1]), pass_r, left)
            direct_r = copies.send(at(right_coords, everywhere, halves[1]), near_l, right)
            direct_l = copies.send(at(left_coords, everywhere, halves[0]), near_r, left)
            yield
            relay_r.wait_recv()

            def merge_right(lead):
                total = at(right_coords, lead, halves[0])[...].astype(f32) + pass_l[
                    lead + whole
                ].astype(f32)
                out_r[lead + whole] = total.astype(out_r.dtype)

            over_leading(rest, merge_right)
            merged_r = copies.send(out_r, sum_l, right)
            relay_l.wait_recv()

            def merge_left(lead):
                total = at(left_coords, lead, halves[1])[...].astype(f32) + pass_r[
                    lead + whole
                ].astype(f32)
                out_l[lead + whole] = total.astype(out_l.dtype)

            over_leading(rest, merge_left)
            merged_l = copies.send(out_l, sum_r, left)
            yield
            direct_r.wait_recv()
            direct_l.wait_recv()
            merged_r.wait_recv()
            merged_l.wait_recv()

            def add(lead):
                for half, one, two in ((halves[0], sum_l, near_r), (halves[1], near_l, sum_r)):
                    total = (
                        at(coords, lead, half)[...].astype(f32)
                        + one[lead + whole].astype(f32)
                        + two[lead + whole].astype(f32)
                    )
                    target[lead + half] = total.astype(target.dtype)

            over_leading(rest, add)
        current = target
        dims = rest


def sum_everywhere_flow(copies, coords, tp, source, result, slots):
    current = source
    for stage, dim in enumerate(("x", "z")):
        ring = slots[stage]
        left = device_at(shifted(coords, dim, -1), tp)
        right = device_at(shifted(coords, dim, 1), tp)
        spot = coords[dim]
        ring[spot] = current[...]
        go_right = copies.send(current, ring.at[spot], right)
        go_left = copies.send(current, ring.at[spot], left)
        yield
        go_right.wait_recv()
        block = ring.at[shifted(coords, dim, -1)[dim]]
        passed = copies.send(block, block, right)
        yield
        go_left.wait_recv()
        passed.wait_recv()
        total = slots[5 + stage]
        total[...] = ring[0] + ring[1] + ring[2] + ring[3]
        current = total
    partners = (
        device_at(shifted(coords, "y", 1), tp),
        (lax.axis_index("ctx"), tp + 1 - 2 * lax.rem(tp, 2)),
        (lax.axis_index("ctx"), lax.rem(tp + 2, 4)),
    )
    for stage, partner in enumerate(partners):
        landed = slots[2 + stage]
        copy = copies.send(current, landed, partner)
        yield
        copy.wait_recv()
        total = slots[7 + stage] if stage < 2 else result
        total[...] = current[...] + landed[...]
        current = total


def sum_everywhere_scratch(shape):
    return [pltpu.VMEM((4,) + shape, jnp.float32)] * 2 + [pltpu.VMEM(shape, jnp.float32)] * 7


def tp_sum_flow(copies, ins, out, landed, chip, far, partner_core, partner_far, core, first, count, rows):
    half = rows // 2
    mine = pl.ds(pl.multiple_of(core * half + first, 16), count)
    theirs = pl.ds(pl.multiple_of((1 - core) * half + first, 16), count)
    local = pl.ds(first, count)
    f32 = jnp.float32
    copy = copies.send(ins.at[theirs], landed.at[local], partner_core)
    yield
    copy.wait_recv()
    chip[local] = (ins[mine].astype(f32) + landed[local].astype(f32)).astype(chip.dtype)
    copy = copies.send(chip.at[local], far.at[local], partner_far)
    yield
    copy.wait_recv()
    out[mine] = (chip[local].astype(f32) + far[local].astype(f32)).astype(out.dtype)
    copy = copies.send(out.at[mine], out.at[mine], partner_core)
    yield
    copy.wait_recv()


def write_results_kernel(*refs):
    number = len(refs) // 2
    for source, target in zip(refs[:number], refs[number:]):
        if source.shape == target.shape:
            target[...] = source[...]
        else:
            target[...] = source[...].T


def write_results(arrays, flipped):
    vmem = pl.BlockSpec(memory_space=pltpu.VMEM)
    return pl.pallas_call(
        write_results_kernel,
        out_shape=tuple(
            jax.ShapeDtypeStruct(a.shape[::-1] if flip else a.shape, a.dtype)
            for a, flip in zip(arrays, flipped)
        ),
        in_specs=[vmem] * len(arrays),
        out_specs=(vmem,) * len(arrays),
        compiler_params=pltpu.CompilerParams(vmem_limit_bytes=24 << 20),
        name="write_results",
    )(*arrays)


def rms_scale(values):
    return lax.rsqrt(jnp.mean(values * values, axis=-1, keepdims=True) + EPSILON)


def norm_backward(grad, normed, scale_rows):
    return scale_rows * (grad - normed * jnp.mean(grad * normed, axis=-1, keepdims=True))


def rope_tables(positions, head_dim):
    half_dim = head_dim // 2
    freqs = jnp.exp(
        -(2.0 * jnp.arange(half_dim, dtype=jnp.float32) / head_dim) * math.log(ROPE_BASE)
    )
    angles = positions.astype(jnp.float32)[:, None] * freqs[None, :]
    return (jnp.cos(angles), jnp.sin(angles))


XZY, ZYX, YXZ = ("x", "z", "y"), ("z", "y", "x"), ("y", "x", "z")
ROW_PARTS = ((XZY, 0, 48), (ZYX, 48, 48), (YXZ, 96, 32))
WEIGHT_ORDERS = {
    "gate": ZYX, "up": XZY, "down": YXZ, "out": YXZ, "query": XZY, "key": ZYX, "value": YXZ,
}
F32, BF16 = jnp.float32, jnp.bfloat16


def rope(values, cosine, sine):
    return values * cosine + pltpu.roll(values, 64, 1) * sine


def rope_back(grad, cosine, sine):
    return grad * cosine - pltpu.roll(grad, 64, 1) * sine


def dot(left, right):
    return jnp.dot(left, right, preferred_element_type=F32)


def stacked(ref, head, groups, width):
    return jnp.concatenate(
        [ref[:, (head * groups + g) * width : (head * groups + g + 1) * width] for g in range(groups)],
        axis=0,
    )


def transposed_dot(left, right):
    return lax.dot_general(left, right, (((1,), (1,)), ((), ())), preferred_element_type=F32)


def first_dims_dot(left, right):
    return lax.dot_general(left, right, (((0,), (0,)), ((), ())), preferred_element_type=F32)


def masked_scores(keys, queries, starts, q_pos, inv_root):
    scores = transposed_dot(keys, queries) * inv_root
    step = lax.broadcasted_iota(jnp.int32, (64, queries.shape[0]), 0)
    pieces = []
    for b, start in enumerate(starts):
        ahead = q_pos - start
        pieces.append(jnp.where(ahead >= step, scores[b * 64 : (b + 1) * 64], MASKED))
    return jnp.concatenate(pieces, axis=0)


def step_forward(flows):
    return [flow for flow in flows if next(flow, "done") != "done"]


def tokens_product(left_ref, right, target):
    def step(i, carry):
        block = left_ref[:, pl.ds(pl.multiple_of(i * 128, 128), 128)]
        part = first_dims_dot(block, right).astype(BF16)
        target[i // 4, lax.rem(i, 4)] = part.reshape(4, 32, right.shape[1])
        return carry

    lax.fori_loop(0, left_ref.shape[1] // 128, step, 0)


def layer_kernel(r, sizes):
    heads_kv, groups, width = sizes
    heads_q = heads_kv * groups
    rows = r.x.shape[0]
    inv_root = 1.0 / math.sqrt(width)
    kv_width = heads_kv * width
    coords, tp = place()
    ctx = lax.axis_index("ctx")
    core = lax.rem(tp, 2)
    partner_core = (ctx, tp + 1 - 2 * core)
    partner_far = (ctx, lax.rem(tp + 2, 4))
    peers = torus_peers(coords, tp) + [partner_core, partner_far]
    own = (coords["y"], coords["z"], coords["x"])
    copies = Copies(r.send_sem, r.recv_sem)

    barrier = pltpu.get_barrier_semaphore()
    for peer in peers:
        pl.semaphore_signal(barrier, inc=1, device_id=peer, device_id_type=MESH)

    loads = {}
    for i, name in enumerate(WEIGHT_NAMES):
        loads[name] = pltpu.make_async_copy(
            getattr(r, name + "_hbm"), getattr(r, name), r.load_sem.at[i]
        )
        loads[name].start()

    cosine, sine = r.cosine[...], r.sine[...]
    x = r.x[...]
    r1 = rms_scale(x)
    xhat1 = x * r1
    normed1 = (xhat1 * r.attention_gain[...]).astype(BF16)
    r.normed1[...] = normed1
    r.r1[...] = r1
    loads["w_k"].wait()
    unnormed = dot(normed1, r.w_k[...])
    for head in range(heads_kv):
        part = unnormed[:, head * width : (head + 1) * width]
        scale = rms_scale(part)
        hat = part * scale
        r.khat[:, head * width : (head + 1) * width] = hat
        r.rk[head] = scale
        r.kv_all[own + (slice(None), slice(head * width, (head + 1) * width))] = rope(
            hat * r.key_gain[...], cosine, sine
        ).astype(BF16)
    loads["w_v"].wait()
    r.kv_all[own + (slice(None), slice(kv_width, 2 * kv_width))] = dot(normed1, r.w_v[...]).astype(BF16)
    r.pos_all[own] = r.starts[...]
    pl.semaphore_wait(barrier, len(peers))
    flows = []
    for order, first, count in ROW_PARTS:
        part_rows = pl.ds(first, count)
        flows.append(
            gather_flow(
                copies, coords, tp, r.kv_all, order,
                (part_rows, slice(None)),
                ((part_rows, pl.ds(0, kv_width)), (part_rows, pl.ds(kv_width, kv_width))),
            )
        )
    whole = (slice(None), slice(None))
    flows.append(gather_flow(copies, coords, tp, r.pos_all, ("y", "z", "x"), whole, (whole, None)))
    flows = step_forward(flows)
    loads["w_q"].wait()
    queries = dot(normed1, r.w_q[...])
    for head in range(heads_q):
        part = queries[:, head * width : (head + 1) * width]
        scale = rms_scale(part)
        hat = part * scale
        r.qhat[:, head * width : (head + 1) * width] = hat
        r.rq[head] = scale
        r.q_rot[:, head * width : (head + 1) * width] = rope(
            hat * r.query_gain[...], cosine, sine
        ).astype(BF16)
    run_together(flows)

    q_pos = r.q_pos[...]
    per = 4 * rows

    def chunk_starts(i):
        starts = []
        for c in range(4):
            row = r.pos_all[i // 4, lax.rem(i, 4), c]
            for b in range(2):
                piece = row[:, b * 128 : (b + 1) * 128]
                starts.append(jnp.concatenate([piece] * groups, axis=1))
        return starts

    def chunk_of(i, begin):
        return r.kv_all[i // 4, lax.rem(i, 4), :, :, begin : begin + width].reshape(per, width)

    for head in range(heads_kv):
        head_queries = stacked(r.q_rot, head, groups, width)

        def score_step(i, top, head=head, head_queries=head_queries):
            scores = masked_scores(
                chunk_of(i, head * width), head_queries, chunk_starts(i), q_pos, inv_root
            )
            r.scores[pl.ds(pl.multiple_of(i * per, per), per), :] = scores
            return jnp.maximum(top, jnp.max(scores, axis=0, keepdims=True))

        top = lax.fori_loop(0, 8, score_step, jnp.full((1, groups * rows), MASKED, F32))

        def weight_step(i, carry, head=head, top=top):
            total, mixed = carry
            values = chunk_of(i, kv_width + head * width)
            weights = jnp.exp(r.scores[pl.ds(pl.multiple_of(i * per, per), per), :] - top)
            total = total + jnp.sum(weights, axis=0, keepdims=True)
            return total, mixed + first_dims_dot(values, weights.astype(BF16))

        total, mixed = lax.fori_loop(
            0, 8, weight_step,
            (jnp.zeros((1, groups * rows), F32), jnp.zeros((width, groups * rows), F32)),
        )
        mixed = mixed / total
        r.lse[head] = top + jnp.log(total)
        for g in range(groups):
            first = (head * groups + g) * width
            r.att[:, first : first + width] = mixed[:, g * rows : (g + 1) * rows].T

    def sum_flows(which, pieces=2):
        half = rows // 2
        count = half // pieces
        return [
            tp_sum_flow(
                copies, r.sum_in.at[which], r.sum_out.at[which], r.sum_landed.at[which],
                r.sum_chip.at[which], r.sum_far.at[which], partner_core, partner_far, core,
                piece * count, count, rows,
            )
            for piece in range(pieces)
        ]

    attb = r.att[...].astype(BF16)
    loads["w_o"].wait()
    r.sum_in[0] = dot(attb, r.w_o[...]).astype(BF16)
    flows = step_forward(sum_flows(0))
    for name in ("w_gate", "w_up", "w_down"):
        loads[name].wait()
    r.gob[...] = r.cotangent[...].astype(BF16)
    r.dhid[...] = transposed_dot(r.gob[...], r.w_down[...])
    run_together(flows)
    xmid = r.x[...] + r.sum_out[0].astype(F32)
    r.xmid[...] = xmid

    r2 = rms_scale(xmid)
    xhat2 = xmid * r2
    r.r2[...] = r2
    normed2 = (xhat2 * r.ffn_gain[...]).astype(BF16)
    r.normed2[...] = normed2
    gate = dot(normed2, r.w_gate[...])
    up = dot(normed2, r.w_up[...])
    sig = jax.nn.sigmoid(gate)
    silu = gate * sig
    hid = (silu * up).astype(BF16)
    d_hid = r.dhid[...]
    d_gate = (d_hid * up * sig * (1.0 + gate * (1.0 - sig))).astype(BF16)
    d_up = (d_hid * silu).astype(BF16)
    r.hid[...] = hid
    r.d_gate[...] = d_gate
    r.d_up[...] = d_up
    dn2_part = transposed_dot(d_gate, r.w_gate[...]) + transposed_dot(d_up, r.w_up[...])
    r.ffn_small[...] = jnp.sum(dn2_part * xhat2, axis=0, keepdims=True)
    r.sum_in[1] = dn2_part.astype(BF16)
    sums = step_forward(sum_flows(1))
    r.sum_in[2] = dot(r.hid[...], r.w_down[...]).astype(BF16)
    hidden_sums = sum_flows(2)

    def weight_flow(name):
        source = getattr(r, "g_" + name)
        return scatter_flow(
            copies, coords, tp, source, getattr(r, "grad_" + name),
            r.weight_buffers[name], WEIGHT_ORDERS[name], 0,
        )

    sums = step_forward(sums)
    tokens_product(r.normed2, r.d_gate[...], r.g_gate)
    scatters = [weight_flow("gate")]
    scatters = step_forward(scatters)
    sums = step_forward(sums)
    hidden_sums = step_forward(hidden_sums)
    tokens_product(r.normed2, r.d_up[...], r.g_up)
    scatters = scatters + step_forward([weight_flow("up")])
    run_together(sums)

    dn2 = r.sum_out[1].astype(F32)
    xhat2 = r.xmid[...] * r.r2[...]
    dmid = r.cotangent[...] + norm_backward(dn2 * r.ffn_gain[...], xhat2, r.r2[...])
    r.dmid[...] = dmid
    dmidb = dmid.astype(BF16)
    r.dmidb[...] = dmidb
    d_att = transposed_dot(dmidb, r.w_o[...])
    r.d_attb[...] = d_att.astype(BF16)
    for head in range(heads_kv):
        pieces = []
        for g in range(groups):
            first = (head * groups + g) * width
            product = d_att[:, first : first + width] * r.att[:, first : first + width]
            pieces.append(jnp.sum(product.T, axis=0, keepdims=True))
        r.delta[head] = jnp.concatenate(pieces, axis=1)
    tokens_product(r.gob, r.hid[...], r.g_down)
    scatters = scatters + step_forward([weight_flow("down")])
    tokens_product(r.dmidb, r.att[...].astype(BF16), r.g_out)
    scatters = scatters + step_forward([weight_flow("out")])
    hidden_sums = step_forward(hidden_sums)

    r.dq_acc[...] = jnp.zeros_like(r.dq_acc)

    def backward_step(i, carry):
        starts = chunk_starts(i)
        for head in range(heads_kv):
            head_queries = stacked(r.q_rot, head, groups, width)
            grads = stacked(r.d_attb, head, groups, width)
            base = kv_width + head * width
            keys = chunk_of(i, head * width)
            values = chunk_of(i, base)
            scores = masked_scores(keys, head_queries, starts, q_pos, inv_root)
            probs = jnp.exp(scores - r.lse[head])
            d_prob = transposed_dot(values, grads)
            d_scores = (probs * (d_prob - r.delta[head])).astype(BF16)
            d_keys = dot(d_scores, head_queries) * inv_root
            d_values = dot(probs.astype(BF16), grads)
            where = (i // 4, lax.rem(i, 4), slice(None), slice(None))
            shape = (4, rows, width)
            r.dkv[where + (slice(head * width, (head + 1) * width),)] = d_keys.astype(BF16).reshape(shape)
            r.dkv[where + (slice(base, base + width),)] = d_values.astype(BF16).reshape(shape)
            r.dq_acc[head] += first_dims_dot(keys, d_scores)
        return carry

    lax.fori_loop(0, 4, backward_step, 0)
    run_together(hidden_sums)
    scatters = step_forward(scatters)
    lax.fori_loop(4, 8, backward_step, 0)
    late = []
    for (order, first, count), buffers in zip(ROW_PARTS, r.kv_buffers):
        part_rows = pl.ds(first, count)
        late.append(
            scatter_flow(
                copies, coords, tp, r.dkv.at[:, :, :, part_rows, :],
                r.dkv_own.at[part_rows, :], buffers, order, 1,
            )
        )
    late = step_forward(late)
    r.hidden_out[...] = r.xmid[...] + r.sum_out[2].astype(F32)

    small_q = jnp.zeros((1, width), F32)
    for head in range(heads_kv):
        for g in range(groups):
            index = head * groups + g
            here = slice(index * width, (index + 1) * width)
            grad = rope_back(r.dq_acc[head, :, g * rows : (g + 1) * rows].T * inv_root, cosine, sine)
            hat = r.qhat[:, here]
            small_q = small_q + jnp.sum(grad * hat, axis=0, keepdims=True)
            r.dqb[:, here] = norm_backward(grad * r.query_gain[...], hat, r.rq[index]).astype(BF16)
    tokens_product(r.normed1, r.dqb[...], r.g_query)
    r.dn1[...] = transposed_dot(r.dqb[...], r.w_q[...])
    late = step_forward(late)
    scatters = step_forward(scatters)
    scatters = scatters + step_forward([weight_flow("query")])
    while late:
        late = step_forward(late)
        scatters = step_forward(scatters)

    small_k = jnp.zeros((1, width), F32)
    for head in range(heads_kv):
        here = slice(head * width, (head + 1) * width)
        grad = rope_back(r.dkv_own[:, here], cosine, sine)
        hat = r.khat[:, here]
        small_k = small_k + jnp.sum(grad * hat, axis=0, keepdims=True)
        r.dkb[:, here] = norm_backward(grad * r.key_gain[...], hat, r.rk[head]).astype(BF16)
    r.dvb[...] = r.dkv_own[:, kv_width:].astype(BF16)
    dn1_part = (
        r.dn1[...] + transposed_dot(r.dkb[...], r.w_k[...]) + transposed_dot(r.dvb[...], r.w_v[...])
    )
    xhat1 = r.x[...] * r.r1[...]
    r.sum_in[3] = dn1_part.astype(BF16)
    sums = step_forward(sum_flows(3))
    r.small_in[0:1, 0:1024] = jnp.sum(dn1_part * xhat1, axis=0, keepdims=True)
    r.small_in[0:1, 1024:2048] = r.ffn_small[...]
    r.small_in[0:1, 2048:2176] = small_q
    r.small_in[0:1, 2176:2304] = small_k
    tokens_product(r.normed1, r.dkb[...], r.g_key)
    tokens_product(r.normed1, r.dvb[...], r.g_value)
    last = [weight_flow("key"), weight_flow("value")]
    small = [sum_everywhere_flow(copies, coords, tp, r.small_in, r.small_out, r.small_slots)]
    flows = step_forward(last + small)
    sums = step_forward(sums)
    scatters = step_forward(scatters)
    flows = step_forward(flows)
    run_together(sums)
    dn1 = r.sum_out[3].astype(F32)
    r.input_gradient[...] = r.dmid[...] + norm_backward(
        dn1 * r.attention_gain[...], r.x[...] * r.r1[...], r.r1[...]
    )
    run_together(flows + scatters)
    copies.drain()


WEIGHT_NAMES = ("w_k", "w_v", "w_q", "w_o", "w_gate", "w_up", "w_down")


def whole_layer(
    layer_input, cotangent, weights, gains, cosine, sine, starts, q_pos, heads_kv, groups
):
    rows, features = layer_input.shape
    width = cosine.shape[1]
    heads_q = heads_kv * groups
    q_width, kv_width = heads_q * width, heads_kv * width
    hidden = weights["w_gate"].shape[1]
    vmem = pl.BlockSpec(memory_space=pltpu.VMEM)
    hbm = pl.BlockSpec(memory_space=pl.ANY)
    inputs = {
        "x": layer_input, "cotangent": cotangent, "cosine": cosine, "sine": sine,
        "starts": starts, "q_pos": q_pos, **gains,
    }
    columns = {
        "gate": hidden, "up": hidden, "down": hidden, "out": q_width,
        "query": q_width, "key": kv_width, "value": kv_width,
    }
    outputs = {
        "hidden_out": ((rows, features), F32),
        "input_gradient": ((rows, features), F32),
        "small_out": ((1, 2304), F32),
    }
    for name, count in columns.items():
        outputs["grad_" + name] = ((32, count), F32)
    scratch = {
        "send_sem": pltpu.SemaphoreType.DMA((210,)),
        "recv_sem": pltpu.SemaphoreType.DMA((210,)),
        "load_sem": pltpu.SemaphoreType.DMA((len(WEIGHT_NAMES),)),
    }
    for name in WEIGHT_NAMES:
        scratch[name] = pltpu.VMEM(weights[name].shape, BF16)
    for name, shape, kind in (
        ("normed1", (rows, features), BF16),
        ("normed2", (rows, features), BF16),
        ("gob", (rows, features), BF16),
        ("dmidb", (rows, features), BF16),
        ("r1", (rows, 1), F32),
        ("r2", (rows, 1), F32),
        ("rq", (heads_q, rows, 1), F32),
        ("rk", (heads_kv, rows, 1), F32),
        ("qhat", (rows, q_width), F32),
        ("khat", (rows, kv_width), F32),
        ("q_rot", (rows, q_width), BF16),
        ("kv_all", (2, 4, 4, rows, 2 * kv_width), BF16),
        ("pos_all", (2, 4, 4, 1, 256), jnp.int32),
        ("scores", (32 * rows, groups * rows), F32),
        ("lse", (heads_kv, 1, groups * rows), F32),
        ("delta", (heads_kv, 1, groups * rows), F32),
        ("att", (rows, q_width), F32),
        ("sum_in", (4, rows, features), BF16),
        ("sum_out", (4, rows, features), BF16),
        ("sum_landed", (4, rows // 2, features), BF16),
        ("sum_chip", (4, rows // 2, features), BF16),
        ("sum_far", (4, rows // 2, features), BF16),
        ("xmid", (rows, features), F32),
        ("dmid", (rows, features), F32),
        ("dn1", (rows, features), F32),
        ("dhid", (rows, hidden), F32),
        ("hid", (rows, hidden), BF16),
        ("d_gate", (rows, hidden), BF16),
        ("d_up", (rows, hidden), BF16),
        ("ffn_small", (1, features), F32),
        ("d_attb", (rows, q_width), BF16),
        ("dq_acc", (heads_kv, width, groups * rows), F32),
        ("dkv", (2, 4, 4, rows, 2 * kv_width), BF16),
        ("dkv_own", (rows, 2 * kv_width), F32),
        ("dqb", (rows, q_width), BF16),
        ("dkb", (rows, kv_width), BF16),
        ("dvb", (rows, kv_width), BF16),
        ("small_in", (1, 2304), F32),
    ):
        scratch[name] = pltpu.VMEM(shape, kind)
    for name, count in columns.items():
        scratch["g_" + name] = pltpu.VMEM((2, 4, 4, 32, count), BF16)
    lists = {"small_slots": sum_everywhere_scratch((1, 2304))}
    for name, count in columns.items():
        lists["weight_" + name] = scatter_scratch((32, count), WEIGHT_ORDERS[name], 0)
    for i, (order, first, count) in enumerate(ROW_PARTS):
        lists["kv_%d" % i] = scatter_scratch((count, 2 * kv_width), order, 1)

    input_names = list(inputs) + [name + "_hbm" for name in WEIGHT_NAMES]
    flat_scratch = list(scratch.values())
    for buffers in lists.values():
        flat_scratch.extend(buffers)

    def kernel(*refs):
        r = types.SimpleNamespace()
        names = input_names + list(outputs) + list(scratch)
        for name, ref in zip(names, refs):
            setattr(r, name, ref)
        rest = list(refs[len(names) :])
        groups_of = {}
        for name, buffers in lists.items():
            groups_of[name], rest = rest[: len(buffers)], rest[len(buffers) :]
        r.small_slots = groups_of["small_slots"]
        r.weight_buffers = {name: groups_of["weight_" + name] for name in columns}
        r.kv_buffers = [groups_of["kv_%d" % i] for i in range(len(ROW_PARTS))]
        layer_kernel(r, (heads_kv, groups, width))

    results = pl.pallas_call(
        kernel,
        out_shape=tuple(jax.ShapeDtypeStruct(shape, kind) for shape, kind in outputs.values()),
        in_specs=[vmem] * len(inputs) + [hbm] * len(WEIGHT_NAMES),
        out_specs=(vmem,) * len(outputs),
        scratch_shapes=flat_scratch,
        compiler_params=pltpu.CompilerParams(
            collective_id=0, has_side_effects=True, vmem_limit_bytes=67043328
        ),
        name="whole_layer",
    )(*inputs.values(), *[weights[name] for name in WEIGHT_NAMES])
    return dict(zip(outputs, results))


def body(
    layer_input,
    positions,
    attention_norm_gain,
    w_query,
    key_projection,
    value_projection,
    query_norm,
    key_norm_gain,
    output_projection,
    feedforward_norm_gain,
    w_gate,
    w_up,
    w_down,
    output_cotangent,
):
    head_dim = query_norm.shape[0]
    heads_q = w_query.shape[1] // head_dim
    heads_kv = key_projection.shape[1] // head_dim
    groups = heads_q // heads_kv
    cosine, sine = rope_tables(positions, head_dim)
    out = whole_layer(
        layer_input,
        output_cotangent,
        {
            "w_q": w_query, "w_k": key_projection, "w_v": value_projection, "w_o": output_projection,
            "w_gate": w_gate, "w_up": w_up, "w_down": w_down,
        },
        {
            "attention_gain": attention_norm_gain.reshape(1, -1),
            "ffn_gain": feedforward_norm_gain.reshape(1, -1),
            "query_gain": query_norm.reshape(1, -1),
            "key_gain": key_norm_gain.reshape(1, -1),
        },
        jnp.concatenate([cosine, cosine], axis=1),
        jnp.concatenate([-sine, sine], axis=1),
        jnp.repeat(positions.reshape(-1, 64)[:, 0], 128).reshape(1, 256),
        jnp.tile(positions, groups).reshape(1, -1),
        heads_kv,
        groups,
    )
    names = (
        "hidden_out", "input_gradient", "grad_query", "grad_key", "grad_value", "grad_out",
        "grad_gate", "grad_up", "grad_down", "small_out",
    )
    done = dict(zip(names, write_results([out[name] for name in names], [False] * len(names))))
    small = done["small_out"].reshape(-1)
    return (
        done["hidden_out"],
        done["input_gradient"],
        small[:1024],
        done["grad_query"],
        done["grad_key"],
        done["grad_value"],
        small[2048:2176],
        small[2176:2304],
        done["grad_out"].T,
        small[1024:2048],
        done["grad_gate"],
        done["grad_up"],
        done["grad_down"].T,
    )


def solution(mesh):
    return jax.shard_map(
        body,
        mesh=mesh,
        in_specs=(
            P("ctx", None),
            P("ctx"),
            P(),
            P(None, "tp"),
            P(None, "tp"),
            P(None, "tp"),
            P(),
            P(),
            P("tp", None),
            P(),
            P(None, "tp"),
            P(None, "tp"),
            P("tp", None),
            P("ctx", None),
        ),
        out_specs=(
            P("ctx", None),
            P("ctx", None),
            P(),
            P("ctx", "tp"),
            P("ctx", "tp"),
            P("ctx", "tp"),
            P(),
            P(),
            P("tp", "ctx"),
            P(),
            P("ctx", "tp"),
            P("ctx", "tp"),
            P("tp", "ctx"),
        ),
        check_vma=False,
    )
```

```python
import math
import types

import jax
import jax.numpy as jnp
from jax import lax
from jax.experimental import pallas as pl
from jax.experimental.pallas import tpu as pltpu
from jax.sharding import PartitionSpec as P

EPSILON = 1e-06
ROPE_BASE = 1000000.0
MASKED = -1e30


MESH = pl.DeviceIdType.MESH
SIZES = {"y": 2, "z": 4, "x": 4}
DIMS = ("y", "z", "x")


def place():
    me = lax.axis_index("ctx")
    return {"y": me // 16, "z": lax.rem(me // 4, 4), "x": lax.rem(me, 4)}, lax.axis_index("tp")


def shifted(coords, dim, step):
    moved = dict(coords)
    moved[dim] = lax.rem(coords[dim] + step + SIZES[dim], SIZES[dim])
    return moved


def device_at(coords, tp):
    return (coords["y"] * 16 + coords["z"] * 4 + coords["x"], tp)


def torus_peers(coords, tp):
    peers = [device_at(shifted(coords, "y", 1), tp)]
    for dim in ("z", "x"):
        peers.append(device_at(shifted(coords, dim, 1), tp))
        peers.append(device_at(shifted(coords, dim, -1), tp))
    return peers


def greet(peers):
    barrier = pltpu.get_barrier_semaphore()
    for peer in peers:
        pl.semaphore_signal(barrier, inc=1, device_id=peer, device_id_type=MESH)
    pl.semaphore_wait(barrier, len(peers))


class Copies:
    def __init__(self, send_sem, recv_sem):
        self.send_sem, self.recv_sem = send_sem, recv_sem
        self.count = 0
        self.started = []

    def make(self, source, target, device):
        slot = self.count
        self.count += 1
        return pltpu.make_async_remote_copy(
            src_ref=source,
            dst_ref=target,
            send_sem=self.send_sem.at[slot],
            recv_sem=self.recv_sem.at[slot],
            device_id=device,
            device_id_type=MESH,
        )

    def send(self, source, target, device):
        copy = self.make(source, target, device)
        copy.start()
        self.started.append(copy)
        return copy

    def drain(self):
        for copy in self.started:
            copy.wait_send()


def run_together(flows):
    live = list(flows)
    while live:
        left = []
        for flow in live:
            try:
                next(flow)
                left.append(flow)
            except StopIteration:
                pass
        live = left


def gather_flow(copies, coords, tp, ref, order, piece, halves):
    def region(held, where, part):
        index = tuple(slice(None) if dim in held else where[dim] for dim in DIMS)
        return ref.at[index + part]

    held = []
    for dim in order:
        right = device_at(shifted(coords, dim, 1), tp)
        mine = region(held, coords, piece)
        if SIZES[dim] == 2:
            copy = copies.send(mine, mine, right)
            yield
            copy.wait_recv()
        else:
            left = device_at(shifted(coords, dim, -1), tp)
            go_right = copies.send(mine, mine, right)
            go_left = copies.send(mine, mine, left)
            yield
            go_right.wait_recv()
            block = region(held, shifted(coords, dim, -1), halves[0])
            pass_right = copies.send(block, block, right)
            pass_left = None
            if halves[1] is not None:
                go_left.wait_recv()
                block = region(held, shifted(coords, dim, 1), halves[1])
                pass_left = copies.send(block, block, left)
            yield
            pass_right.wait_recv()
            if pass_left is None:
                go_left.wait_recv()
            else:
                pass_left.wait_recv()
        held.append(dim)


def leading_index(flat, dims):
    index = []
    for dim in reversed(dims):
        index.insert(0, lax.rem(flat, SIZES[dim]))
        flat = flat // SIZES[dim]
    return tuple(index)


def leading_shape(dims):
    return tuple(SIZES[dim] for dim in dims)


def over_leading(dims, step):
    count = math.prod(leading_shape(dims))
    if count == 1:
        step(())
        return

    def body(flat, carry):
        step(leading_index(flat, dims))
        return carry

    lax.fori_loop(0, count, body, 0)


def scatter_scratch(shape, order, axis):
    half = tuple(size // 2 if i == axis else size for i, size in enumerate(shape))
    buffers = []
    rest = list(DIMS)
    for dim in order:
        rest.remove(dim)
        lead = leading_shape(rest)
        if SIZES[dim] == 2:
            buffers.append(pltpu.VMEM(lead + shape, jnp.bfloat16))
        else:
            buffers.extend([pltpu.VMEM(lead + half, jnp.bfloat16)] * 8)
        if rest:
            buffers.append(pltpu.VMEM(lead + shape, jnp.bfloat16))
    return buffers


def scatter_flow(copies, coords, tp, source, result, buffers, order, axis):
    buffers = list(buffers)
    shape = source.shape[-2:]
    size = shape[axis] // 2
    halves = [
        tuple(pl.ds(h * size, size) if i == axis else slice(None) for i in range(2))
        for h in range(2)
    ]
    whole = (slice(None), slice(None))
    current = source
    dims = list(DIMS)

    for dim in order:
        rest = [d for d in dims if d != dim]
        spot = dims.index(dim)

        def at(where, lead, part, spot=spot, current=current):
            index = tuple(lead[:spot]) + (where[dim],) + tuple(lead[spot:])
            return current.at[index + part]

        everywhere = (slice(None),) * len(rest)
        right_coords = shifted(coords, dim, 1)
        right = device_at(right_coords, tp)
        f32 = jnp.float32
        if SIZES[dim] == 2:
            landed = buffers.pop(0)
            copy = copies.send(at(right_coords, everywhere, whole), landed, right)
            target = buffers.pop(0) if rest else result
            yield
            copy.wait_recv()

            def add(lead):
                total = at(coords, lead, whole)[...].astype(f32) + landed[lead + whole].astype(f32)
                target[lead + whole] = total.astype(target.dtype)

            over_leading(rest, add)
        else:
            left_coords = shifted(coords, dim, -1)
            far_coords = shifted(coords, dim, 2)
            left = device_at(left_coords, tp)
            pass_l, pass_r, near_l, near_r, sum_l, sum_r, out_r, out_l = buffers[:8]
            buffers = buffers[8:]
            target = buffers.pop(0) if rest else result
            relay_r = copies.send(at(far_coords, everywhere, halves[0]), pass_l, right)
            relay_l = copies.send(at(far_coords, everywhere, halves[1]), pass_r, left)
            direct_r = copies.send(at(right_coords, everywhere, halves[1]), near_l, right)
            direct_l = copies.send(at(left_coords, everywhere, halves[0]), near_r, left)
            yield
            relay_r.wait_recv()

            def merge_right(lead):
                total = at(right_coords, lead, halves[0])[...].astype(f32) + pass_l[
                    lead + whole
                ].astype(f32)
                out_r[lead + whole] = total.astype(out_r.dtype)

            over_leading(rest, merge_right)
            merged_r = copies.send(out_r, sum_l, right)
            relay_l.wait_recv()

            def merge_left(lead):
                total = at(left_coords, lead, halves[1])[...].astype(f32) + pass_r[
                    lead + whole
                ].astype(f32)
                out_l[lead + whole] = total.astype(out_l.dtype)

            over_leading(rest, merge_left)
            merged_l = copies.send(out_l, sum_r, left)
            yield
            direct_r.wait_recv()
            direct_l.wait_recv()
            merged_r.wait_recv()
            merged_l.wait_recv()

            def add(lead):
                for half, one, two in ((halves[0], sum_l, near_r), (halves[1], near_l, sum_r)):
                    total = (
                        at(coords, lead, half)[...].astype(f32)
                        + one[lead + whole].astype(f32)
                        + two[lead + whole].astype(f32)
                    )
                    target[lead + half] = total.astype(target.dtype)

            over_leading(rest, add)
        current = target
        dims = rest


def sum_everywhere_flow(copies, coords, tp, source, result, slots):
    current = source
    for stage, dim in enumerate(("x", "z")):
        ring = slots[stage]
        left = device_at(shifted(coords, dim, -1), tp)
        right = device_at(shifted(coords, dim, 1), tp)
        spot = coords[dim]
        ring[spot] = current[...]
        go_right = copies.send(current, ring.at[spot], right)
        go_left = copies.send(current, ring.at[spot], left)
        yield
        go_right.wait_recv()
        block = ring.at[shifted(coords, dim, -1)[dim]]
        passed = copies.send(block, block, right)
        yield
        go_left.wait_recv()
        passed.wait_recv()
        total = slots[5 + stage]
        total[...] = ring[0] + ring[1] + ring[2] + ring[3]
        current = total
    partners = (
        device_at(shifted(coords, "y", 1), tp),
        (lax.axis_index("ctx"), tp + 1 - 2 * lax.rem(tp, 2)),
        (lax.axis_index("ctx"), lax.rem(tp + 2, 4)),
    )
    for stage, partner in enumerate(partners):
        landed = slots[2 + stage]
        copy = copies.send(current, landed, partner)
        yield
        copy.wait_recv()
        total = slots[7 + stage] if stage < 2 else result
        total[...] = current[...] + landed[...]
        current = total


def sum_everywhere_scratch(shape):
    return [pltpu.VMEM((4,) + shape, jnp.float32)] * 2 + [pltpu.VMEM(shape, jnp.float32)] * 7


def tp_sum_flow(copies, ins, out, landed, chip, far, partner_core, partner_far, core, first, count, rows):
    half = rows // 2
    mine = pl.ds(pl.multiple_of(core * half + first, 16), count)
    theirs = pl.ds(pl.multiple_of((1 - core) * half + first, 16), count)
    local = pl.ds(first, count)
    f32 = jnp.float32
    copy = copies.send(ins.at[theirs], landed.at[local], partner_core)
    yield
    copy.wait_recv()
    chip[local] = (ins[mine].astype(f32) + landed[local].astype(f32)).astype(chip.dtype)
    copy = copies.send(chip.at[local], far.at[local], partner_far)
    yield
    copy.wait_recv()
    out[mine] = (chip[local].astype(f32) + far[local].astype(f32)).astype(out.dtype)
    copy = copies.send(out.at[mine], out.at[mine], partner_core)
    yield
    copy.wait_recv()


def write_results(arrays, splits):
    number = len(arrays)
    pieces = [(array.shape[0], size) for array, size in zip(arrays[-1:] * len(splits), splits)]
    shapes = [array.shape for array in arrays[:-1]] + pieces

    def kernel(*refs):
        ins, outs = refs[:number], refs[number : number + len(shapes)]
        held, (in_sem, out_sem) = refs[number + len(shapes) : -2], refs[-2:]
        loads = [
            pltpu.make_async_copy(source, target, in_sem.at[i])
            for i, (source, target) in enumerate(zip(ins, held))
        ]
        for load in loads:
            load.start()
        stores = []
        for i, load in enumerate(loads[:-1]):
            load.wait()
            stores.append(pltpu.make_async_copy(held[i], outs[i], out_sem.at[i]))
            stores[-1].start()
        loads[-1].wait()
        begin = 0
        for i, size in enumerate(splits):
            slot = number - 1 + i
            source = held[-1].at[:, pl.ds(begin, size)]
            stores.append(pltpu.make_async_copy(source, outs[slot], out_sem.at[slot]))
            stores[-1].start()
            begin += size
        for store in stores:
            store.wait()

    hbm = pl.BlockSpec(memory_space=pl.ANY)
    return pl.pallas_call(
        kernel,
        out_shape=tuple(jax.ShapeDtypeStruct(shape, jnp.float32) for shape in shapes),
        in_specs=[hbm] * number,
        out_specs=(hbm,) * len(shapes),
        scratch_shapes=[pltpu.VMEM(array.shape, jnp.float32) for array in arrays]
        + [pltpu.SemaphoreType.DMA((number,)), pltpu.SemaphoreType.DMA((len(shapes),))],
        compiler_params=pltpu.CompilerParams(vmem_limit_bytes=60 << 20),
        name="write_results",
    )(*arrays)


def rms_scale(values):
    return lax.rsqrt(jnp.mean(values * values, axis=-1, keepdims=True) + EPSILON)


def norm_backward(grad, normed, scale_rows):
    return scale_rows * (grad - normed * jnp.mean(grad * normed, axis=-1, keepdims=True))


def rope_tables(positions, head_dim):
    half_dim = head_dim // 2
    freqs = jnp.exp(
        -(2.0 * jnp.arange(half_dim, dtype=jnp.float32) / head_dim) * math.log(ROPE_BASE)
    )
    angles = positions.astype(jnp.float32)[:, None] * freqs[None, :]
    return (jnp.cos(angles), jnp.sin(angles))


XZY, ZYX, YXZ = ("x", "z", "y"), ("z", "y", "x"), ("y", "x", "z")
ROW_PARTS = ((XZY, 0, 48), (ZYX, 48, 48), (YXZ, 96, 32))
THREE_PARTS = ((XZY, 0, 256), (ZYX, 256, 256), (YXZ, 512, 256))
TWO_PARTS = ((XZY, 0, 256), (ZYX, 256, 256))
WEIGHT_PARTS = {
    "gate": THREE_PARTS,
    "up": THREE_PARTS,
    "down": THREE_PARTS,
    "out": TWO_PARTS,
    "query": TWO_PARTS,
    "key": ((YXZ, 0, 256),),
    "value": ((XZY, 0, 128), (ZYX, 128, 128)),
}
F32, BF16 = jnp.float32, jnp.bfloat16


def rope(values, cosine, sine):
    return values * cosine + pltpu.roll(values, 64, 1) * sine


def rope_back(grad, cosine, sine):
    return grad * cosine - pltpu.roll(grad, 64, 1) * sine


def dot(left, right):
    return jnp.dot(left, right, preferred_element_type=F32)


def stacked(ref, head, groups, width):
    return jnp.concatenate(
        [ref[:, (head * groups + g) * width : (head * groups + g + 1) * width] for g in range(groups)],
        axis=0,
    )


def transposed_dot(left, right):
    return lax.dot_general(left, right, (((1,), (1,)), ((), ())), preferred_element_type=F32)


def first_dims_dot(left, right):
    return lax.dot_general(left, right, (((0,), (0,)), ((), ())), preferred_element_type=F32)


def masked_scores(keys, queries, starts, q_pos, inv_root):
    scores = transposed_dot(keys, queries) * inv_root
    step = lax.broadcasted_iota(jnp.int32, (64, queries.shape[0]), 0)
    pieces = []
    for b, start in enumerate(starts):
        ahead = q_pos - start
        pieces.append(jnp.where(ahead >= step, scores[b * 64 : (b + 1) * 64], MASKED))
    return jnp.concatenate(pieces, axis=0)


def step_forward(flows):
    return [flow for flow in flows if next(flow, "done") != "done"]


def tokens_product(left_ref, right, target):
    def step(i, carry):
        block = left_ref[:, pl.ds(pl.multiple_of(i * 128, 128), 128)]
        part = first_dims_dot(block, right).astype(BF16)
        target[i // 4, lax.rem(i, 4)] = part.reshape(4, 32, right.shape[1])
        return carry

    lax.fori_loop(0, left_ref.shape[1] // 128, step, 0)


def layer_kernel(r, sizes):
    heads_kv, groups, width = sizes
    heads_q = heads_kv * groups
    rows = r.x.shape[0]
    inv_root = 1.0 / math.sqrt(width)
    kv_width = heads_kv * width
    coords, tp = place()
    ctx = lax.axis_index("ctx")
    core = lax.rem(tp, 2)
    partner_core = (ctx, tp + 1 - 2 * core)
    partner_far = (ctx, lax.rem(tp + 2, 4))
    peers = torus_peers(coords, tp) + [partner_core, partner_far]
    own = (coords["y"], coords["z"], coords["x"])
    copies = Copies(r.send_sem, r.recv_sem)

    barrier = pltpu.get_barrier_semaphore()
    for peer in peers:
        pl.semaphore_signal(barrier, inc=1, device_id=peer, device_id_type=MESH)

    loads = {}
    for i, name in enumerate(WEIGHT_NAMES):
        loads[name] = pltpu.make_async_copy(
            getattr(r, name + "_hbm"), getattr(r, name), r.load_sem.at[i]
        )
        loads[name].start()

    cosine, sine = r.cosine[...], r.sine[...]
    x = r.x[...]
    r1 = rms_scale(x)
    xhat1 = x * r1
    normed1 = (xhat1 * r.attention_gain[...]).astype(BF16)
    r.normed1[...] = normed1
    r.r1[...] = r1
    loads["w_k"].wait()
    unnormed = dot(normed1, r.w_k[...])
    for head in range(heads_kv):
        part = unnormed[:, head * width : (head + 1) * width]
        scale = rms_scale(part)
        hat = part * scale
        r.khat[:, head * width : (head + 1) * width] = hat
        r.rk[head] = scale
        r.kv_all[own + (slice(None), slice(head * width, (head + 1) * width))] = rope(
            hat * r.key_gain[...], cosine, sine
        ).astype(BF16)
    loads["w_v"].wait()
    r.kv_all[own + (slice(None), slice(kv_width, 2 * kv_width))] = dot(normed1, r.w_v[...]).astype(BF16)
    r.pos_all[own] = r.starts[...]
    pl.semaphore_wait(barrier, len(peers))
    flows = []
    for order, first, count in ROW_PARTS:
        part_rows = pl.ds(first, count)
        flows.append(
            gather_flow(
                copies, coords, tp, r.kv_all, order,
                (part_rows, slice(None)),
                ((part_rows, pl.ds(0, kv_width)), (part_rows, pl.ds(kv_width, kv_width))),
            )
        )
    whole = (slice(None), slice(None))
    flows.append(gather_flow(copies, coords, tp, r.pos_all, ("y", "z", "x"), whole, (whole, None)))
    flows = step_forward(flows)
    loads["w_q"].wait()
    queries = dot(normed1, r.w_q[...])
    for head in range(heads_q):
        part = queries[:, head * width : (head + 1) * width]
        scale = rms_scale(part)
        hat = part * scale
        r.qhat[:, head * width : (head + 1) * width] = hat
        r.rq[head] = scale
        r.q_rot[:, head * width : (head + 1) * width] = rope(
            hat * r.query_gain[...], cosine, sine
        ).astype(BF16)
    run_together(flows)

    q_pos = r.q_pos[...]
    per = 4 * rows

    def chunk_starts(i):
        starts = []
        for c in range(4):
            row = r.pos_all[i // 4, lax.rem(i, 4), c]
            for b in range(2):
                piece = row[:, b * 128 : (b + 1) * 128]
                starts.append(jnp.concatenate([piece] * groups, axis=1))
        return starts

    def chunk_of(i, begin):
        return r.kv_all[i // 4, lax.rem(i, 4), :, :, begin : begin + width].reshape(per, width)

    for head in range(heads_kv):
        head_queries = stacked(r.q_rot, head, groups, width)

        def score_step(i, top, head=head, head_queries=head_queries):
            scores = masked_scores(
                chunk_of(i, head * width), head_queries, chunk_starts(i), q_pos, inv_root
            )
            r.scores[pl.ds(pl.multiple_of(i * per, per), per), :] = scores
            return jnp.maximum(top, jnp.max(scores, axis=0, keepdims=True))

        top = lax.fori_loop(0, 8, score_step, jnp.full((1, groups * rows), MASKED, F32))

        def weight_step(i, carry, head=head, top=top):
            total, mixed = carry
            values = chunk_of(i, kv_width + head * width)
            weights = jnp.exp(r.scores[pl.ds(pl.multiple_of(i * per, per), per), :] - top)
            total = total + jnp.sum(weights, axis=0, keepdims=True)
            return total, mixed + first_dims_dot(values, weights.astype(BF16))

        total, mixed = lax.fori_loop(
            0, 8, weight_step,
            (jnp.zeros((1, groups * rows), F32), jnp.zeros((width, groups * rows), F32)),
        )
        mixed = mixed / total
        r.lse[head] = top + jnp.log(total)
        for g in range(groups):
            first = (head * groups + g) * width
            r.att[:, first : first + width] = mixed[:, g * rows : (g + 1) * rows].T

    def sum_flows(which, pieces=2):
        half = rows // 2
        count = half // pieces
        return [
            tp_sum_flow(
                copies, r.sum_in.at[which], r.sum_out.at[which], r.sum_landed.at[which],
                r.sum_chip.at[which], r.sum_far.at[which], partner_core, partner_far, core,
                piece * count, count, rows,
            )
            for piece in range(pieces)
        ]

    attb = r.att[...].astype(BF16)
    loads["w_o"].wait()
    r.sum_in[0] = dot(attb, r.w_o[...]).astype(BF16)
    flows = step_forward(sum_flows(0))
    for name in ("w_gate", "w_up", "w_down"):
        loads[name].wait()
    r.gob[...] = r.cotangent[...].astype(BF16)
    r.dhid[...] = transposed_dot(r.gob[...], r.w_down[...])
    run_together(flows)
    xmid = r.x[...] + r.sum_out[0].astype(F32)
    r.xmid[...] = xmid

    r2 = rms_scale(xmid)
    xhat2 = xmid * r2
    r.r2[...] = r2
    normed2 = (xhat2 * r.ffn_gain[...]).astype(BF16)
    r.normed2[...] = normed2
    gate = dot(normed2, r.w_gate[...])
    up = dot(normed2, r.w_up[...])
    sig = jax.nn.sigmoid(gate)
    silu = gate * sig
    hid = (silu * up).astype(BF16)
    d_hid = r.dhid[...]
    d_gate = (d_hid * up * sig * (1.0 + gate * (1.0 - sig))).astype(BF16)
    d_up = (d_hid * silu).astype(BF16)
    r.hid[...] = hid
    r.d_gate[...] = d_gate
    r.d_up[...] = d_up
    dn2_part = transposed_dot(d_gate, r.w_gate[...]) + transposed_dot(d_up, r.w_up[...])
    r.ffn_small[...] = jnp.sum(dn2_part * xhat2, axis=0, keepdims=True)
    r.sum_in[1] = dn2_part.astype(BF16)
    sums = step_forward(sum_flows(1))
    r.sum_in[2] = dot(r.hid[...], r.w_down[...]).astype(BF16)
    hidden_sums = sum_flows(2)

    groups_of_flows = {}

    def start(name):
        flows = []
        source, result = getattr(r, "g_" + name), getattr(r, "grad_" + name)
        for (order, first, count), buffers in zip(WEIGHT_PARTS[name], r.weight_buffers[name]):
            columns = pl.ds(first, count)
            flows.append(
                scatter_flow(
                    copies, coords, tp, source.at[:, :, :, :, columns], result.at[:, columns],
                    buffers, order, 0,
                )
            )
        groups_of_flows[name] = step_forward(flows)

    def tick(*names):
        for name in names:
            groups_of_flows[name] = step_forward(groups_of_flows[name])

    sums = step_forward(sums)
    tokens_product(r.normed2, r.d_gate[...], r.g_gate)
    start("gate")
    sums = step_forward(sums)
    hidden_sums = step_forward(hidden_sums)
    tokens_product(r.normed2, r.d_up[...], r.g_up)
    start("up")
    run_together(sums)

    dn2 = r.sum_out[1].astype(F32)
    xhat2 = r.xmid[...] * r.r2[...]
    dmid = r.cotangent[...] + norm_backward(dn2 * r.ffn_gain[...], xhat2, r.r2[...])
    r.dmid[...] = dmid
    dmidb = dmid.astype(BF16)
    r.dmidb[...] = dmidb
    d_att = transposed_dot(dmidb, r.w_o[...])
    r.d_attb[...] = d_att.astype(BF16)
    for head in range(heads_kv):
        pieces = []
        for g in range(groups):
            first = (head * groups + g) * width
            product = d_att[:, first : first + width] * r.att[:, first : first + width]
            pieces.append(jnp.sum(product.T, axis=0, keepdims=True))
        r.delta[head] = jnp.concatenate(pieces, axis=1)
    tick("gate")
    tokens_product(r.gob, r.hid[...], r.g_down)
    start("down")
    tick("up")
    tokens_product(r.dmidb, r.att[...].astype(BF16), r.g_out)
    start("out")
    hidden_sums = step_forward(hidden_sums)

    r.dq_acc[...] = jnp.zeros_like(r.dq_acc)

    def backward_step(i, carry):
        starts = chunk_starts(i)
        for head in range(heads_kv):
            head_queries = stacked(r.q_rot, head, groups, width)
            grads = stacked(r.d_attb, head, groups, width)
            base = kv_width + head * width
            keys = chunk_of(i, head * width)
            values = chunk_of(i, base)
            scores = masked_scores(keys, head_queries, starts, q_pos, inv_root)
            probs = jnp.exp(scores - r.lse[head])
            d_prob = transposed_dot(values, grads)
            d_scores = (probs * (d_prob - r.delta[head])).astype(BF16)
            d_keys = dot(d_scores, head_queries) * inv_root
            d_values = dot(probs.astype(BF16), grads)
            where = (i // 4, lax.rem(i, 4), slice(None), slice(None))
            shape = (4, rows, width)
            r.dkv[where + (slice(head * width, (head + 1) * width),)] = d_keys.astype(BF16).reshape(shape)
            r.dkv[where + (slice(base, base + width),)] = d_values.astype(BF16).reshape(shape)
            r.dq_acc[head] += first_dims_dot(keys, d_scores)
        return carry

    lax.fori_loop(0, 2, backward_step, 0)
    run_together(hidden_sums)
    tick("gate", "down", "out")
    lax.fori_loop(2, 4, backward_step, 0)
    tick("up", "gate")
    lax.fori_loop(4, 6, backward_step, 0)
    tick("down", "out", "up", "gate")
    lax.fori_loop(6, 8, backward_step, 0)
    late = []
    for (order, first, count), buffers in zip(ROW_PARTS, r.kv_buffers):
        part_rows = pl.ds(first, count)
        late.append(
            scatter_flow(
                copies, coords, tp, r.dkv.at[:, :, :, part_rows, :],
                r.dkv_own.at[part_rows, :], buffers, order, 1,
            )
        )
    groups_of_flows["kv"] = step_forward(late)
    tick("gate", "up", "down", "out")
    r.hidden_out[...] = r.xmid[...] + r.sum_out[2].astype(F32)

    small_q = jnp.zeros((1, width), F32)
    for head in range(heads_kv):
        for g in range(groups):
            index = head * groups + g
            here = slice(index * width, (index + 1) * width)
            grad = rope_back(r.dq_acc[head, :, g * rows : (g + 1) * rows].T * inv_root, cosine, sine)
            hat = r.qhat[:, here]
            small_q = small_q + jnp.sum(grad * hat, axis=0, keepdims=True)
            r.dqb[:, here] = norm_backward(grad * r.query_gain[...], hat, r.rq[index]).astype(BF16)
    tokens_product(r.normed1, r.dqb[...], r.g_query)
    r.dn1[...] = transposed_dot(r.dqb[...], r.w_q[...])
    tick("kv")
    start("query")
    tick("up", "down", "out", "kv", "query")
    tick("down", "out", "kv", "query")
    tick("kv", "query")
    tick("kv")

    small_k = jnp.zeros((1, width), F32)
    for head in range(heads_kv):
        here = slice(head * width, (head + 1) * width)
        grad = rope_back(r.dkv_own[:, here], cosine, sine)
        hat = r.khat[:, here]
        small_k = small_k + jnp.sum(grad * hat, axis=0, keepdims=True)
        r.dkb[:, here] = norm_backward(grad * r.key_gain[...], hat, r.rk[head]).astype(BF16)
    r.dvb[...] = r.dkv_own[:, kv_width:].astype(BF16)
    dn1_part = (
        r.dn1[...] + transposed_dot(r.dkb[...], r.w_k[...]) + transposed_dot(r.dvb[...], r.w_v[...])
    )
    xhat1 = r.x[...] * r.r1[...]
    r.sum_in[3] = dn1_part.astype(BF16)
    sums = step_forward(sum_flows(3))
    r.small_in[0:1, 0:1024] = jnp.sum(dn1_part * xhat1, axis=0, keepdims=True)
    r.small_in[0:1, 1024:2048] = r.ffn_small[...]
    r.small_in[0:1, 2048:2176] = small_q
    r.small_in[0:1, 2176:2304] = small_k
    tokens_product(r.normed1, r.dkb[...], r.g_key)
    tokens_product(r.normed1, r.dvb[...], r.g_value)
    start("key")
    start("value")
    groups_of_flows["small"] = step_forward(
        [sum_everywhere_flow(copies, coords, tp, r.small_in, r.small_out, r.small_slots)]
    )
    sums = step_forward(sums)
    tick("query", "key", "value", "small")
    run_together(sums)
    flows = []
    dn1 = r.sum_out[3].astype(F32)
    r.input_gradient[...] = r.dmid[...] + norm_backward(
        dn1 * r.attention_gain[...], r.x[...] * r.r1[...], r.r1[...]
    )
    for name in ("query", "key", "value", "small"):
        flows = flows + groups_of_flows.pop(name)
    assert not any(groups_of_flows.values())
    run_together(flows)
    copies.drain()


WEIGHT_NAMES = ("w_k", "w_v", "w_q", "w_o", "w_gate", "w_up", "w_down")


def whole_layer(
    layer_input, cotangent, weights, gains, cosine, sine, starts, q_pos, heads_kv, groups
):
    rows, features = layer_input.shape
    width = cosine.shape[1]
    heads_q = heads_kv * groups
    q_width, kv_width = heads_q * width, heads_kv * width
    hidden = weights["w_gate"].shape[1]
    vmem = pl.BlockSpec(memory_space=pltpu.VMEM)
    hbm = pl.BlockSpec(memory_space=pl.ANY)
    inputs = {
        "x": layer_input, "cotangent": cotangent, "cosine": cosine, "sine": sine,
        "starts": starts, "q_pos": q_pos, **gains,
    }
    columns = {
        "gate": hidden, "up": hidden, "down": hidden, "out": q_width,
        "query": q_width, "key": kv_width, "value": kv_width,
    }
    outputs = {
        "hidden_out": ((rows, features), F32),
        "input_gradient": ((rows, features), F32),
        "small_out": ((1, 2304), F32),
    }
    for name, count in columns.items():
        outputs["grad_" + name] = ((32, count), F32)
    scratch = {
        "send_sem": pltpu.SemaphoreType.DMA((320,)),
        "recv_sem": pltpu.SemaphoreType.DMA((320,)),
        "load_sem": pltpu.SemaphoreType.DMA((len(WEIGHT_NAMES),)),
    }
    for name in WEIGHT_NAMES:
        scratch[name] = pltpu.VMEM(weights[name].shape, BF16)
    for name, shape, kind in (
        ("normed1", (rows, features), BF16),
        ("normed2", (rows, features), BF16),
        ("gob", (rows, features), BF16),
        ("dmidb", (rows, features), BF16),
        ("r1", (rows, 1), F32),
        ("r2", (rows, 1), F32),
        ("rq", (heads_q, rows, 1), F32),
        ("rk", (heads_kv, rows, 1), F32),
        ("qhat", (rows, q_width), F32),
        ("khat", (rows, kv_width), F32),
        ("q_rot", (rows, q_width), BF16),
        ("kv_all", (2, 4, 4, rows, 2 * kv_width), BF16),
        ("pos_all", (2, 4, 4, 1, 256), jnp.int32),
        ("scores", (32 * rows, groups * rows), F32),
        ("lse", (heads_kv, 1, groups * rows), F32),
        ("delta", (heads_kv, 1, groups * rows), F32),
        ("att", (rows, q_width), F32),
        ("sum_in", (4, rows, features), BF16),
        ("sum_out", (4, rows, features), BF16),
        ("sum_landed", (4, rows // 2, features), BF16),
        ("sum_chip", (4, rows // 2, features), BF16),
        ("sum_far", (4, rows // 2, features), BF16),
        ("xmid", (rows, features), F32),
        ("dmid", (rows, features), F32),
        ("dn1", (rows, features), F32),
        ("dhid", (rows, hidden), F32),
        ("hid", (rows, hidden), BF16),
        ("d_gate", (rows, hidden), BF16),
        ("d_up", (rows, hidden), BF16),
        ("ffn_small", (1, features), F32),
        ("d_attb", (rows, q_width), BF16),
        ("dq_acc", (heads_kv, width, groups * rows), F32),
        ("dkv", (2, 4, 4, rows, 2 * kv_width), BF16),
        ("dkv_own", (rows, 2 * kv_width), F32),
        ("dqb", (rows, q_width), BF16),
        ("dkb", (rows, kv_width), BF16),
        ("dvb", (rows, kv_width), BF16),
        ("small_in", (1, 2304), F32),
    ):
        scratch[name] = pltpu.VMEM(shape, kind)
    for name, count in columns.items():
        scratch["g_" + name] = pltpu.VMEM((2, 4, 4, 32, count), BF16)
    lists = {"small_slots": sum_everywhere_scratch((1, 2304))}
    for name, count in columns.items():
        for i, (order, first, size) in enumerate(WEIGHT_PARTS[name]):
            lists["%s_%d" % (name, i)] = scatter_scratch((32, size), order, 0)
    for i, (order, first, count) in enumerate(ROW_PARTS):
        lists["kv_%d" % i] = scatter_scratch((count, 2 * kv_width), order, 1)

    input_names = list(inputs) + [name + "_hbm" for name in WEIGHT_NAMES]
    flat_scratch = list(scratch.values())
    for buffers in lists.values():
        flat_scratch.extend(buffers)

    def kernel(*refs):
        r = types.SimpleNamespace()
        names = input_names + list(outputs) + list(scratch)
        for name, ref in zip(names, refs):
            setattr(r, name, ref)
        rest = list(refs[len(names) :])
        groups_of = {}
        for name, buffers in lists.items():
            groups_of[name], rest = rest[: len(buffers)], rest[len(buffers) :]
        r.small_slots = groups_of["small_slots"]
        r.weight_buffers = {
            name: [groups_of["%s_%d" % (name, i)] for i in range(len(WEIGHT_PARTS[name]))]
            for name in columns
        }
        r.kv_buffers = [groups_of["kv_%d" % i] for i in range(len(ROW_PARTS))]
        layer_kernel(r, (heads_kv, groups, width))

    results = pl.pallas_call(
        kernel,
        out_shape=tuple(jax.ShapeDtypeStruct(shape, kind) for shape, kind in outputs.values()),
        in_specs=[vmem] * len(inputs) + [hbm] * len(WEIGHT_NAMES),
        out_specs=(vmem,) * len(outputs),
        scratch_shapes=flat_scratch,
        compiler_params=pltpu.CompilerParams(
            collective_id=0, has_side_effects=True, vmem_limit_bytes=67043328
        ),
        name="whole_layer",
    )(*inputs.values(), *[weights[name] for name in WEIGHT_NAMES])
    return dict(zip(outputs, results))


def body(
    layer_input,
    positions,
    attention_norm_gain,
    w_query,
    key_projection,
    value_projection,
    query_norm,
    key_norm_gain,
    output_projection,
    feedforward_norm_gain,
    w_gate,
    w_up,
    w_down,
    output_cotangent,
):
    head_dim = query_norm.shape[0]
    heads_q = w_query.shape[1] // head_dim
    heads_kv = key_projection.shape[1] // head_dim
    groups = heads_q // heads_kv
    cosine, sine = rope_tables(positions, head_dim)
    out = whole_layer(
        layer_input,
        output_cotangent,
        {
            "w_q": w_query, "w_k": key_projection, "w_v": value_projection, "w_o": output_projection,
            "w_gate": w_gate, "w_up": w_up, "w_down": w_down,
        },
        {
            "attention_gain": attention_norm_gain.reshape(1, -1),
            "ffn_gain": feedforward_norm_gain.reshape(1, -1),
            "query_gain": query_norm.reshape(1, -1),
            "key_gain": key_norm_gain.reshape(1, -1),
        },
        jnp.concatenate([cosine, cosine], axis=1),
        jnp.concatenate([-sine, sine], axis=1),
        jnp.repeat(positions.reshape(-1, 64)[:, 0], 128).reshape(1, 256),
        jnp.tile(positions, groups).reshape(1, -1),
        heads_kv,
        groups,
    )
    names = (
        "hidden_out", "input_gradient", "grad_query", "grad_key", "grad_value", "grad_out",
        "grad_gate", "grad_up", "grad_down", "small_out",
    )
    written = write_results([out[name] for name in names], (1024, 1024, 128, 128))
    done = dict(zip(names[:-1], written))
    small = [piece.reshape(-1) for piece in written[len(names) - 1 :]]
    return (
        done["hidden_out"],
        done["input_gradient"],
        small[0],
        done["grad_query"],
        done["grad_key"],
        done["grad_value"],
        small[2],
        small[3],
        done["grad_out"].T,
        small[1],
        done["grad_gate"],
        done["grad_up"],
        done["grad_down"].T,
    )


def solution(mesh):
    return jax.shard_map(
        body,
        mesh=mesh,
        in_specs=(
            P("ctx", None),
            P("ctx"),
            P(),
            P(None, "tp"),
            P(None, "tp"),
            P(None, "tp"),
            P(),
            P(),
            P("tp", None),
            P(),
            P(None, "tp"),
            P(None, "tp"),
            P("tp", None),
            P("ctx", None),
        ),
        out_specs=(
            P("ctx", None),
            P("ctx", None),
            P(),
            P("ctx", "tp"),
            P("ctx", "tp"),
            P("ctx", "tp"),
            P(),
            P(),
            P("tp", "ctx"),
            P(),
            P("ctx", "tp"),
            P("ctx", "tp"),
            P("tp", "ctx"),
        ),
        check_vma=False,
    )
```

```python
import math
import types

import jax
import jax.numpy as jnp
from jax import lax
from jax.experimental import pallas as pl
from jax.experimental.pallas import tpu as pltpu
from jax.sharding import PartitionSpec as P

EPSILON = 1e-06
ROPE_BASE = 1000000.0
MASKED = -1e30


MESH = pl.DeviceIdType.MESH
SIZES = {"y": 2, "z": 4, "x": 4}
DIMS = ("y", "z", "x")


def place():
    me = lax.axis_index("ctx")
    return {"y": me // 16, "z": lax.rem(me // 4, 4), "x": lax.rem(me, 4)}, lax.axis_index("tp")


def shifted(coords, dim, step):
    moved = dict(coords)
    moved[dim] = lax.rem(coords[dim] + step + SIZES[dim], SIZES[dim])
    return moved


def device_at(coords, tp):
    return (coords["y"] * 16 + coords["z"] * 4 + coords["x"], tp)


class Copies:
    def __init__(self, send_sem, recv_sem):
        self.send_sem, self.recv_sem = send_sem, recv_sem
        self.count = 0
        self.sends = 0
        self.free = []
        self.started = {}

    def slot(self):
        self.count += 1
        return self.count - 1

    def send(self, source, target, device, slot=None):
        if self.free:
            place = self.free.pop(0)
        else:
            place = self.sends
            self.sends += 1
        copy = pltpu.make_async_remote_copy(
            src_ref=source,
            dst_ref=target,
            send_sem=self.send_sem.at[place],
            recv_sem=self.recv_sem.at[self.slot() if slot is None else slot],
            device_id=device,
            device_id_type=MESH,
        )
        copy.start()
        self.started[id(copy)] = (copy, place)
        return copy

    def landed(self, ref, slot, device):
        pltpu.make_async_remote_copy(
            src_ref=ref,
            dst_ref=ref,
            send_sem=self.send_sem.at[0],
            recv_sem=self.recv_sem.at[slot],
            device_id=device,
            device_id_type=MESH,
        ).wait_recv()

    def sent(self, *copies):
        for copy in copies:
            unused, place = self.started.pop(id(copy))
            copy.wait_send()
            self.free.append(place)

    def drain(self):
        for copy, unused in self.started.values():
            copy.wait_send()


def run_together(flows):
    live = list(flows)
    while live:
        left = []
        for flow in live:
            try:
                next(flow)
                left.append(flow)
            except StopIteration:
                pass
        live = left


def gather_small_flow(copies, coords, tp, ref, order, piece, halves):
    def region(held, where, part):
        index = tuple(slice(None) if dim in held else where[dim] for dim in DIMS)
        return ref.at[index + part]

    held = []
    for dim in order:
        right = device_at(shifted(coords, dim, 1), tp)
        mine = region(held, coords, piece)
        if SIZES[dim] == 2:
            copy = copies.send(mine, mine, right)
            yield
            copy.wait_recv()
        else:
            left = device_at(shifted(coords, dim, -1), tp)
            go_right = copies.send(mine, mine, right)
            go_left = copies.send(mine, mine, left)
            yield
            go_right.wait_recv()
            block = region(held, shifted(coords, dim, -1), halves[0])
            pass_right = copies.send(block, block, right)
            pass_left = None
            if halves[1] is not None:
                go_left.wait_recv()
                block = region(held, shifted(coords, dim, 1), halves[1])
                pass_left = copies.send(block, block, left)
            yield
            pass_right.wait_recv()
            if pass_left is None:
                go_left.wait_recv()
            else:
                pass_left.wait_recv()
        held.append(dim)


def gather_flow(copies, coords, tp, ref, order, piece, halves):
    first, second, last = order

    def to(dim, step):
        return device_at(shifted(coords, dim, step), tp)

    def spot(dim, step):
        return shifted(coords, dim, step)[dim]

    def region(where, part):
        return ref.at[tuple(where[dim] for dim in DIMS) + part]

    pending, passed = [], []

    def send_last(where):
        block = region({**where, last: coords[last]}, piece)
        right = copies.send(block, block, to(last, 1))
        left = copies.send(block, block, to(last, -1)) if SIZES[last] == 4 else None
        pending.append((where, right, left))

    def pass_on(count):
        for unused in range(count):
            where, right, left = pending.pop(0)
            right.wait_recv()
            copies.sent(right)
            if left is None:
                continue
            block = region({**where, last: spot(last, -1)}, halves[0])
            passed.append(copies.send(block, block, to(last, 1)))
            left.wait_recv()
            copies.sent(left)
            block = region({**where, last: spot(last, 1)}, halves[1])
            passed.append(copies.send(block, block, to(last, -1)))

    def spread(dim, where, after):
        block = region({**where, dim: coords[dim], last: coords[last]}, piece)
        right = copies.send(block, block, to(dim, 1))
        left = copies.send(block, block, to(dim, -1)) if SIZES[dim] == 4 else None
        after()
        yield
        older = len(pending)
        right.wait_recv()
        if left is None:
            send_last({**where, dim: spot(dim, 1)})
            pass_on(older)
            return
        here = {**where, last: coords[last]}
        block = region({**here, dim: spot(dim, -1)}, halves[0])
        far_right = copies.send(block, block, to(dim, 1))
        send_last({**where, dim: spot(dim, -1)})
        left.wait_recv()
        block = region({**here, dim: spot(dim, 1)}, halves[1])
        far_left = copies.send(block, block, to(dim, -1))
        send_last({**where, dim: spot(dim, 1)})
        pass_on(older)
        yield
        older = len(pending)
        far_right.wait_recv()
        far_left.wait_recv()
        send_last({**where, dim: spot(dim, 2)})
        pass_on(older)

    yield from spread(
        first,
        {second: coords[second]},
        lambda: send_last({first: coords[first], second: coords[second]}),
    )
    yield from spread(second, {first: slice(None)}, lambda: None)
    yield
    pass_on(len(pending))
    yield
    for copy in passed:
        copy.wait_recv()
    copies.sent(*passed)


def leading_index(flat, dims):
    index = []
    for dim in reversed(dims):
        index.insert(0, lax.rem(flat, SIZES[dim]))
        flat = flat // SIZES[dim]
    return tuple(index)


def leading_shape(dims):
    return tuple(SIZES[dim] for dim in dims)


def over_leading(dims, step):
    count = math.prod(leading_shape(dims))
    if count == 1:
        step(())
        return

    def body(flat, carry):
        step(leading_index(flat, dims))
        return carry

    lax.fori_loop(0, count, body, 0)


def scatter_scratch(shape, order, axis):
    half = tuple(size // 2 if i == axis else size for i, size in enumerate(shape))
    buffers = []
    rest = list(DIMS)
    for dim in order:
        rest.remove(dim)
        lead = leading_shape(rest)
        if SIZES[dim] == 2:
            buffers.append(pltpu.VMEM(lead + shape, jnp.bfloat16))
        elif dim != order[0]:
            buffers.append(pltpu.VMEM((3,) + lead + shape, jnp.bfloat16))
        else:
            buffers.extend([pltpu.VMEM(lead + half, jnp.bfloat16)] * 4)
            buffers.append(pltpu.VMEM((4,) + lead + half, jnp.bfloat16))
        if rest:
            buffers.append(pltpu.VMEM(lead + shape, jnp.bfloat16))
    return buffers


def scatter_flow(copies, coords, tp, source, result, buffers, order, axis):
    buffers = list(buffers)
    shape = source.shape[-2:]
    size = shape[axis] // 2
    halves = [
        tuple(pl.ds(h * size, size) if i == axis else slice(None) for i in range(2))
        for h in range(2)
    ]
    whole = (slice(None), slice(None))
    current = source
    dims = list(DIMS)

    for dim in order:
        rest = [d for d in dims if d != dim]
        spot = dims.index(dim)

        def at(where, lead, part, spot=spot, current=current):
            index = tuple(lead[:spot]) + (where[dim],) + tuple(lead[spot:])
            return current.at[index + part]

        everywhere = (slice(None),) * len(rest)
        right_coords = shifted(coords, dim, 1)
        right = device_at(right_coords, tp)
        f32 = jnp.float32
        if SIZES[dim] == 2:
            landed = buffers.pop(0)
            copy = copies.send(at(right_coords, everywhere, whole), landed, right)
            target = buffers.pop(0) if rest else result
            yield
            copy.wait_recv()
            copies.sent(copy)

            def add(lead):
                total = at(coords, lead, whole)[...].astype(f32) + landed[lead + whole].astype(f32)
                target[lead + whole] = total.astype(target.dtype)

            over_leading(rest, add)
        elif dim != order[0]:
            landed = buffers.pop(0)
            target = buffers.pop(0) if rest else result
            sent = []
            slot = copies.slot()
            for step in (1, 2, 3):
                there = shifted(coords, dim, step)
                block = at(there, everywhere, whole)
                sent.append(copies.send(block, landed.at[step - 1], device_at(there, tp), slot))
            yield
            copies.landed(landed, slot, right)
            copies.sent(*sent)

            def add(lead):
                total = at(coords, lead, whole)[...].astype(f32)
                for i in range(3):
                    total = total + landed[(i,) + lead + whole].astype(f32)
                target[lead + whole] = total.astype(target.dtype)

            over_leading(rest, add)
        else:
            left_coords = shifted(coords, dim, -1)
            far_coords = shifted(coords, dim, 2)
            left = device_at(left_coords, tp)
            pass_l, pass_r, out_r, out_l, arrived = buffers[:5]
            buffers = buffers[5:]
            near_l, near_r, sum_l, sum_r = [arrived.at[i] for i in range(4)]
            slot = copies.slot()
            target = buffers.pop(0) if rest else result
            relay_r = copies.send(at(far_coords, everywhere, halves[0]), pass_l, right)
            relay_l = copies.send(at(far_coords, everywhere, halves[1]), pass_r, left)
            direct_r = copies.send(at(right_coords, everywhere, halves[1]), near_l, right, slot)
            direct_l = copies.send(at(left_coords, everywhere, halves[0]), near_r, left, slot)
            yield
            relay_r.wait_recv()

            def merge_right(lead):
                total = at(right_coords, lead, halves[0])[...].astype(f32) + pass_l[
                    lead + whole
                ].astype(f32)
                out_r[lead + whole] = total.astype(out_r.dtype)

            over_leading(rest, merge_right)
            merged_r = copies.send(out_r, sum_l, right, slot)
            relay_l.wait_recv()

            def merge_left(lead):
                total = at(left_coords, lead, halves[1])[...].astype(f32) + pass_r[
                    lead + whole
                ].astype(f32)
                out_l[lead + whole] = total.astype(out_l.dtype)

            over_leading(rest, merge_left)
            merged_l = copies.send(out_l, sum_r, left, slot)
            yield
            copies.landed(arrived, slot, right)
            copies.sent(relay_r, relay_l, direct_r, direct_l, merged_r, merged_l)

            def add(lead):
                for half, one, two in ((halves[0], sum_l, near_r), (halves[1], near_l, sum_r)):
                    total = (
                        at(coords, lead, half)[...].astype(f32)
                        + one[lead + whole].astype(f32)
                        + two[lead + whole].astype(f32)
                    )
                    target[lead + half] = total.astype(target.dtype)

            over_leading(rest, add)
        current = target
        dims = rest


def column_peers(coords, tp):
    place_in_column = coords["y"] * 4 + tp
    peers = []
    for step in range(1, 8):
        other = lax.rem(place_in_column + step, 8)
        peers.append(device_at({**coords, "y": other // 4}, lax.rem(other, 4)))
    return place_in_column, peers


def sum_everywhere_flow(copies, coords, tp, source, result, slots):
    current = source
    column, peers = column_peers(coords, tp)
    stages = [
        (coords[dim], [device_at(shifted(coords, dim, step), tp) for step in (1, 2, 3)])
        for dim in ("x", "z")
    ] + [(column, peers)]
    for stage, (spot, others) in enumerate(stages):
        ring = slots[stage]
        ring[spot] = current[...]
        slot = copies.slot()
        sent = [copies.send(current, ring.at[spot], other, slot) for other in others]
        yield
        copies.landed(ring.at[pl.ds(0, len(others))], slot, others[0])
        copies.sent(*sent)
        total = ring[0]
        for i in range(1, len(others) + 1):
            total = total + ring[i]
        target = slots[3 + stage] if stage < 2 else result
        target[...] = total
        current = target


def sum_everywhere_scratch(shape):
    rings = [pltpu.VMEM((count,) + shape, jnp.float32) for count in (4, 4, 8)]
    return rings + [pltpu.VMEM(shape, jnp.float32)] * 2


def tp_sum_flow(copies, ins, out, landed, chip, far, partner_core, partner_far, core, first, count, rows):
    half = rows // 2
    mine = pl.ds(pl.multiple_of(core * half + first, 16), count)
    theirs = pl.ds(pl.multiple_of((1 - core) * half + first, 16), count)
    local = pl.ds(first, count)
    f32 = jnp.float32
    copy = copies.send(ins.at[theirs], landed.at[local], partner_core)
    yield
    copy.wait_recv()
    copies.sent(copy)
    chip[local] = (ins[mine].astype(f32) + landed[local].astype(f32)).astype(chip.dtype)
    copy = copies.send(chip.at[local], far.at[local], partner_far)
    yield
    copy.wait_recv()
    copies.sent(copy)
    out[mine] = (chip[local].astype(f32) + far[local].astype(f32)).astype(out.dtype)
    copy = copies.send(out.at[mine], out.at[mine], partner_core)
    yield
    copy.wait_recv()
    copies.sent(copy)


def write_results(arrays, splits):
    number = len(arrays)
    pieces = [(array.shape[0], size) for array, size in zip(arrays[-1:] * len(splits), splits)]
    shapes = [array.shape for array in arrays[:-1]] + pieces

    def kernel(*refs):
        ins, outs = refs[:number], refs[number : number + len(shapes)]
        held, (in_sem, out_sem) = refs[number + len(shapes) : -2], refs[-2:]
        loads = [
            pltpu.make_async_copy(source, target, in_sem.at[i])
            for i, (source, target) in enumerate(zip(ins, held))
        ]
        for load in loads:
            load.start()
        stores = []
        for i, load in enumerate(loads[:-1]):
            load.wait()
            stores.append(pltpu.make_async_copy(held[i], outs[i], out_sem.at[i]))
            stores[-1].start()
        loads[-1].wait()
        begin = 0
        for i, size in enumerate(splits):
            slot = number - 1 + i
            source = held[-1].at[:, pl.ds(begin, size)]
            stores.append(pltpu.make_async_copy(source, outs[slot], out_sem.at[slot]))
            stores[-1].start()
            begin += size
        for store in stores:
            store.wait()

    hbm = pl.BlockSpec(memory_space=pl.ANY)
    return pl.pallas_call(
        kernel,
        out_shape=tuple(jax.ShapeDtypeStruct(shape, jnp.float32) for shape in shapes),
        in_specs=[hbm] * number,
        out_specs=(hbm,) * len(shapes),
        scratch_shapes=[pltpu.VMEM(array.shape, jnp.float32) for array in arrays]
        + [pltpu.SemaphoreType.DMA((number,)), pltpu.SemaphoreType.DMA((len(shapes),))],
        compiler_params=pltpu.CompilerParams(vmem_limit_bytes=60 << 20),
        name="write_results",
    )(*arrays)


def rms_scale(values):
    return lax.rsqrt(jnp.mean(values * values, axis=-1, keepdims=True) + EPSILON)


def norm_backward(grad, normed, scale_rows):
    return scale_rows * (grad - normed * jnp.mean(grad * normed, axis=-1, keepdims=True))


def rope_tables(positions, head_dim):
    half_dim = head_dim // 2
    lane = jnp.arange(head_dim, dtype=jnp.int32)
    pair = jnp.where(lane < half_dim, lane, lane - half_dim).astype(jnp.float32)
    freqs = jnp.exp(-(2.0 * pair / head_dim) * math.log(ROPE_BASE))
    angles = positions.astype(jnp.float32)[:, None] * freqs[None, :]
    sign = jnp.where(lane < half_dim, -1.0, 1.0).astype(jnp.float32)
    return (jnp.cos(angles), jnp.sin(angles) * sign[None, :])


XZY, ZYX, YXZ = ("x", "z", "y"), ("z", "y", "x"), ("y", "x", "z")
ROW_PARTS = ((XZY, 0, 48), (ZYX, 48, 48), (YXZ, 96, 32))
THREE_PARTS = ((XZY, 0, 256), (ZYX, 256, 256), (YXZ, 512, 256))
TWO_PARTS = ((XZY, 0, 256), (ZYX, 256, 256))
WEIGHT_PARTS = {
    "gate": THREE_PARTS,
    "up": THREE_PARTS,
    "down": THREE_PARTS,
    "out": TWO_PARTS,
    "query": TWO_PARTS,
    "key": ((YXZ, 0, 256),),
    "value": ((XZY, 0, 128), (ZYX, 128, 128)),
}
F32, BF16 = jnp.float32, jnp.bfloat16


def rope(values, cosine, sine):
    return values * cosine + pltpu.roll(values, 64, 1) * sine


def rope_back(grad, cosine, sine):
    return grad * cosine - pltpu.roll(grad, 64, 1) * sine


def dot(left, right):
    return jnp.dot(left, right, preferred_element_type=F32)


def stacked(ref, head, groups, width):
    return jnp.concatenate(
        [ref[:, (head * groups + g) * width : (head * groups + g + 1) * width] for g in range(groups)],
        axis=0,
    )


def transposed_dot(left, right):
    return lax.dot_general(left, right, (((1,), (1,)), ((), ())), preferred_element_type=F32)


def first_dims_dot(left, right):
    return lax.dot_general(left, right, (((0,), (0,)), ((), ())), preferred_element_type=F32)


def masked_scores(keys, queries, starts, q_pos, inv_root):
    scores = transposed_dot(keys, queries) * inv_root
    step = lax.broadcasted_iota(jnp.int32, (64, queries.shape[0]), 0)
    pieces = []
    for b, start in enumerate(starts):
        ahead = q_pos - start
        pieces.append(jnp.where(ahead >= step, scores[b * 64 : (b + 1) * 64], MASKED))
    return jnp.concatenate(pieces, axis=0)


def step_forward(flows):
    return [flow for flow in flows if next(flow, "done") != "done"]


def tokens_product(left_ref, right, target):
    def step(i, carry):
        block = left_ref[:, pl.ds(pl.multiple_of(i * 128, 128), 128)]
        part = first_dims_dot(block, right).astype(BF16)
        target[i // 4, lax.rem(i, 4)] = part.reshape(4, 32, right.shape[1])
        return carry

    lax.fori_loop(0, left_ref.shape[1] // 128, step, 0)


def layer_kernel(r, sizes):
    heads_kv, groups, width = sizes
    heads_q = heads_kv * groups
    rows = r.x.shape[0]
    inv_root = 1.0 / math.sqrt(width)
    kv_width = heads_kv * width
    coords, tp = place()
    ctx = lax.axis_index("ctx")
    core = lax.rem(tp, 2)
    partner_core = (ctx, tp + 1 - 2 * core)
    partner_far = (ctx, lax.rem(tp + 2, 4))
    peers = [
        device_at(shifted(coords, dim, step), tp) for dim in ("z", "x") for step in (1, 2, 3)
    ] + column_peers(coords, tp)[1]
    own = (coords["y"], coords["z"], coords["x"])
    copies = Copies(r.send_sem, r.recv_sem)

    barrier = pltpu.get_barrier_semaphore()
    for peer in peers:
        pl.semaphore_signal(barrier, inc=1, device_id=peer, device_id_type=MESH)

    loads = {}
    for i, name in enumerate(r.input_names + WEIGHT_NAMES):
        loads[name] = pltpu.make_async_copy(
            getattr(r, name + "_hbm"), getattr(r, name), r.load_sem.at[i]
        )
    for name in r.input_names + WEIGHT_NAMES[:3]:
        loads[name].start()

    for name in r.input_names:
        loads[name].wait()
    cosine, sine = r.cosine[...], r.sine[...]
    x = r.x[...]
    r1 = rms_scale(x)
    xhat1 = x * r1
    normed1 = (xhat1 * r.attention_gain[...]).astype(BF16)
    r.normed1[...] = normed1
    r.r1[...] = r1
    loads["w_k"].wait()
    unnormed = dot(normed1, r.w_k[...])
    for head in range(heads_kv):
        part = unnormed[:, head * width : (head + 1) * width]
        scale = rms_scale(part)
        hat = part * scale
        r.khat[:, head * width : (head + 1) * width] = hat
        r.rk[head] = scale
        r.kv_all[own + (slice(None), slice(head * width, (head + 1) * width))] = rope(
            hat * r.key_gain[...], cosine, sine
        ).astype(BF16)
    loads["w_v"].wait()
    r.kv_all[own + (slice(None), slice(kv_width, 2 * kv_width))] = dot(normed1, r.w_v[...]).astype(BF16)
    positions = r.positions[...]
    r.pos_all[own] = jnp.concatenate(
        [jnp.broadcast_to(positions[:, first : first + 1], (1, 128)) for first in (0, 64)], axis=1
    )
    pl.semaphore_wait(barrier, len(peers))
    flows = []
    for order, first, count in ROW_PARTS:
        part_rows = pl.ds(first, count)
        flows.append(
            gather_flow(
                copies, coords, tp, r.kv_all, order,
                (part_rows, slice(None)),
                ((part_rows, pl.ds(0, kv_width)), (part_rows, pl.ds(kv_width, kv_width))),
            )
        )
    whole = (slice(None), slice(None))
    flows.append(gather_small_flow(copies, coords, tp, r.pos_all, ("y", "z", "x"), whole, (whole, None)))
    flows = step_forward(flows)
    for name in WEIGHT_NAMES[3:]:
        loads[name].start()
    loads["w_q"].wait()
    queries = dot(normed1, r.w_q[...])
    for head in range(heads_q):
        part = queries[:, head * width : (head + 1) * width]
        scale = rms_scale(part)
        hat = part * scale
        r.qhat[:, head * width : (head + 1) * width] = hat
        r.rq[head] = scale
        r.q_rot[:, head * width : (head + 1) * width] = rope(
            hat * r.query_gain[...], cosine, sine
        ).astype(BF16)
    run_together(flows)

    q_pos = jnp.concatenate([r.positions[...]] * groups, axis=1)
    per = 4 * rows

    def chunk_starts(i):
        starts = []
        for c in range(4):
            row = r.pos_all[i // 4, lax.rem(i, 4), c]
            for b in range(2):
                piece = row[:, b * 128 : (b + 1) * 128]
                starts.append(jnp.concatenate([piece] * groups, axis=1))
        return starts

    def chunk_of(i, begin):
        return r.kv_all[i // 4, lax.rem(i, 4), :, :, begin : begin + width].reshape(per, width)

    for head in range(heads_kv):
        head_queries = stacked(r.q_rot, head, groups, width)

        def score_step(i, top, head=head, head_queries=head_queries):
            scores = masked_scores(
                chunk_of(i, head * width), head_queries, chunk_starts(i), q_pos, inv_root
            )
            r.scores[pl.ds(pl.multiple_of(i * per, per), per), :] = scores
            return jnp.maximum(top, jnp.max(scores, axis=0, keepdims=True))

        top = lax.fori_loop(0, 8, score_step, jnp.full((1, groups * rows), MASKED, F32))

        def weight_step(i, carry, head=head, top=top):
            total, mixed = carry
            values = chunk_of(i, kv_width + head * width)
            weights = jnp.exp(r.scores[pl.ds(pl.multiple_of(i * per, per), per), :] - top)
            total = total + jnp.sum(weights, axis=0, keepdims=True)
            return total, mixed + first_dims_dot(values, weights.astype(BF16))

        total, mixed = lax.fori_loop(
            0, 8, weight_step,
            (jnp.zeros((1, groups * rows), F32), jnp.zeros((width, groups * rows), F32)),
        )
        mixed = mixed / total
        r.lse[head] = top + jnp.log(total)
        for g in range(groups):
            first = (head * groups + g) * width
            r.att[:, first : first + width] = mixed[:, g * rows : (g + 1) * rows].T

    def sum_flows(which, pieces=2):
        half = rows // 2
        count = half // pieces
        return [
            tp_sum_flow(
                copies, r.sum_in.at[which], r.sum_out.at[which], r.sum_landed.at[which],
                r.sum_chip.at[which], r.sum_far.at[which], partner_core, partner_far, core,
                piece * count, count, rows,
            )
            for piece in range(pieces)
        ]

    attb = r.att[...].astype(BF16)
    loads["w_o"].wait()
    r.sum_in[0] = dot(attb, r.w_o[...]).astype(BF16)
    flows = step_forward(sum_flows(0))
    for name in ("w_gate", "w_up", "w_down"):
        loads[name].wait()
    r.gob[...] = r.cotangent[...].astype(BF16)
    r.dhid[...] = transposed_dot(r.gob[...], r.w_down[...])
    run_together(flows)
    xmid = r.x[...] + r.sum_out[0].astype(F32)
    r.xmid[...] = xmid

    r2 = rms_scale(xmid)
    xhat2 = xmid * r2
    r.r2[...] = r2
    normed2 = (xhat2 * r.ffn_gain[...]).astype(BF16)
    r.normed2[...] = normed2
    gate = dot(normed2, r.w_gate[...])
    up = dot(normed2, r.w_up[...])
    sig = jax.nn.sigmoid(gate)
    silu = gate * sig
    hid = (silu * up).astype(BF16)
    d_hid = r.dhid[...]
    d_gate = (d_hid * up * sig * (1.0 + gate * (1.0 - sig))).astype(BF16)
    d_up = (d_hid * silu).astype(BF16)
    r.hid[...] = hid
    r.d_gate[...] = d_gate
    r.d_up[...] = d_up
    dn2_part = transposed_dot(d_gate, r.w_gate[...]) + transposed_dot(d_up, r.w_up[...])
    r.ffn_small[...] = jnp.sum(dn2_part * xhat2, axis=0, keepdims=True)
    r.sum_in[1] = dn2_part.astype(BF16)
    sums = step_forward(sum_flows(1))
    r.sum_in[2] = dot(r.hid[...], r.w_down[...]).astype(BF16)
    hidden_sums = sum_flows(2)

    groups_of_flows = {}

    def start(name):
        flows = []
        source, result = getattr(r, "g_" + name), getattr(r, "grad_" + name)
        for (order, first, count), buffers in zip(WEIGHT_PARTS[name], r.weight_buffers[name]):
            columns = pl.ds(first, count)
            flows.append(
                scatter_flow(
                    copies, coords, tp, source.at[:, :, :, :, columns], result.at[:, columns],
                    buffers, order, 0,
                )
            )
        groups_of_flows[name] = step_forward(flows)

    def tick(*names):
        for name in names:
            groups_of_flows[name] = step_forward(groups_of_flows[name])

    sums = step_forward(sums)
    tokens_product(r.normed2, r.d_gate[...], r.g_gate)
    start("gate")
    sums = step_forward(sums)
    hidden_sums = step_forward(hidden_sums)
    tokens_product(r.normed2, r.d_up[...], r.g_up)
    start("up")
    run_together(sums)

    dn2 = r.sum_out[1].astype(F32)
    xhat2 = r.xmid[...] * r.r2[...]
    dmid = r.cotangent[...] + norm_backward(dn2 * r.ffn_gain[...], xhat2, r.r2[...])
    r.dmid[...] = dmid
    dmidb = dmid.astype(BF16)
    r.dmidb[...] = dmidb
    d_att = transposed_dot(dmidb, r.w_o[...])
    r.d_attb[...] = d_att.astype(BF16)
    for head in range(heads_kv):
        pieces = []
        for g in range(groups):
            first = (head * groups + g) * width
            product = d_att[:, first : first + width] * r.att[:, first : first + width]
            pieces.append(jnp.sum(product.T, axis=0, keepdims=True))
        r.delta[head] = jnp.concatenate(pieces, axis=1)
    tick("gate")
    tokens_product(r.gob, r.hid[...], r.g_down)
    start("down")
    tick("up")
    hidden_sums = step_forward(hidden_sums)

    r.dq_acc[...] = jnp.zeros_like(r.dq_acc)

    def backward_step(i, carry):
        starts = chunk_starts(i)
        for head in range(heads_kv):
            head_queries = stacked(r.q_rot, head, groups, width)
            grads = stacked(r.d_attb, head, groups, width)
            base = kv_width + head * width
            keys = chunk_of(i, head * width)
            values = chunk_of(i, base)
            scores = masked_scores(keys, head_queries, starts, q_pos, inv_root)
            probs = jnp.exp(scores - r.lse[head])
            d_prob = transposed_dot(values, grads)
            d_scores = (probs * (d_prob - r.delta[head])).astype(BF16)
            d_keys = dot(d_scores, head_queries) * inv_root
            d_values = dot(probs.astype(BF16), grads)
            where = (i // 4, lax.rem(i, 4), slice(None), slice(None))
            shape = (4, rows, width)
            r.dkv[where + (slice(head * width, (head + 1) * width),)] = d_keys.astype(BF16).reshape(shape)
            r.dkv[where + (slice(base, base + width),)] = d_values.astype(BF16).reshape(shape)
            r.dq_acc[head] += first_dims_dot(keys, d_scores)
        return carry

    lax.fori_loop(0, 2, backward_step, 0)
    run_together(hidden_sums)
    tick("gate", "down")
    lax.fori_loop(2, 4, backward_step, 0)
    tick("up", "gate")
    lax.fori_loop(4, 6, backward_step, 0)
    tick("down", "up", "gate")
    lax.fori_loop(6, 8, backward_step, 0)
    late = []
    for (order, first, count), buffers in zip(ROW_PARTS, r.kv_buffers):
        part_rows = pl.ds(first, count)
        late.append(
            scatter_flow(
                copies, coords, tp, r.dkv.at[:, :, :, part_rows, :],
                r.dkv_own.at[part_rows, :], buffers, order, 1,
            )
        )
    groups_of_flows["kv"] = step_forward(late)
    tick("up", "down")
    r.hidden_out[...] = r.xmid[...] + r.sum_out[2].astype(F32)

    def store(name):
        copy = pltpu.make_async_copy(
            getattr(r, name), getattr(r, name + "_hbm"), r.store_sem.at[r.output_names.index(name)]
        )
        copy.start()
        return copy

    stores = [store("hidden_out")]

    small_q = jnp.zeros((1, width), F32)
    for head in range(heads_kv):
        for g in range(groups):
            index = head * groups + g
            here = slice(index * width, (index + 1) * width)
            grad = rope_back(r.dq_acc[head, :, g * rows : (g + 1) * rows].T * inv_root, cosine, sine)
            hat = r.qhat[:, here]
            small_q = small_q + jnp.sum(grad * hat, axis=0, keepdims=True)
            r.dqb[:, here] = norm_backward(grad * r.query_gain[...], hat, r.rq[index]).astype(BF16)
    tokens_product(r.normed1, r.dqb[...], r.g_query)
    r.dn1[...] = transposed_dot(r.dqb[...], r.w_q[...])
    tick("kv")
    start("query")
    tick("down")
    tick("kv")
    tokens_product(r.dmidb, r.att[...].astype(BF16), r.g_out)
    start("out")
    tick("query")
    tick("kv")
    tick("out", "query")
    tick("kv")

    small_k = jnp.zeros((1, width), F32)
    for head in range(heads_kv):
        here = slice(head * width, (head + 1) * width)
        grad = rope_back(r.dkv_own[:, here], cosine, sine)
        hat = r.khat[:, here]
        small_k = small_k + jnp.sum(grad * hat, axis=0, keepdims=True)
        r.dkb[:, here] = norm_backward(grad * r.key_gain[...], hat, r.rk[head]).astype(BF16)
    r.dvb[...] = r.dkv_own[:, kv_width:].astype(BF16)
    dn1_part = (
        r.dn1[...] + transposed_dot(r.dkb[...], r.w_k[...]) + transposed_dot(r.dvb[...], r.w_v[...])
    )
    xhat1 = r.x[...] * r.r1[...]
    r.sum_in[3] = dn1_part.astype(BF16)
    sums = step_forward(sum_flows(3))
    r.small_in[0:1, 0:1024] = jnp.sum(dn1_part * xhat1, axis=0, keepdims=True)
    r.small_in[0:1, 1024:2048] = r.ffn_small[...]
    r.small_in[0:1, 2048:2176] = small_q
    r.small_in[0:1, 2176:2304] = small_k
    tokens_product(r.normed1, r.dkb[...], r.g_key)
    tokens_product(r.normed1, r.dvb[...], r.g_value)
    start("key")
    start("value")
    groups_of_flows["small"] = step_forward(
        [sum_everywhere_flow(copies, coords, tp, r.small_in, r.small_out, r.small_slots)]
    )
    sums = step_forward(sums)
    tick("out", "query", "key", "value", "small")
    run_together(sums)
    flows = []
    dn1 = r.sum_out[3].astype(F32)
    r.input_gradient[...] = r.dmid[...] + norm_backward(
        dn1 * r.attention_gain[...], r.x[...] * r.r1[...], r.r1[...]
    )
    stores.append(store("input_gradient"))
    for name in list(groups_of_flows):
        flows = flows + groups_of_flows.pop(name)
    assert not any(groups_of_flows.values())
    run_together(flows)
    stores += [store(name) for name in r.output_names if name not in ("hidden_out", "input_gradient")]
    copies.drain()
    assert (copies.sends, copies.count) == (SENDS, RECEIVES), (copies.sends, copies.count)
    for copy in stores:
        copy.wait()


SENDS, RECEIVES = 66, 184
WEIGHT_NAMES = ("w_k", "w_v", "w_q", "w_o", "w_gate", "w_up", "w_down")


def whole_layer(
    layer_input, cotangent, weights, gains, cosine, sine, positions, heads_kv, groups
):
    rows, features = layer_input.shape
    width = cosine.shape[1]
    heads_q = heads_kv * groups
    q_width, kv_width = heads_q * width, heads_kv * width
    hidden = weights["w_gate"].shape[1]
    hbm = pl.BlockSpec(memory_space=pl.ANY)
    inputs = {
        "x": layer_input, "cotangent": cotangent, "cosine": cosine, "sine": sine,
        "positions": positions, **gains,
    }
    columns = {
        "gate": hidden, "up": hidden, "down": hidden, "out": q_width,
        "query": q_width, "key": kv_width, "value": kv_width,
    }
    outputs = {
        "hidden_out": ((rows, features), F32),
        "input_gradient": ((rows, features), F32),
        "small_out": ((1, 2304), F32),
    }
    for name, count in columns.items():
        outputs["grad_" + name] = ((32, count), F32)
    scratch = {
        "send_sem": pltpu.SemaphoreType.DMA((SENDS,)),
        "recv_sem": pltpu.SemaphoreType.DMA((RECEIVES,)),
        "load_sem": pltpu.SemaphoreType.DMA((len(WEIGHT_NAMES) + len(inputs),)),
        "store_sem": pltpu.SemaphoreType.DMA((len(outputs),)),
    }
    for name in WEIGHT_NAMES:
        scratch[name] = pltpu.VMEM(weights[name].shape, BF16)
    for name, shape, kind in (
        ("normed1", (rows, features), BF16),
        ("normed2", (rows, features), BF16),
        ("gob", (rows, features), BF16),
        ("dmidb", (rows, features), BF16),
        ("r1", (rows, 1), F32),
        ("r2", (rows, 1), F32),
        ("rq", (heads_q, rows, 1), F32),
        ("rk", (heads_kv, rows, 1), F32),
        ("qhat", (rows, q_width), F32),
        ("khat", (rows, kv_width), F32),
        ("q_rot", (rows, q_width), BF16),
        ("kv_all", (2, 4, 4, rows, 2 * kv_width), BF16),
        ("pos_all", (2, 4, 4, 1, 256), jnp.int32),
        ("scores", (32 * rows, groups * rows), F32),
        ("lse", (heads_kv, 1, groups * rows), F32),
        ("delta", (heads_kv, 1, groups * rows), F32),
        ("att", (rows, q_width), F32),
        ("sum_in", (4, rows, features), BF16),
        ("sum_out", (4, rows, features), BF16),
        ("sum_landed", (4, rows // 2, features), BF16),
        ("sum_chip", (4, rows // 2, features), BF16),
        ("sum_far", (4, rows // 2, features), BF16),
        ("xmid", (rows, features), F32),
        ("dmid", (rows, features), F32),
        ("dn1", (rows, features), F32),
        ("dhid", (rows, hidden), F32),
        ("hid", (rows, hidden), BF16),
        ("d_gate", (rows, hidden), BF16),
        ("d_up", (rows, hidden), BF16),
        ("ffn_small", (1, features), F32),
        ("d_attb", (rows, q_width), BF16),
        ("dq_acc", (heads_kv, width, groups * rows), F32),
        ("dkv", (2, 4, 4, rows, 2 * kv_width), BF16),
        ("dkv_own", (rows, 2 * kv_width), F32),
        ("dqb", (rows, q_width), BF16),
        ("dkb", (rows, kv_width), BF16),
        ("dvb", (rows, kv_width), BF16),
        ("small_in", (1, 2304), F32),
    ):
        scratch[name] = pltpu.VMEM(shape, kind)
    for name, count in columns.items():
        scratch["g_" + name] = pltpu.VMEM((2, 4, 4, 32, count), BF16)
    lists = {"small_slots": sum_everywhere_scratch((1, 2304))}
    for name, count in columns.items():
        for i, (order, first, size) in enumerate(WEIGHT_PARTS[name]):
            lists["%s_%d" % (name, i)] = scatter_scratch((32, size), order, 0)
    for i, (order, first, count) in enumerate(ROW_PARTS):
        lists["kv_%d" % i] = scatter_scratch((count, 2 * kv_width), order, 1)

    load_names = tuple(inputs) + WEIGHT_NAMES
    for name, value in inputs.items():
        scratch[name] = pltpu.VMEM(value.shape, value.dtype)
    for name, (shape, kind) in outputs.items():
        scratch[name] = pltpu.VMEM(shape, kind)
    input_names = [name + "_hbm" for name in load_names]
    flat_scratch = list(scratch.values())
    for buffers in lists.values():
        flat_scratch.extend(buffers)

    def kernel(*refs):
        r = types.SimpleNamespace()
        r.input_names = tuple(inputs)
        r.output_names = tuple(outputs)
        names = input_names + [name + "_hbm" for name in outputs] + list(scratch)
        for name, ref in zip(names, refs):
            setattr(r, name, ref)
        rest = list(refs[len(names) :])
        groups_of = {}
        for name, buffers in lists.items():
            groups_of[name], rest = rest[: len(buffers)], rest[len(buffers) :]
        r.small_slots = groups_of["small_slots"]
        r.weight_buffers = {
            name: [groups_of["%s_%d" % (name, i)] for i in range(len(WEIGHT_PARTS[name]))]
            for name in columns
        }
        r.kv_buffers = [groups_of["kv_%d" % i] for i in range(len(ROW_PARTS))]
        layer_kernel(r, (heads_kv, groups, width))

    results = pl.pallas_call(
        kernel,
        out_shape=tuple(jax.ShapeDtypeStruct(shape, kind) for shape, kind in outputs.values()),
        in_specs=[hbm] * len(load_names),
        out_specs=(hbm,) * len(outputs),
        scratch_shapes=flat_scratch,
        compiler_params=pltpu.CompilerParams(
            collective_id=0, has_side_effects=True, vmem_limit_bytes=67043328
        ),
        name="whole_layer",
    )(*inputs.values(), *[weights[name] for name in WEIGHT_NAMES])
    return dict(zip(outputs, results))


def body(
    layer_input,
    positions,
    attention_norm_gain,
    w_query,
    key_projection,
    value_projection,
    query_norm,
    key_norm_gain,
    output_projection,
    feedforward_norm_gain,
    w_gate,
    w_up,
    w_down,
    output_cotangent,
):
    head_dim = query_norm.shape[0]
    heads_q = w_query.shape[1] // head_dim
    heads_kv = key_projection.shape[1] // head_dim
    groups = heads_q // heads_kv
    cosine, sine = rope_tables(positions, head_dim)
    out = whole_layer(
        layer_input,
        output_cotangent,
        {
            "w_q": w_query, "w_k": key_projection, "w_v": value_projection, "w_o": output_projection,
            "w_gate": w_gate, "w_up": w_up, "w_down": w_down,
        },
        {
            "attention_gain": attention_norm_gain.reshape(1, -1),
            "ffn_gain": feedforward_norm_gain.reshape(1, -1),
            "query_gain": query_norm.reshape(1, -1),
            "key_gain": key_norm_gain.reshape(1, -1),
        },
        cosine,
        sine,
        positions.reshape(1, -1),
        heads_kv,
        groups,
    )
    names = (
        "hidden_out", "input_gradient", "grad_query", "grad_key", "grad_value", "grad_out",
        "grad_gate", "grad_up", "grad_down", "small_out",
    )
    written = write_results([out[name] for name in names], (1024, 1024, 128, 128))
    done = dict(zip(names[:-1], written))
    small = [piece.reshape(-1) for piece in written[len(names) - 1 :]]
    return (
        done["hidden_out"],
        done["input_gradient"],
        small[0],
        done["grad_query"],
        done["grad_key"],
        done["grad_value"],
        small[2],
        small[3],
        done["grad_out"].T,
        small[1],
        done["grad_gate"],
        done["grad_up"],
        done["grad_down"].T,
    )


def solution(mesh):
    return jax.shard_map(
        body,
        mesh=mesh,
        in_specs=(
            P("ctx", None),
            P("ctx"),
            P(),
            P(None, "tp"),
            P(None, "tp"),
            P(None, "tp"),
            P(),
            P(),
            P("tp", None),
            P(),
            P(None, "tp"),
            P(None, "tp"),
            P("tp", None),
            P("ctx", None),
        ),
        out_specs=(
            P("ctx", None),
            P("ctx", None),
            P(),
            P("ctx", "tp"),
            P("ctx", "tp"),
            P("ctx", "tp"),
            P(),
            P(),
            P("tp", "ctx"),
            P(),
            P("ctx", "tp"),
            P("ctx", "tp"),
            P("tp", "ctx"),
        ),
        check_vma=False,
    )
```

```python
import math
import types

import jax
import jax.numpy as jnp
from jax import lax
from jax.experimental import pallas as pl
from jax.experimental.pallas import tpu as pltpu
from jax.sharding import PartitionSpec as P

EPSILON = 1e-06
ROPE_BASE = 1000000.0
MASKED = -1e30


MESH = pl.DeviceIdType.MESH
SIZES = {"y": 2, "z": 4, "x": 4}
DIMS = ("y", "z", "x")


def place():
    me = lax.axis_index("ctx")
    return {"y": me // 16, "z": lax.rem(me // 4, 4), "x": lax.rem(me, 4)}, lax.axis_index("tp")


def shifted(coords, dim, step):
    moved = dict(coords)
    moved[dim] = lax.rem(coords[dim] + step + SIZES[dim], SIZES[dim])
    return moved


def device_at(coords, tp):
    return (coords["y"] * 16 + coords["z"] * 4 + coords["x"], tp)


class Copies:
    def __init__(self, send_sem, recv_sem):
        self.send_sem, self.recv_sem = send_sem, recv_sem
        self.count = 0
        self.sends = 0
        self.free = []
        self.started = {}

    def slot(self):
        self.count += 1
        return self.count - 1

    def send(self, source, target, device, slot=None):
        if self.free:
            place = self.free.pop(0)
        else:
            place = self.sends
            self.sends += 1
        copy = pltpu.make_async_remote_copy(
            src_ref=source,
            dst_ref=target,
            send_sem=self.send_sem.at[place],
            recv_sem=self.recv_sem.at[self.slot() if slot is None else slot],
            device_id=device,
            device_id_type=MESH,
        )
        copy.start()
        self.started[id(copy)] = (copy, place)
        return copy

    def landed(self, ref, slot, device):
        pltpu.make_async_remote_copy(
            src_ref=ref,
            dst_ref=ref,
            send_sem=self.send_sem.at[0],
            recv_sem=self.recv_sem.at[slot],
            device_id=device,
            device_id_type=MESH,
        ).wait_recv()

    def sent(self, *copies):
        for copy in copies:
            unused, place = self.started.pop(id(copy))
            copy.wait_send()
            self.free.append(place)

    def drain(self):
        for copy, unused in self.started.values():
            copy.wait_send()


def run_together(flows):
    live = list(flows)
    while live:
        left = []
        for flow in live:
            try:
                next(flow)
                left.append(flow)
            except StopIteration:
                pass
        live = left


def gather_small_flow(copies, coords, tp, ref, order, piece, halves):
    def region(held, where, part):
        index = tuple(slice(None) if dim in held else where[dim] for dim in DIMS)
        return ref.at[index + part]

    held = []
    for dim in order:
        right = device_at(shifted(coords, dim, 1), tp)
        mine = region(held, coords, piece)
        if SIZES[dim] == 2:
            copy = copies.send(mine, mine, right)
            yield
            copy.wait_recv()
        else:
            left = device_at(shifted(coords, dim, -1), tp)
            go_right = copies.send(mine, mine, right)
            go_left = copies.send(mine, mine, left)
            yield
            go_right.wait_recv()
            block = region(held, shifted(coords, dim, -1), halves[0])
            pass_right = copies.send(block, block, right)
            pass_left = None
            if halves[1] is not None:
                go_left.wait_recv()
                block = region(held, shifted(coords, dim, 1), halves[1])
                pass_left = copies.send(block, block, left)
            yield
            pass_right.wait_recv()
            if pass_left is None:
                go_left.wait_recv()
            else:
                pass_left.wait_recv()
        held.append(dim)


def gather_flow(copies, coords, tp, ref, order, piece, halves):
    first, second, last = order

    def to(dim, step):
        return device_at(shifted(coords, dim, step), tp)

    def spot(dim, step):
        return shifted(coords, dim, step)[dim]

    def region(where, part):
        return ref.at[tuple(where[dim] for dim in DIMS) + part]

    pending, passed = [], []

    def send_last(where):
        block = region({**where, last: coords[last]}, piece)
        right = copies.send(block, block, to(last, 1))
        left = copies.send(block, block, to(last, -1)) if SIZES[last] == 4 else None
        pending.append((where, right, left))

    def pass_on(count):
        for unused in range(count):
            where, right, left = pending.pop(0)
            right.wait_recv()
            copies.sent(right)
            if left is None:
                continue
            block = region({**where, last: spot(last, -1)}, halves[0])
            passed.append(copies.send(block, block, to(last, 1)))
            left.wait_recv()
            copies.sent(left)
            block = region({**where, last: spot(last, 1)}, halves[1])
            passed.append(copies.send(block, block, to(last, -1)))

    def spread(dim, where, after):
        block = region({**where, dim: coords[dim], last: coords[last]}, piece)
        right = copies.send(block, block, to(dim, 1))
        left = copies.send(block, block, to(dim, -1)) if SIZES[dim] == 4 else None
        after()
        yield
        older = len(pending)
        right.wait_recv()
        if left is None:
            send_last({**where, dim: spot(dim, 1)})
            pass_on(older)
            return
        here = {**where, last: coords[last]}
        block = region({**here, dim: spot(dim, -1)}, halves[0])
        far_right = copies.send(block, block, to(dim, 1))
        send_last({**where, dim: spot(dim, -1)})
        left.wait_recv()
        block = region({**here, dim: spot(dim, 1)}, halves[1])
        far_left = copies.send(block, block, to(dim, -1))
        send_last({**where, dim: spot(dim, 1)})
        pass_on(older)
        yield
        older = len(pending)
        far_right.wait_recv()
        far_left.wait_recv()
        send_last({**where, dim: spot(dim, 2)})
        pass_on(older)

    yield from spread(
        first,
        {second: coords[second]},
        lambda: send_last({first: coords[first], second: coords[second]}),
    )
    yield from spread(second, {first: slice(None)}, lambda: None)
    yield
    pass_on(len(pending))
    yield
    for copy in passed:
        copy.wait_recv()
    copies.sent(*passed)


def leading_index(flat, dims):
    index = []
    for dim in reversed(dims):
        index.insert(0, lax.rem(flat, SIZES[dim]))
        flat = flat // SIZES[dim]
    return tuple(index)


def leading_shape(dims):
    return tuple(SIZES[dim] for dim in dims)


def over_leading(dims, step):
    count = math.prod(leading_shape(dims))
    if count == 1:
        step(())
        return

    def body(flat, carry):
        step(leading_index(flat, dims))
        return carry

    lax.fori_loop(0, count, body, 0)


def scatter_scratch(shape, order, axis):
    half = tuple(size // 2 if i == axis else size for i, size in enumerate(shape))
    buffers = []
    rest = list(DIMS)
    for dim in order:
        rest.remove(dim)
        lead = leading_shape(rest)
        if SIZES[dim] == 2:
            buffers.append(pltpu.VMEM(lead + shape, jnp.bfloat16))
        elif dim != order[0]:
            buffers.append(pltpu.VMEM((3,) + lead + shape, jnp.bfloat16))
        else:
            buffers.extend([pltpu.VMEM(lead + half, jnp.bfloat16)] * 4)
            buffers.append(pltpu.VMEM((4,) + lead + half, jnp.bfloat16))
        if rest:
            buffers.append(pltpu.VMEM(lead + shape, jnp.bfloat16))
    return buffers


def scatter_flow(copies, coords, tp, source, result, buffers, order, axis):
    buffers = list(buffers)
    shape = source.shape[-2:]
    size = shape[axis] // 2
    halves = [
        tuple(pl.ds(h * size, size) if i == axis else slice(None) for i in range(2))
        for h in range(2)
    ]
    whole = (slice(None), slice(None))
    current = source
    dims = list(DIMS)

    for dim in order:
        rest = [d for d in dims if d != dim]
        spot = dims.index(dim)

        def at(where, lead, part, spot=spot, current=current):
            index = tuple(lead[:spot]) + (where[dim],) + tuple(lead[spot:])
            return current.at[index + part]

        everywhere = (slice(None),) * len(rest)
        right_coords = shifted(coords, dim, 1)
        right = device_at(right_coords, tp)
        f32 = jnp.float32
        if SIZES[dim] == 2:
            landed = buffers.pop(0)
            copy = copies.send(at(right_coords, everywhere, whole), landed, right)
            target = buffers.pop(0) if rest else result
            yield
            copy.wait_recv()
            copies.sent(copy)

            def add(lead):
                total = at(coords, lead, whole)[...].astype(f32) + landed[lead + whole].astype(f32)
                target[lead + whole] = total.astype(target.dtype)

            over_leading(rest, add)
        elif dim != order[0]:
            landed = buffers.pop(0)
            target = buffers.pop(0) if rest else result
            sent = []
            slot = copies.slot()
            for step in (1, 2, 3):
                there = shifted(coords, dim, step)
                block = at(there, everywhere, whole)
                sent.append(copies.send(block, landed.at[step - 1], device_at(there, tp), slot))
            yield
            copies.landed(landed, slot, right)
            copies.sent(*sent)

            def add(lead):
                total = at(coords, lead, whole)[...].astype(f32)
                for i in range(3):
                    total = total + landed[(i,) + lead + whole].astype(f32)
                target[lead + whole] = total.astype(target.dtype)

            over_leading(rest, add)
        else:
            left_coords = shifted(coords, dim, -1)
            far_coords = shifted(coords, dim, 2)
            left = device_at(left_coords, tp)
            pass_l, pass_r, out_r, out_l, arrived = buffers[:5]
            buffers = buffers[5:]
            near_l, near_r, sum_l, sum_r = [arrived.at[i] for i in range(4)]
            slot = copies.slot()
            target = buffers.pop(0) if rest else result
            relay_r = copies.send(at(far_coords, everywhere, halves[0]), pass_l, right)
            relay_l = copies.send(at(far_coords, everywhere, halves[1]), pass_r, left)
            direct_r = copies.send(at(right_coords, everywhere, halves[1]), near_l, right, slot)
            direct_l = copies.send(at(left_coords, everywhere, halves[0]), near_r, left, slot)
            yield
            relay_r.wait_recv()

            def merge_right(lead):
                total = at(right_coords, lead, halves[0])[...].astype(f32) + pass_l[
                    lead + whole
                ].astype(f32)
                out_r[lead + whole] = total.astype(out_r.dtype)

            over_leading(rest, merge_right)
            merged_r = copies.send(out_r, sum_l, right, slot)
            relay_l.wait_recv()

            def merge_left(lead):
                total = at(left_coords, lead, halves[1])[...].astype(f32) + pass_r[
                    lead + whole
                ].astype(f32)
                out_l[lead + whole] = total.astype(out_l.dtype)

            over_leading(rest, merge_left)
            merged_l = copies.send(out_l, sum_r, left, slot)
            yield
            copies.landed(arrived, slot, right)
            copies.sent(relay_r, relay_l, direct_r, direct_l, merged_r, merged_l)

            def add(lead):
                for half, one, two in ((halves[0], sum_l, near_r), (halves[1], near_l, sum_r)):
                    total = (
                        at(coords, lead, half)[...].astype(f32)
                        + one[lead + whole].astype(f32)
                        + two[lead + whole].astype(f32)
                    )
                    target[lead + half] = total.astype(target.dtype)

            over_leading(rest, add)
        current = target
        dims = rest


def column_peers(coords, tp):
    place_in_column = coords["y"] * 4 + tp
    peers = []
    for step in range(1, 8):
        other = lax.rem(place_in_column + step, 8)
        peers.append(device_at({**coords, "y": other // 4}, lax.rem(other, 4)))
    return place_in_column, peers


def sum_everywhere_flow(copies, coords, tp, source, result, slots):
    current = source
    column, peers = column_peers(coords, tp)
    stages = [
        (coords[dim], [device_at(shifted(coords, dim, step), tp) for step in (1, 2, 3)])
        for dim in ("x", "z")
    ] + [(column, peers)]
    for stage, (spot, others) in enumerate(stages):
        ring = slots[stage]
        ring[spot] = current[...]
        slot = copies.slot()
        sent = [copies.send(current, ring.at[spot], other, slot) for other in others]
        yield
        copies.landed(ring.at[pl.ds(0, len(others))], slot, others[0])
        copies.sent(*sent)
        total = ring[0]
        for i in range(1, len(others) + 1):
            total = total + ring[i]
        target = slots[3 + stage] if stage < 2 else result
        target[...] = total
        current = target


def sum_everywhere_scratch(shape):
    rings = [pltpu.VMEM((count,) + shape, jnp.float32) for count in (4, 4, 8)]
    return rings + [pltpu.VMEM(shape, jnp.float32)] * 2


def tp_sum_flow(copies, ins, out, landed, chip, far, partner_core, partner_far, core, first, count, rows):
    half = rows // 2
    mine = pl.ds(pl.multiple_of(core * half + first, 16), count)
    theirs = pl.ds(pl.multiple_of((1 - core) * half + first, 16), count)
    local = pl.ds(first, count)
    f32 = jnp.float32
    copy = copies.send(ins.at[theirs], landed.at[local], partner_core)
    yield
    copy.wait_recv()
    copies.sent(copy)
    chip[local] = (ins[mine].astype(f32) + landed[local].astype(f32)).astype(chip.dtype)
    copy = copies.send(chip.at[local], far.at[local], partner_far)
    yield
    copy.wait_recv()
    copies.sent(copy)
    out[mine] = (chip[local].astype(f32) + far[local].astype(f32)).astype(out.dtype)
    copy = copies.send(out.at[mine], out.at[mine], partner_core)
    yield
    copy.wait_recv()
    copies.sent(copy)


def write_results(arrays, splits):
    number = len(arrays)
    pieces = [(array.shape[0], size) for array, size in zip(arrays[-1:] * len(splits), splits)]
    shapes = [array.shape for array in arrays[:-1]] + pieces

    def kernel(*refs):
        ins, outs = refs[:number], refs[number : number + len(shapes)]
        held, (in_sem, out_sem) = refs[number + len(shapes) : -2], refs[-2:]
        loads = [
            pltpu.make_async_copy(source, target, in_sem.at[i])
            for i, (source, target) in enumerate(zip(ins, held))
        ]
        for load in loads:
            load.start()
        stores = []
        for i, load in enumerate(loads[:-1]):
            load.wait()
            stores.append(pltpu.make_async_copy(held[i], outs[i], out_sem.at[i]))
            stores[-1].start()
        loads[-1].wait()
        begin = 0
        for i, size in enumerate(splits):
            slot = number - 1 + i
            source = held[-1].at[:, pl.ds(begin, size)]
            stores.append(pltpu.make_async_copy(source, outs[slot], out_sem.at[slot]))
            stores[-1].start()
            begin += size
        for store in stores:
            store.wait()

    hbm = pl.BlockSpec(memory_space=pl.ANY)
    return pl.pallas_call(
        kernel,
        out_shape=tuple(jax.ShapeDtypeStruct(shape, jnp.float32) for shape in shapes),
        in_specs=[hbm] * number,
        out_specs=(hbm,) * len(shapes),
        scratch_shapes=[pltpu.VMEM(array.shape, jnp.float32) for array in arrays]
        + [pltpu.SemaphoreType.DMA((number,)), pltpu.SemaphoreType.DMA((len(shapes),))],
        compiler_params=pltpu.CompilerParams(vmem_limit_bytes=60 << 20),
        name="write_results",
    )(*arrays)


def rms_scale(values):
    return lax.rsqrt(jnp.mean(values * values, axis=-1, keepdims=True) + EPSILON)


def norm_backward(grad, normed, scale_rows):
    return scale_rows * (grad - normed * jnp.mean(grad * normed, axis=-1, keepdims=True))


def rope_tables(positions, head_dim):
    half_dim = head_dim // 2
    lane = jnp.arange(head_dim, dtype=jnp.int32)
    pair = jnp.where(lane < half_dim, lane, lane - half_dim).astype(jnp.float32)
    freqs = jnp.exp(-(2.0 * pair / head_dim) * math.log(ROPE_BASE))
    angles = positions.astype(jnp.float32)[:, None] * freqs[None, :]
    sign = jnp.where(lane < half_dim, -1.0, 1.0).astype(jnp.float32)
    return (jnp.cos(angles), jnp.sin(angles) * sign[None, :])


XZY, ZYX, YXZ = ("x", "z", "y"), ("z", "y", "x"), ("y", "x", "z")
ROW_PARTS = ((XZY, 0, 48), (ZYX, 48, 48), (YXZ, 96, 32))
THREE_PARTS = ((XZY, 0, 256), (ZYX, 256, 256), (YXZ, 512, 256))
TWO_PARTS = ((XZY, 0, 256), (ZYX, 256, 256))
WEIGHT_PARTS = {
    "gate": THREE_PARTS,
    "up": THREE_PARTS,
    "down": THREE_PARTS,
    "out": TWO_PARTS,
    "query": TWO_PARTS,
    "key": ((YXZ, 0, 256),),
    "value": ((XZY, 0, 128), (ZYX, 128, 128)),
}
F32, BF16 = jnp.float32, jnp.bfloat16


def rope(values, cosine, sine):
    return values * cosine + pltpu.roll(values, 64, 1) * sine


def rope_back(grad, cosine, sine):
    return grad * cosine - pltpu.roll(grad, 64, 1) * sine


def dot(left, right):
    return jnp.dot(left, right, preferred_element_type=F32)


def stacked(ref, head, groups, width):
    return jnp.concatenate(
        [ref[:, (head * groups + g) * width : (head * groups + g + 1) * width] for g in range(groups)],
        axis=0,
    )


def transposed_dot(left, right):
    return lax.dot_general(left, right, (((1,), (1,)), ((), ())), preferred_element_type=F32)


def first_dims_dot(left, right):
    return lax.dot_general(left, right, (((0,), (0,)), ((), ())), preferred_element_type=F32)


def masked_scores(keys, queries, starts, q_pos, inv_root):
    scores = transposed_dot(keys, queries) * inv_root
    step = lax.broadcasted_iota(jnp.int32, (64, queries.shape[0]), 0)
    pieces = []
    for b, start in enumerate(starts):
        ahead = q_pos - start
        pieces.append(jnp.where(ahead >= step, scores[b * 64 : (b + 1) * 64], MASKED))
    return jnp.concatenate(pieces, axis=0)


def step_forward(flows):
    return [flow for flow in flows if next(flow, "done") != "done"]


def tokens_product(left_ref, right, target):
    def step(i, carry):
        for j in range(4):
            block = left_ref[:, pl.ds(pl.multiple_of(i * 512 + j * 128, 128), 128)]
            part = first_dims_dot(block, right).astype(BF16)
            target[i, j] = part.reshape(4, 32, right.shape[1])
        return carry

    lax.fori_loop(0, left_ref.shape[1] // 512, step, 0)


def layer_kernel(r, sizes):
    heads_kv, groups, width = sizes
    heads_q = heads_kv * groups
    rows = r.x.shape[0]
    inv_root = 1.0 / math.sqrt(width)
    kv_width = heads_kv * width
    coords, tp = place()
    ctx = lax.axis_index("ctx")
    core = lax.rem(tp, 2)
    partner_core = (ctx, tp + 1 - 2 * core)
    partner_far = (ctx, lax.rem(tp + 2, 4))
    peers = [
        device_at(shifted(coords, dim, step), tp) for dim in ("z", "x") for step in (1, 2, 3)
    ] + column_peers(coords, tp)[1]
    own = (coords["y"], coords["z"], coords["x"])
    copies = Copies(r.send_sem, r.recv_sem)

    barrier = pltpu.get_barrier_semaphore()
    for peer in peers:
        pl.semaphore_signal(barrier, inc=1, device_id=peer, device_id_type=MESH)

    loads = {}
    for i, name in enumerate(r.input_names + WEIGHT_NAMES):
        loads[name] = pltpu.make_async_copy(
            getattr(r, name + "_hbm"), getattr(r, name), r.load_sem.at[i]
        )
    for name in r.input_names + WEIGHT_NAMES[:3]:
        loads[name].start()

    for name in r.input_names:
        loads[name].wait()
    cosine, sine = r.cosine[...], r.sine[...]
    x = r.x[...]
    r1 = rms_scale(x)
    xhat1 = x * r1
    normed1 = (xhat1 * r.attention_gain[...]).astype(BF16)
    r.normed1[...] = normed1
    r.r1[...] = r1
    loads["w_k"].wait()
    unnormed = dot(normed1, r.w_k[...])
    for head in range(heads_kv):
        part = unnormed[:, head * width : (head + 1) * width]
        scale = rms_scale(part)
        hat = part * scale
        r.khat[:, head * width : (head + 1) * width] = hat
        r.rk[head] = scale
        r.kv_all[own + (slice(None), slice(2 * head * width, (2 * head + 1) * width))] = rope(
            hat * r.key_gain[...], cosine, sine
        ).astype(BF16)
    loads["w_v"].wait()
    values = dot(normed1, r.w_v[...]).astype(BF16)
    for head in range(heads_kv):
        r.kv_all[own + (slice(None), slice((2 * head + 1) * width, (2 * head + 2) * width))] = values[
            :, head * width : (head + 1) * width
        ]
    positions = r.positions[...]
    r.pos_all[own] = jnp.concatenate(
        [jnp.broadcast_to(positions[:, first : first + 1], (1, 128)) for first in (0, 64)], axis=1
    )
    pl.semaphore_wait(barrier, len(peers))
    head_flows = []
    for head in range(heads_kv):
        key_columns = pl.ds(2 * head * width, width)
        value_columns = pl.ds((2 * head + 1) * width, width)
        both = pl.ds(2 * head * width, 2 * width)
        head_flows.append(
            [
                gather_flow(
                    copies, coords, tp, r.kv_all, order,
                    (pl.ds(first, count), both),
                    ((pl.ds(first, count), key_columns), (pl.ds(first, count), value_columns)),
                )
                for order, first, count in ROW_PARTS
            ]
        )
    whole = (slice(None), slice(None))
    head_flows[0].append(
        gather_small_flow(copies, coords, tp, r.pos_all, ("y", "z", "x"), whole, (whole, None))
    )
    head_flows[0] = step_forward(head_flows[0])
    for later in head_flows[1:]:
        later[:] = step_forward(later)
    for name in WEIGHT_NAMES[3:]:
        loads[name].start()
    loads["w_q"].wait()
    queries = dot(normed1, r.w_q[...])
    for head in range(heads_q):
        part = queries[:, head * width : (head + 1) * width]
        scale = rms_scale(part)
        hat = part * scale
        r.qhat[:, head * width : (head + 1) * width] = hat
        r.rq[head] = scale
        r.q_rot[:, head * width : (head + 1) * width] = rope(
            hat * r.query_gain[...], cosine, sine
        ).astype(BF16)
    while head_flows[0]:
        head_flows[0] = step_forward(head_flows[0])
        if head_flows[0]:
            for later in head_flows[1:]:
                later[:] = step_forward(later)

    q_pos = jnp.concatenate([r.positions[...]] * groups, axis=1)
    per = 4 * rows

    def chunk_starts(i):
        starts = []
        for c in range(4):
            row = r.pos_all[i // 4, lax.rem(i, 4), c]
            for b in range(2):
                piece = row[:, b * 128 : (b + 1) * 128]
                starts.append(jnp.concatenate([piece] * groups, axis=1))
        return starts

    def chunk_of(i, begin):
        return r.kv_all[i // 4, lax.rem(i, 4), :, :, begin : begin + width].reshape(per, width)

    for head in range(heads_kv):
        head_queries = stacked(r.q_rot, head, groups, width)

        def score_step(i, top, head=head, head_queries=head_queries):
            scores = masked_scores(
                chunk_of(i, 2 * head * width), head_queries, chunk_starts(i), q_pos, inv_root
            )
            r.scores[pl.ds(pl.multiple_of(i * per, per), per), :] = scores
            return jnp.maximum(top, jnp.max(scores, axis=0, keepdims=True))

        top = lax.fori_loop(
            0, 8, score_step, jnp.full((1, groups * rows), MASKED, F32), unroll=2
        )

        for later in head_flows[head + 1 :]:
            later[:] = step_forward(later)

        def weight_step(i, carry, head=head, top=top):
            total, mixed = carry
            values = chunk_of(i, (2 * head + 1) * width)
            weights = jnp.exp(r.scores[pl.ds(pl.multiple_of(i * per, per), per), :] - top)
            total = total + jnp.sum(weights, axis=0, keepdims=True)
            return total, mixed + first_dims_dot(values, weights.astype(BF16))

        total, mixed = lax.fori_loop(
            0, 8, weight_step,
            (jnp.zeros((1, groups * rows), F32), jnp.zeros((width, groups * rows), F32)),
            unroll=2,
        )
        for later in head_flows[head + 1 : head + 2]:
            run_together(later)
            later[:] = []
        mixed = mixed / total
        r.lse[head] = top + jnp.log(total)
        for g in range(groups):
            first = (head * groups + g) * width
            r.att[:, first : first + width] = mixed[:, g * rows : (g + 1) * rows].T

    def sum_flows(which, pieces=2):
        half = rows // 2
        count = half // pieces
        return [
            tp_sum_flow(
                copies, r.sum_in.at[which], r.sum_out.at[which], r.sum_landed.at[which],
                r.sum_chip.at[which], r.sum_far.at[which], partner_core, partner_far, core,
                piece * count, count, rows,
            )
            for piece in range(pieces)
        ]

    attb = r.att[...].astype(BF16)
    loads["w_o"].wait()
    r.sum_in[0] = dot(attb, r.w_o[...]).astype(BF16)
    flows = step_forward(sum_flows(0))
    for name in ("w_gate", "w_up", "w_down"):
        loads[name].wait()
    r.gob[...] = r.cotangent[...].astype(BF16)
    r.dhid[...] = transposed_dot(r.gob[...], r.w_down[...])
    run_together(flows)
    xmid = r.x[...] + r.sum_out[0].astype(F32)
    r.xmid[...] = xmid

    r2 = rms_scale(xmid)
    xhat2 = xmid * r2
    r.r2[...] = r2
    normed2 = (xhat2 * r.ffn_gain[...]).astype(BF16)
    r.normed2[...] = normed2
    gate = dot(normed2, r.w_gate[...])
    up = dot(normed2, r.w_up[...])
    sig = jax.nn.sigmoid(gate)
    silu = gate * sig
    hid = (silu * up).astype(BF16)
    d_hid = r.dhid[...]
    d_gate = (d_hid * up * sig * (1.0 + gate * (1.0 - sig))).astype(BF16)
    d_up = (d_hid * silu).astype(BF16)
    r.hid[...] = hid
    r.d_gate[...] = d_gate
    r.d_up[...] = d_up
    dn2_part = transposed_dot(d_gate, r.w_gate[...]) + transposed_dot(d_up, r.w_up[...])
    r.ffn_small[...] = jnp.sum(dn2_part * xhat2, axis=0, keepdims=True)
    r.sum_in[1] = dn2_part.astype(BF16)
    sums = step_forward(sum_flows(1))
    r.sum_in[2] = dot(r.hid[...], r.w_down[...]).astype(BF16)
    hidden_sums = sum_flows(2)

    groups_of_flows = {}

    def start(name):
        flows = []
        source, result = getattr(r, "g_" + name), getattr(r, "grad_" + name)
        for (order, first, count), buffers in zip(WEIGHT_PARTS[name], r.weight_buffers[name]):
            columns = pl.ds(first, count)
            flows.append(
                scatter_flow(
                    copies, coords, tp, source.at[:, :, :, :, columns], result.at[:, columns],
                    buffers, order, 0,
                )
            )
        groups_of_flows[name] = step_forward(flows)

    def tick(*names):
        for name in names:
            groups_of_flows[name] = step_forward(groups_of_flows[name])

    sums = step_forward(sums)
    tokens_product(r.normed2, r.d_gate[...], r.g_gate)
    start("gate")
    sums = step_forward(sums)
    hidden_sums = step_forward(hidden_sums)
    tokens_product(r.normed2, r.d_up[...], r.g_up)
    start("up")
    run_together(sums)

    dn2 = r.sum_out[1].astype(F32)
    xhat2 = r.xmid[...] * r.r2[...]
    dmid = r.cotangent[...] + norm_backward(dn2 * r.ffn_gain[...], xhat2, r.r2[...])
    r.dmid[...] = dmid
    dmidb = dmid.astype(BF16)
    r.dmidb[...] = dmidb
    d_att = transposed_dot(dmidb, r.w_o[...])
    r.d_attb[...] = d_att.astype(BF16)
    for head in range(heads_kv):
        pieces = []
        for g in range(groups):
            first = (head * groups + g) * width
            product = d_att[:, first : first + width] * r.att[:, first : first + width]
            pieces.append(jnp.sum(product.T, axis=0, keepdims=True))
        r.delta[head] = jnp.concatenate(pieces, axis=1)
    tick("gate")
    tick("up")
    hidden_sums = step_forward(hidden_sums)

    r.dq_acc[...] = jnp.zeros_like(r.dq_acc)

    def backward_step(head, i):
        head_queries = stacked(r.q_rot, head, groups, width)
        grads = stacked(r.d_attb, head, groups, width)
        base = 2 * head * width
        keys = chunk_of(i, base)
        values = chunk_of(i, base + width)
        scores = masked_scores(keys, head_queries, chunk_starts(i), q_pos, inv_root)
        probs = jnp.exp(scores - r.lse[head])
        d_prob = transposed_dot(values, grads)
        d_scores = (probs * (d_prob - r.delta[head])).astype(BF16)
        d_keys = dot(d_scores, head_queries) * inv_root
        d_values = dot(probs.astype(BF16), grads)
        where = (i // 4, lax.rem(i, 4), slice(None), slice(None))
        shape = (4, rows, width)
        r.dkv[where + (slice(base, base + width),)] = d_keys.astype(BF16).reshape(shape)
        r.dkv[where + (slice(base + width, base + 2 * width),)] = d_values.astype(BF16).reshape(shape)
        r.dq_acc[head] += first_dims_dot(keys, d_scores)

    def backward_range(head, begin, end):
        def body(i, carry):
            backward_step(head, i)
            return carry

        lax.fori_loop(begin, end, body, 0, unroll=2)

    def start_kv(head):
        flows = []
        columns = pl.ds(2 * head * width, 2 * width)
        for (order, first, count), buffers in zip(ROW_PARTS, r.kv_buffers[3 * head : 3 * head + 3]):
            part_rows = pl.ds(first, count)
            flows.append(
                scatter_flow(
                    copies, coords, tp, r.dkv.at[:, :, :, part_rows, columns],
                    r.dkv_own.at[part_rows, columns], buffers, order, 1,
                )
            )
        groups_of_flows["kv%d" % head] = step_forward(flows)

    backward_range(0, 0, 4)
    run_together(hidden_sums)
    tick("gate")
    backward_range(0, 4, 8)
    start_kv(0)
    tick("up", "gate")
    backward_range(1, 0, 4)
    tick("kv0", "up", "gate")
    backward_range(1, 4, 8)
    start_kv(1)
    tick("up")
    r.hidden_out[...] = r.xmid[...] + r.sum_out[2].astype(F32)

    def store(name):
        copy = pltpu.make_async_copy(
            getattr(r, name), getattr(r, name + "_hbm"), r.store_sem.at[r.output_names.index(name)]
        )
        copy.start()
        return copy

    stores = [store("hidden_out")]

    small_q = jnp.zeros((1, width), F32)
    for head in range(heads_kv):
        for g in range(groups):
            index = head * groups + g
            here = slice(index * width, (index + 1) * width)
            grad = rope_back(r.dq_acc[head, :, g * rows : (g + 1) * rows].T * inv_root, cosine, sine)
            hat = r.qhat[:, here]
            small_q = small_q + jnp.sum(grad * hat, axis=0, keepdims=True)
            r.dqb[:, here] = norm_backward(grad * r.query_gain[...], hat, r.rq[index]).astype(BF16)
    tokens_product(r.normed1, r.dqb[...], r.g_query)
    r.dn1[...] = transposed_dot(r.dqb[...], r.w_q[...])
    tick("kv0", "kv1")
    start("query")
    tick("kv0", "kv1")
    tokens_product(r.gob, r.hid[...], r.g_down)
    start("down")
    tick("query")
    tick("kv0", "kv1")
    tokens_product(r.dmidb, r.att[...].astype(BF16), r.g_out)
    start("out")
    tick("down", "query")
    tick("kv0", "kv1")

    small_k = jnp.zeros((1, width), F32)
    for head in range(heads_kv):
        here = slice(head * width, (head + 1) * width)
        base = 2 * head * width
        grad = rope_back(r.dkv_own[:, base : base + width], cosine, sine)
        hat = r.khat[:, here]
        small_k = small_k + jnp.sum(grad * hat, axis=0, keepdims=True)
        r.dvb[:, here] = r.dkv_own[:, base + width : base + 2 * width].astype(BF16)
        r.dkb[:, here] = norm_backward(grad * r.key_gain[...], hat, r.rk[head]).astype(BF16)
    dn1_part = (
        r.dn1[...] + transposed_dot(r.dkb[...], r.w_k[...]) + transposed_dot(r.dvb[...], r.w_v[...])
    )
    xhat1 = r.x[...] * r.r1[...]
    r.sum_in[3] = dn1_part.astype(BF16)
    sums = step_forward(sum_flows(3))
    r.small_in[0:1, 0:1024] = jnp.sum(dn1_part * xhat1, axis=0, keepdims=True)
    r.small_in[0:1, 1024:2048] = r.ffn_small[...]
    r.small_in[0:1, 2048:2176] = small_q
    r.small_in[0:1, 2176:2304] = small_k
    groups_of_flows["small"] = step_forward(
        [sum_everywhere_flow(copies, coords, tp, r.small_in, r.small_out, r.small_slots)]
    )
    tokens_product(r.normed1, r.dkb[...], r.g_key)
    start("key")
    sums = step_forward(sums)
    tokens_product(r.normed1, r.dvb[...], r.g_value)
    start("value")
    tick("small", "key", "value", "query", "down", "out")
    run_together(sums)
    flows = []
    dn1 = r.sum_out[3].astype(F32)
    r.input_gradient[...] = r.dmid[...] + norm_backward(
        dn1 * r.attention_gain[...], r.x[...] * r.r1[...], r.r1[...]
    )
    stores.append(store("input_gradient"))
    for name in ("small", "key", "value", "query", "down", "out", "up", "gate", "kv0", "kv1"):
        flows = flows + groups_of_flows.pop(name)
    assert not any(groups_of_flows.values())
    run_together(flows)
    stores += [store(name) for name in r.output_names if name not in ("hidden_out", "input_gradient")]
    copies.drain()
    assert (copies.sends, copies.count) == (SENDS, RECEIVES)
    for copy in stores:
        copy.wait()


SENDS, RECEIVES = 90, 262
WEIGHT_NAMES = ("w_k", "w_v", "w_q", "w_o", "w_gate", "w_up", "w_down")


def whole_layer(
    layer_input, cotangent, weights, gains, cosine, sine, positions, heads_kv, groups
):
    rows, features = layer_input.shape
    width = cosine.shape[1]
    heads_q = heads_kv * groups
    q_width, kv_width = heads_q * width, heads_kv * width
    hidden = weights["w_gate"].shape[1]
    hbm = pl.BlockSpec(memory_space=pl.ANY)
    inputs = {
        "x": layer_input, "cotangent": cotangent, "cosine": cosine, "sine": sine,
        "positions": positions, **gains,
    }
    columns = {
        "gate": hidden, "up": hidden, "down": hidden, "out": q_width,
        "query": q_width, "key": kv_width, "value": kv_width,
    }
    outputs = {
        "hidden_out": ((rows, features), F32),
        "input_gradient": ((rows, features), F32),
        "small_out": ((1, 2304), F32),
    }
    for name, count in columns.items():
        outputs["grad_" + name] = ((32, count), F32)
    scratch = {
        "send_sem": pltpu.SemaphoreType.DMA((SENDS,)),
        "recv_sem": pltpu.SemaphoreType.DMA((RECEIVES,)),
        "load_sem": pltpu.SemaphoreType.DMA((len(WEIGHT_NAMES) + len(inputs),)),
        "store_sem": pltpu.SemaphoreType.DMA((len(outputs),)),
    }
    for name in WEIGHT_NAMES:
        scratch[name] = pltpu.VMEM(weights[name].shape, BF16)
    for name, shape, kind in (
        ("normed1", (rows, features), BF16),
        ("normed2", (rows, features), BF16),
        ("gob", (rows, features), BF16),
        ("dmidb", (rows, features), BF16),
        ("r1", (rows, 1), F32),
        ("r2", (rows, 1), F32),
        ("rq", (heads_q, rows, 1), F32),
        ("rk", (heads_kv, rows, 1), F32),
        ("qhat", (rows, q_width), F32),
        ("khat", (rows, kv_width), F32),
        ("q_rot", (rows, q_width), BF16),
        ("kv_all", (2, 4, 4, rows, 2 * kv_width), BF16),
        ("pos_all", (2, 4, 4, 1, 256), jnp.int32),
        ("scores", (32 * rows, groups * rows), F32),
        ("lse", (heads_kv, 1, groups * rows), F32),
        ("delta", (heads_kv, 1, groups * rows), F32),
        ("att", (rows, q_width), F32),
        ("sum_in", (4, rows, features), BF16),
        ("sum_out", (4, rows, features), BF16),
        ("sum_landed", (4, rows // 2, features), BF16),
        ("sum_chip", (4, rows // 2, features), BF16),
        ("sum_far", (4, rows // 2, features), BF16),
        ("xmid", (rows, features), F32),
        ("dmid", (rows, features), F32),
        ("dn1", (rows, features), F32),
        ("dhid", (rows, hidden), F32),
        ("hid", (rows, hidden), BF16),
        ("d_gate", (rows, hidden), BF16),
        ("d_up", (rows, hidden), BF16),
        ("ffn_small", (1, features), F32),
        ("d_attb", (rows, q_width), BF16),
        ("dq_acc", (heads_kv, width, groups * rows), F32),
        ("dkv", (2, 4, 4, rows, 2 * kv_width), BF16),
        ("dkv_own", (rows, 2 * kv_width), F32),
        ("dqb", (rows, q_width), BF16),
        ("dkb", (rows, kv_width), BF16),
        ("dvb", (rows, kv_width), BF16),
        ("small_in", (1, 2304), F32),
    ):
        scratch[name] = pltpu.VMEM(shape, kind)
    for name, count in columns.items():
        scratch["g_" + name] = pltpu.VMEM((2, 4, 4, 32, count), BF16)
    lists = {"small_slots": sum_everywhere_scratch((1, 2304))}
    for name, count in columns.items():
        for i, (order, first, size) in enumerate(WEIGHT_PARTS[name]):
            lists["%s_%d" % (name, i)] = scatter_scratch((32, size), order, 0)
    for i, (order, first, count) in enumerate(ROW_PARTS):
        for head in range(heads_kv):
            lists["kv_%d_%d" % (head, i)] = scatter_scratch((count, 2 * width), order, 1)

    load_names = tuple(inputs) + WEIGHT_NAMES
    for name, value in inputs.items():
        scratch[name] = pltpu.VMEM(value.shape, value.dtype)
    for name, (shape, kind) in outputs.items():
        scratch[name] = pltpu.VMEM(shape, kind)
    input_names = [name + "_hbm" for name in load_names]
    flat_scratch = list(scratch.values())
    for buffers in lists.values():
        flat_scratch.extend(buffers)

    def kernel(*refs):
        r = types.SimpleNamespace()
        r.input_names = tuple(inputs)
        r.output_names = tuple(outputs)
        names = input_names + [name + "_hbm" for name in outputs] + list(scratch)
        for name, ref in zip(names, refs):
            setattr(r, name, ref)
        rest = list(refs[len(names) :])
        groups_of = {}
        for name, buffers in lists.items():
            groups_of[name], rest = rest[: len(buffers)], rest[len(buffers) :]
        r.small_slots = groups_of["small_slots"]
        r.weight_buffers = {
            name: [groups_of["%s_%d" % (name, i)] for i in range(len(WEIGHT_PARTS[name]))]
            for name in columns
        }
        r.kv_buffers = [
            groups_of["kv_%d_%d" % (head, i)]
            for head in range(heads_kv)
            for i in range(len(ROW_PARTS))
        ]
        layer_kernel(r, (heads_kv, groups, width))

    results = pl.pallas_call(
        kernel,
        out_shape=tuple(jax.ShapeDtypeStruct(shape, kind) for shape, kind in outputs.values()),
        in_specs=[hbm] * len(load_names),
        out_specs=(hbm,) * len(outputs),
        scratch_shapes=flat_scratch,
        compiler_params=pltpu.CompilerParams(
            collective_id=0, has_side_effects=True, vmem_limit_bytes=67043328
        ),
        name="whole_layer",
    )(*inputs.values(), *[weights[name] for name in WEIGHT_NAMES])
    return dict(zip(outputs, results))


def body(
    layer_input,
    positions,
    attention_norm_gain,
    w_query,
    key_projection,
    value_projection,
    query_norm,
    key_norm_gain,
    output_projection,
    feedforward_norm_gain,
    w_gate,
    w_up,
    w_down,
    output_cotangent,
):
    head_dim = query_norm.shape[0]
    heads_q = w_query.shape[1] // head_dim
    heads_kv = key_projection.shape[1] // head_dim
    groups = heads_q // heads_kv
    cosine, sine = rope_tables(positions, head_dim)
    out = whole_layer(
        layer_input,
        output_cotangent,
        {
            "w_q": w_query, "w_k": key_projection, "w_v": value_projection, "w_o": output_projection,
            "w_gate": w_gate, "w_up": w_up, "w_down": w_down,
        },
        {
            "attention_gain": attention_norm_gain.reshape(1, -1),
            "ffn_gain": feedforward_norm_gain.reshape(1, -1),
            "query_gain": query_norm.reshape(1, -1),
            "key_gain": key_norm_gain.reshape(1, -1),
        },
        cosine,
        sine,
        positions.reshape(1, -1),
        heads_kv,
        groups,
    )
    names = (
        "hidden_out", "input_gradient", "grad_query", "grad_key", "grad_value", "grad_out",
        "grad_gate", "grad_up", "grad_down", "small_out",
    )
    written = write_results([out[name] for name in names], (1024, 1024, 128, 128))
    done = dict(zip(names[:-1], written))
    small = [piece.reshape(-1) for piece in written[len(names) - 1 :]]
    return (
        done["hidden_out"],
        done["input_gradient"],
        small[0],
        done["grad_query"],
        done["grad_key"],
        done["grad_value"],
        small[2],
        small[3],
        done["grad_out"].T,
        small[1],
        done["grad_gate"],
        done["grad_up"],
        done["grad_down"].T,
    )


def solution(mesh):
    return jax.shard_map(
        body,
        mesh=mesh,
        in_specs=(
            P("ctx", None),
            P("ctx"),
            P(),
            P(None, "tp"),
            P(None, "tp"),
            P(None, "tp"),
            P(),
            P(),
            P("tp", None),
            P(),
            P(None, "tp"),
            P(None, "tp"),
            P("tp", None),
            P("ctx", None),
        ),
        out_specs=(
            P("ctx", None),
            P("ctx", None),
            P(),
            P("ctx", "tp"),
            P("ctx", "tp"),
            P("ctx", "tp"),
            P(),
            P(),
            P("tp", "ctx"),
            P(),
            P("ctx", "tp"),
            P("ctx", "tp"),
            P("tp", "ctx"),
        ),
        check_vma=False,
    )
```

```python
import math
import types

import jax
import jax.numpy as jnp
from jax import lax
from jax.experimental import pallas as pl
from jax.experimental.pallas import tpu as pltpu
from jax.sharding import PartitionSpec as P

EPSILON = 1e-06
ROPE_BASE = 1000000.0
MASKED = -1e30


MESH = pl.DeviceIdType.MESH
SIZES = {"y": 2, "z": 4, "x": 4}
DIMS = ("y", "z", "x")


def place():
    me = lax.axis_index("ctx")
    return {"y": me // 16, "z": lax.rem(me // 4, 4), "x": lax.rem(me, 4)}, lax.axis_index("tp")


def shifted(coords, dim, step):
    moved = dict(coords)
    moved[dim] = lax.rem(coords[dim] + step + SIZES[dim], SIZES[dim])
    return moved


def device_at(coords, tp):
    return (coords["y"] * 16 + coords["z"] * 4 + coords["x"], tp)


class Copies:
    def __init__(self, send_sem, recv_sem):
        self.send_sem, self.recv_sem = send_sem, recv_sem
        self.count = 0
        self.sends = 0
        self.free = []
        self.started = {}

    def slot(self):
        self.count += 1
        return self.count - 1

    def send(self, source, target, device, slot=None):
        if self.free:
            place = self.free.pop(0)
        else:
            place = self.sends
            self.sends += 1
        copy = pltpu.make_async_remote_copy(
            src_ref=source,
            dst_ref=target,
            send_sem=self.send_sem.at[place],
            recv_sem=self.recv_sem.at[self.slot() if slot is None else slot],
            device_id=device,
            device_id_type=MESH,
        )
        copy.start()
        self.started[id(copy)] = (copy, place)
        return copy

    def landed(self, ref, slot, device):
        pltpu.make_async_remote_copy(
            src_ref=ref,
            dst_ref=ref,
            send_sem=self.send_sem.at[0],
            recv_sem=self.recv_sem.at[slot],
            device_id=device,
            device_id_type=MESH,
        ).wait_recv()

    def sent(self, *copies):
        for copy in copies:
            unused, place = self.started.pop(id(copy))
            copy.wait_send()
            self.free.append(place)

    def drain(self):
        for copy, unused in self.started.values():
            copy.wait_send()


def run_together(flows):
    live = list(flows)
    while live:
        left = []
        for flow in live:
            try:
                next(flow)
                left.append(flow)
            except StopIteration:
                pass
        live = left


def gather_small_flow(copies, coords, tp, ref, order, piece, halves):
    def region(held, where, part):
        index = tuple(slice(None) if dim in held else where[dim] for dim in DIMS)
        return ref.at[index + part]

    held = []
    for dim in order:
        right = device_at(shifted(coords, dim, 1), tp)
        mine = region(held, coords, piece)
        if SIZES[dim] == 2:
            copy = copies.send(mine, mine, right)
            yield
            copy.wait_recv()
        else:
            left = device_at(shifted(coords, dim, -1), tp)
            go_right = copies.send(mine, mine, right)
            go_left = copies.send(mine, mine, left)
            yield
            go_right.wait_recv()
            block = region(held, shifted(coords, dim, -1), halves[0])
            pass_right = copies.send(block, block, right)
            pass_left = None
            if halves[1] is not None:
                go_left.wait_recv()
                block = region(held, shifted(coords, dim, 1), halves[1])
                pass_left = copies.send(block, block, left)
            yield
            pass_right.wait_recv()
            if pass_left is None:
                go_left.wait_recv()
            else:
                pass_left.wait_recv()
        held.append(dim)


def gather_flow(copies, coords, tp, ref, order, piece, halves):
    first, second, last = order

    def to(dim, step):
        return device_at(shifted(coords, dim, step), tp)

    def spot(dim, step):
        return shifted(coords, dim, step)[dim]

    def region(where, part):
        return ref.at[tuple(where[dim] for dim in DIMS) + part]

    pending, passed = [], []

    def send_last(where):
        block = region({**where, last: coords[last]}, piece)
        right = copies.send(block, block, to(last, 1))
        left = copies.send(block, block, to(last, -1)) if SIZES[last] == 4 else None
        pending.append((where, right, left))

    def pass_on(count):
        for unused in range(count):
            where, right, left = pending.pop(0)
            right.wait_recv()
            copies.sent(right)
            if left is None:
                continue
            block = region({**where, last: spot(last, -1)}, halves[0])
            passed.append(copies.send(block, block, to(last, 1)))
            left.wait_recv()
            copies.sent(left)
            block = region({**where, last: spot(last, 1)}, halves[1])
            passed.append(copies.send(block, block, to(last, -1)))

    def spread(dim, where, after):
        block = region({**where, dim: coords[dim], last: coords[last]}, piece)
        right = copies.send(block, block, to(dim, 1))
        left = copies.send(block, block, to(dim, -1)) if SIZES[dim] == 4 else None
        after()
        yield
        older = len(pending)
        right.wait_recv()
        if left is None:
            send_last({**where, dim: spot(dim, 1)})
            pass_on(older)
            return
        here = {**where, last: coords[last]}
        block = region({**here, dim: spot(dim, -1)}, halves[0])
        far_right = copies.send(block, block, to(dim, 1))
        send_last({**where, dim: spot(dim, -1)})
        left.wait_recv()
        block = region({**here, dim: spot(dim, 1)}, halves[1])
        far_left = copies.send(block, block, to(dim, -1))
        send_last({**where, dim: spot(dim, 1)})
        pass_on(older)
        yield
        older = len(pending)
        far_right.wait_recv()
        far_left.wait_recv()
        send_last({**where, dim: spot(dim, 2)})
        pass_on(older)

    yield from spread(
        first,
        {second: coords[second]},
        lambda: send_last({first: coords[first], second: coords[second]}),
    )
    yield from spread(second, {first: slice(None)}, lambda: None)
    yield
    pass_on(len(pending))
    yield
    for copy in passed:
        copy.wait_recv()
    copies.sent(*passed)


def leading_index(flat, dims):
    index = []
    for dim in reversed(dims):
        index.insert(0, lax.rem(flat, SIZES[dim]))
        flat = flat // SIZES[dim]
    return tuple(index)


def leading_shape(dims):
    return tuple(SIZES[dim] for dim in dims)


def over_leading(dims, step):
    count = math.prod(leading_shape(dims))
    if count == 1:
        step(())
        return

    def body(flat, carry):
        step(leading_index(flat, dims))
        return carry

    lax.fori_loop(0, count, body, 0, unroll=4 if count % 4 == 0 else 2)


def scatter_scratch(shape, order, axis):
    half = tuple(size // 2 if i == axis else size for i, size in enumerate(shape))
    buffers = []
    rest = list(DIMS)
    for dim in order:
        rest.remove(dim)
        lead = leading_shape(rest)
        if SIZES[dim] == 2:
            buffers.append(pltpu.VMEM(lead + shape, jnp.bfloat16))
        elif dim != order[0]:
            buffers.append(pltpu.VMEM((3,) + lead + shape, jnp.bfloat16))
        else:
            buffers.extend([pltpu.VMEM(lead + half, jnp.bfloat16)] * 4)
            buffers.append(pltpu.VMEM((4,) + lead + half, jnp.bfloat16))
        if rest:
            buffers.append(pltpu.VMEM(lead + shape, jnp.bfloat16))
    return buffers


def scatter_flow(copies, coords, tp, source, result, buffers, order, axis):
    buffers = list(buffers)
    shape = source.shape[-2:]
    size = shape[axis] // 2
    halves = [
        tuple(pl.ds(h * size, size) if i == axis else slice(None) for i in range(2))
        for h in range(2)
    ]
    whole = (slice(None), slice(None))
    current = source
    dims = list(DIMS)

    for dim in order:
        rest = [d for d in dims if d != dim]
        spot = dims.index(dim)

        def at(where, lead, part, spot=spot, current=current):
            index = tuple(lead[:spot]) + (where[dim],) + tuple(lead[spot:])
            return current.at[index + part]

        everywhere = (slice(None),) * len(rest)
        right_coords = shifted(coords, dim, 1)
        right = device_at(right_coords, tp)
        f32 = jnp.float32
        if SIZES[dim] == 2:
            landed = buffers.pop(0)
            copy = copies.send(at(right_coords, everywhere, whole), landed, right)
            target = buffers.pop(0) if rest else result
            yield
            copy.wait_recv()
            copies.sent(copy)

            def add(lead):
                total = at(coords, lead, whole)[...].astype(f32) + landed[lead + whole].astype(f32)
                target[lead + whole] = total.astype(target.dtype)

            over_leading(rest, add)
        elif dim != order[0]:
            landed = buffers.pop(0)
            target = buffers.pop(0) if rest else result
            sent = []
            slot = copies.slot()
            for step in (1, 2, 3):
                there = shifted(coords, dim, step)
                block = at(there, everywhere, whole)
                sent.append(copies.send(block, landed.at[step - 1], device_at(there, tp), slot))
            yield
            copies.landed(landed, slot, right)
            copies.sent(*sent)

            def add(lead):
                total = at(coords, lead, whole)[...].astype(f32)
                for i in range(3):
                    total = total + landed[(i,) + lead + whole].astype(f32)
                target[lead + whole] = total.astype(target.dtype)

            over_leading(rest, add)
        else:
            left_coords = shifted(coords, dim, -1)
            far_coords = shifted(coords, dim, 2)
            left = device_at(left_coords, tp)
            pass_l, pass_r, out_r, out_l, arrived = buffers[:5]
            buffers = buffers[5:]
            near_l, near_r, sum_l, sum_r = [arrived.at[i] for i in range(4)]
            slot = copies.slot()
            target = buffers.pop(0) if rest else result
            relay_r = copies.send(at(far_coords, everywhere, halves[0]), pass_l, right)
            relay_l = copies.send(at(far_coords, everywhere, halves[1]), pass_r, left)
            direct_r = copies.send(at(right_coords, everywhere, halves[1]), near_l, right, slot)
            direct_l = copies.send(at(left_coords, everywhere, halves[0]), near_r, left, slot)
            yield
            relay_r.wait_recv()

            def merge_right(lead):
                total = at(right_coords, lead, halves[0])[...].astype(f32) + pass_l[
                    lead + whole
                ].astype(f32)
                out_r[lead + whole] = total.astype(out_r.dtype)

            over_leading(rest, merge_right)
            merged_r = copies.send(out_r, sum_l, right, slot)
            relay_l.wait_recv()

            def merge_left(lead):
                total = at(left_coords, lead, halves[1])[...].astype(f32) + pass_r[
                    lead + whole
                ].astype(f32)
                out_l[lead + whole] = total.astype(out_l.dtype)

            over_leading(rest, merge_left)
            merged_l = copies.send(out_l, sum_r, left, slot)
            yield
            copies.landed(arrived, slot, right)
            copies.sent(relay_r, relay_l, direct_r, direct_l, merged_r, merged_l)

            def add(lead):
                for half, one, two in ((halves[0], sum_l, near_r), (halves[1], near_l, sum_r)):
                    total = (
                        at(coords, lead, half)[...].astype(f32)
                        + one[lead + whole].astype(f32)
                        + two[lead + whole].astype(f32)
                    )
                    target[lead + half] = total.astype(target.dtype)

            over_leading(rest, add)
        current = target
        dims = rest


def column_peers(coords, tp):
    place_in_column = coords["y"] * 4 + tp
    peers = []
    for step in range(1, 8):
        other = lax.rem(place_in_column + step, 8)
        peers.append(device_at({**coords, "y": other // 4}, lax.rem(other, 4)))
    return place_in_column, peers


def sum_everywhere_flow(copies, coords, tp, source, result, slots):
    current = source
    column, peers = column_peers(coords, tp)
    stages = [
        (coords[dim], [device_at(shifted(coords, dim, step), tp) for step in (1, 2, 3)])
        for dim in ("x", "z")
    ] + [(column, peers)]
    for stage, (spot, others) in enumerate(stages):
        ring = slots[stage]
        ring[spot] = current[...]
        slot = copies.slot()
        sent = [copies.send(current, ring.at[spot], other, slot) for other in others]
        yield
        copies.landed(ring.at[pl.ds(0, len(others))], slot, others[0])
        copies.sent(*sent)
        total = ring[0]
        for i in range(1, len(others) + 1):
            total = total + ring[i]
        target = slots[3 + stage] if stage < 2 else result
        target[...] = total
        current = target


def sum_everywhere_scratch(shape):
    rings = [pltpu.VMEM((count,) + shape, jnp.float32) for count in (4, 4, 8)]
    return rings + [pltpu.VMEM(shape, jnp.float32)] * 2


def tp_sum_flow(copies, ins, out, landed, chip, far, partner_core, partner_far, core, first, count, rows):
    half = rows // 2
    mine = pl.ds(pl.multiple_of(core * half + first, 16), count)
    theirs = pl.ds(pl.multiple_of((1 - core) * half + first, 16), count)
    local = pl.ds(first, count)
    f32 = jnp.float32
    copy = copies.send(ins.at[theirs], landed.at[local], partner_core)
    yield
    copy.wait_recv()
    copies.sent(copy)
    chip[local] = (ins[mine].astype(f32) + landed[local].astype(f32)).astype(chip.dtype)
    copy = copies.send(chip.at[local], far.at[local], partner_far)
    yield
    copy.wait_recv()
    copies.sent(copy)
    out[mine] = (chip[local].astype(f32) + far[local].astype(f32)).astype(out.dtype)
    copy = copies.send(out.at[mine], out.at[mine], partner_core)
    yield
    copy.wait_recv()
    copies.sent(copy)


def write_results(arrays, splits):
    number = len(arrays)
    pieces = [(array.shape[0], size) for array, size in zip(arrays[-1:] * len(splits), splits)]
    shapes = [array.shape for array in arrays[:-1]] + pieces

    def kernel(*refs):
        ins, outs = refs[:number], refs[number : number + len(shapes)]
        held, (in_sem, out_sem) = refs[number + len(shapes) : -2], refs[-2:]
        loads = [
            pltpu.make_async_copy(source, target, in_sem.at[i])
            for i, (source, target) in enumerate(zip(ins, held))
        ]
        for load in loads:
            load.start()
        stores = []
        for i, load in enumerate(loads[:-1]):
            load.wait()
            stores.append(pltpu.make_async_copy(held[i], outs[i], out_sem.at[i]))
            stores[-1].start()
        loads[-1].wait()
        begin = 0
        for i, size in enumerate(splits):
            slot = number - 1 + i
            source = held[-1].at[:, pl.ds(begin, size)]
            stores.append(pltpu.make_async_copy(source, outs[slot], out_sem.at[slot]))
            stores[-1].start()
            begin += size
        for store in stores:
            store.wait()

    hbm = pl.BlockSpec(memory_space=pl.ANY)
    return pl.pallas_call(
        kernel,
        out_shape=tuple(jax.ShapeDtypeStruct(shape, jnp.float32) for shape in shapes),
        in_specs=[hbm] * number,
        out_specs=(hbm,) * len(shapes),
        scratch_shapes=[pltpu.VMEM(array.shape, jnp.float32) for array in arrays]
        + [pltpu.SemaphoreType.DMA((number,)), pltpu.SemaphoreType.DMA((len(shapes),))],
        compiler_params=pltpu.CompilerParams(vmem_limit_bytes=60 << 20),
        name="write_results",
    )(*arrays)


def rms_scale(values):
    return lax.rsqrt(jnp.mean(values * values, axis=-1, keepdims=True) + EPSILON)


def norm_backward(grad, normed, scale_rows):
    return scale_rows * (grad - normed * jnp.mean(grad * normed, axis=-1, keepdims=True))


def rope_tables(positions, head_dim):
    half_dim = head_dim // 2
    lane = jnp.arange(head_dim, dtype=jnp.int32)
    pair = jnp.where(lane < half_dim, lane, lane - half_dim).astype(jnp.float32)
    freqs = jnp.exp(-(2.0 * pair / head_dim) * math.log(ROPE_BASE))
    angles = positions.astype(jnp.float32)[:, None] * freqs[None, :]
    sign = jnp.where(lane < half_dim, -1.0, 1.0).astype(jnp.float32)
    return (jnp.cos(angles), jnp.sin(angles) * sign[None, :])


XZY, ZYX, YXZ = ("x", "z", "y"), ("z", "y", "x"), ("y", "x", "z")
ROW_PARTS = ((XZY, 0, 48), (ZYX, 48, 48), (YXZ, 96, 32))
THREE_PARTS = ((XZY, 0, 256), (ZYX, 256, 256), (YXZ, 512, 256))
TWO_PARTS = ((XZY, 0, 256), (ZYX, 256, 256))
WEIGHT_PARTS = {
    "gate": THREE_PARTS,
    "up": THREE_PARTS,
    "down": THREE_PARTS,
    "out": TWO_PARTS,
    "query": TWO_PARTS,
    "key": ((YXZ, 0, 256),),
    "value": ((XZY, 0, 128), (ZYX, 128, 128)),
}
F32, BF16 = jnp.float32, jnp.bfloat16


def rope(values, cosine, sine):
    return values * cosine + pltpu.roll(values, 64, 1) * sine


def rope_back(grad, cosine, sine):
    return grad * cosine - pltpu.roll(grad, 64, 1) * sine


def dot(left, right):
    return jnp.dot(left, right, preferred_element_type=F32)


def stacked(ref, head, groups, width):
    return jnp.concatenate(
        [ref[:, (head * groups + g) * width : (head * groups + g + 1) * width] for g in range(groups)],
        axis=0,
    )


def transposed_dot(left, right):
    return lax.dot_general(left, right, (((1,), (1,)), ((), ())), preferred_element_type=F32)


def first_dims_dot(left, right):
    return lax.dot_general(left, right, (((0,), (0,)), ((), ())), preferred_element_type=F32)


def masked_scores(keys, queries, starts, q_pos, inv_root):
    scores = transposed_dot(keys, queries) * inv_root
    step = lax.broadcasted_iota(jnp.int32, (64, queries.shape[0]), 0)
    pieces = []
    for b, start in enumerate(starts):
        ahead = q_pos - start
        pieces.append(jnp.where(ahead >= step, scores[b * 64 : (b + 1) * 64], MASKED))
    return jnp.concatenate(pieces, axis=0)


def step_forward(flows):
    return [flow for flow in flows if next(flow, "done") != "done"]


def tokens_product(left_ref, right, target):
    def step(i, carry):
        for j in range(4):
            block = left_ref[:, pl.ds(pl.multiple_of(i * 512 + j * 128, 128), 128)]
            part = first_dims_dot(block, right).astype(BF16)
            target[i, j] = part.reshape(4, 32, right.shape[1])
        return carry

    lax.fori_loop(0, left_ref.shape[1] // 512, step, 0)


def layer_kernel(r, sizes):
    heads_kv, groups, width = sizes
    heads_q = heads_kv * groups
    rows = r.x.shape[0]
    inv_root = 1.0 / math.sqrt(width)
    kv_width = heads_kv * width
    coords, tp = place()
    ctx = lax.axis_index("ctx")
    core = lax.rem(tp, 2)
    partner_core = (ctx, tp + 1 - 2 * core)
    partner_far = (ctx, lax.rem(tp + 2, 4))
    peers = [
        device_at(shifted(coords, dim, step), tp) for dim in ("z", "x") for step in (1, 2, 3)
    ] + column_peers(coords, tp)[1]
    own = (coords["y"], coords["z"], coords["x"])
    copies = Copies(r.send_sem, r.recv_sem)

    barrier = pltpu.get_barrier_semaphore()
    for peer in peers:
        pl.semaphore_signal(barrier, inc=1, device_id=peer, device_id_type=MESH)

    loads = {}
    for i, name in enumerate(r.input_names + WEIGHT_NAMES):
        loads[name] = pltpu.make_async_copy(
            getattr(r, name + "_hbm"), getattr(r, name), r.load_sem.at[i]
        )
    for name in r.input_names + WEIGHT_NAMES[:3]:
        loads[name].start()

    for name in r.input_names:
        loads[name].wait()
    cosine, sine = r.cosine[...], r.sine[...]
    x = r.x[...]
    r1 = rms_scale(x)
    xhat1 = x * r1
    normed1 = (xhat1 * r.attention_gain[...]).astype(BF16)
    r.normed1[...] = normed1
    r.r1[...] = r1
    loads["w_k"].wait()
    unnormed = dot(normed1, r.w_k[...])
    for head in range(heads_kv):
        part = unnormed[:, head * width : (head + 1) * width]
        scale = rms_scale(part)
        hat = part * scale
        r.khat[:, head * width : (head + 1) * width] = hat
        r.rk[head] = scale
        r.kv_all[own + (slice(None), slice(2 * head * width, (2 * head + 1) * width))] = rope(
            hat * r.key_gain[...], cosine, sine
        ).astype(BF16)
    loads["w_v"].wait()
    values = dot(normed1, r.w_v[...]).astype(BF16)
    for head in range(heads_kv):
        r.kv_all[own + (slice(None), slice((2 * head + 1) * width, (2 * head + 2) * width))] = values[
            :, head * width : (head + 1) * width
        ]
    positions = r.positions[...]
    r.pos_all[own] = jnp.concatenate(
        [jnp.broadcast_to(positions[:, first : first + 1], (1, 128)) for first in (0, 64)], axis=1
    )
    pl.semaphore_wait(barrier, len(peers))
    head_flows = []
    for head in range(heads_kv):
        key_columns = pl.ds(2 * head * width, width)
        value_columns = pl.ds((2 * head + 1) * width, width)
        both = pl.ds(2 * head * width, 2 * width)
        head_flows.append(
            [
                gather_flow(
                    copies, coords, tp, r.kv_all, order,
                    (pl.ds(first, count), both),
                    ((pl.ds(first, count), key_columns), (pl.ds(first, count), value_columns)),
                )
                for order, first, count in ROW_PARTS
            ]
        )
    whole = (slice(None), slice(None))
    head_flows[0].append(
        gather_small_flow(copies, coords, tp, r.pos_all, ("y", "z", "x"), whole, (whole, None))
    )
    head_flows[0] = step_forward(head_flows[0])
    for later in head_flows[1:]:
        later[:] = step_forward(later)
    for name in WEIGHT_NAMES[3:]:
        loads[name].start()
    loads["w_q"].wait()
    queries = dot(normed1, r.w_q[...])
    for head in range(heads_q):
        part = queries[:, head * width : (head + 1) * width]
        scale = rms_scale(part)
        hat = part * scale
        r.qhat[:, head * width : (head + 1) * width] = hat
        r.rq[head] = scale
        r.q_rot[:, head * width : (head + 1) * width] = rope(
            hat * r.query_gain[...], cosine, sine
        ).astype(BF16)
    while head_flows[0]:
        head_flows[0] = step_forward(head_flows[0])
        if head_flows[0]:
            for later in head_flows[1:]:
                later[:] = step_forward(later)

    q_pos = jnp.concatenate([r.positions[...]] * groups, axis=1)
    per = 4 * rows

    def chunk_starts(i):
        starts = []
        for c in range(4):
            row = r.pos_all[i // 4, lax.rem(i, 4), c]
            for b in range(2):
                piece = row[:, b * 128 : (b + 1) * 128]
                starts.append(jnp.concatenate([piece] * groups, axis=1))
        return starts

    def chunk_of(i, begin):
        return r.kv_all[i // 4, lax.rem(i, 4), :, :, begin : begin + width].reshape(per, width)

    for head in range(heads_kv):
        head_queries = stacked(r.q_rot, head, groups, width)

        def score_step(i, top, head=head, head_queries=head_queries):
            scores = masked_scores(
                chunk_of(i, 2 * head * width), head_queries, chunk_starts(i), q_pos, inv_root
            )
            r.scores[pl.ds(pl.multiple_of(i * per, per), per), :] = scores
            return jnp.maximum(top, jnp.max(scores, axis=0, keepdims=True))

        top = lax.fori_loop(
            0, 8, score_step, jnp.full((1, groups * rows), MASKED, F32), unroll=4
        )

        for later in head_flows[head + 1 :]:
            later[:] = step_forward(later)

        def weight_step(i, carry, head=head, top=top):
            total, mixed = carry
            values = chunk_of(i, (2 * head + 1) * width)
            weights = jnp.exp(r.scores[pl.ds(pl.multiple_of(i * per, per), per), :] - top)
            total = total + jnp.sum(weights, axis=0, keepdims=True)
            return total, mixed + first_dims_dot(values, weights.astype(BF16))

        total, mixed = lax.fori_loop(
            0, 8, weight_step,
            (jnp.zeros((1, groups * rows), F32), jnp.zeros((width, groups * rows), F32)),
            unroll=4,
        )
        for later in head_flows[head + 1 : head + 2]:
            run_together(later)
            later[:] = []
        mixed = mixed / total
        r.lse[head] = top + jnp.log(total)
        for g in range(groups):
            first = (head * groups + g) * width
            r.att[:, first : first + width] = mixed[:, g * rows : (g + 1) * rows].T

    def sum_flows(which, pieces=2):
        half = rows // 2
        count = half // pieces
        return [
            tp_sum_flow(
                copies, r.sum_in.at[which], r.sum_out.at[which], r.sum_landed.at[which],
                r.sum_chip.at[which], r.sum_far.at[which], partner_core, partner_far, core,
                piece * count, count, rows,
            )
            for piece in range(pieces)
        ]

    attb = r.att[...].astype(BF16)
    loads["w_o"].wait()
    r.sum_in[0] = dot(attb, r.w_o[...]).astype(BF16)
    flows = step_forward(sum_flows(0))
    for name in ("w_gate", "w_up", "w_down"):
        loads[name].wait()
    r.gob[...] = r.cotangent[...].astype(BF16)
    r.dhid[...] = transposed_dot(r.gob[...], r.w_down[...])
    run_together(flows)
    xmid = r.x[...] + r.sum_out[0].astype(F32)
    r.xmid[...] = xmid

    r2 = rms_scale(xmid)
    xhat2 = xmid * r2
    r.r2[...] = r2
    normed2 = (xhat2 * r.ffn_gain[...]).astype(BF16)
    r.normed2[...] = normed2
    gate = dot(normed2, r.w_gate[...])
    up = dot(normed2, r.w_up[...])
    sig = jax.nn.sigmoid(gate)
    silu = gate * sig
    hid = (silu * up).astype(BF16)
    d_hid = r.dhid[...]
    d_gate = (d_hid * up * sig * (1.0 + gate * (1.0 - sig))).astype(BF16)
    d_up = (d_hid * silu).astype(BF16)
    r.hid[...] = hid
    r.d_gate[...] = d_gate
    r.d_up[...] = d_up
    dn2_part = transposed_dot(d_gate, r.w_gate[...]) + transposed_dot(d_up, r.w_up[...])
    r.ffn_small[...] = jnp.sum(dn2_part * xhat2, axis=0, keepdims=True)
    r.sum_in[1] = dn2_part.astype(BF16)
    sums = step_forward(sum_flows(1))
    r.sum_in[2] = dot(r.hid[...], r.w_down[...]).astype(BF16)
    hidden_sums = sum_flows(2)

    groups_of_flows = {}

    def start(name):
        flows = []
        source, result = getattr(r, "g_" + name), getattr(r, "grad_" + name)
        for (order, first, count), buffers in zip(WEIGHT_PARTS[name], r.weight_buffers[name]):
            columns = pl.ds(first, count)
            flows.append(
                scatter_flow(
                    copies, coords, tp, source.at[:, :, :, :, columns], result.at[:, columns],
                    buffers, order, 0,
                )
            )
        groups_of_flows[name] = step_forward(flows)

    def tick(*names):
        for name in names:
            groups_of_flows[name] = step_forward(groups_of_flows[name])

    sums = step_forward(sums)
    tokens_product(r.normed2, r.d_gate[...], r.g_gate)
    start("gate")
    sums = step_forward(sums)
    hidden_sums = step_forward(hidden_sums)
    tokens_product(r.normed2, r.d_up[...], r.g_up)
    start("up")
    run_together(sums)

    dn2 = r.sum_out[1].astype(F32)
    xhat2 = r.xmid[...] * r.r2[...]
    dmid = r.cotangent[...] + norm_backward(dn2 * r.ffn_gain[...], xhat2, r.r2[...])
    r.dmid[...] = dmid
    dmidb = dmid.astype(BF16)
    r.dmidb[...] = dmidb
    d_att = transposed_dot(dmidb, r.w_o[...])
    r.d_attb[...] = d_att.astype(BF16)
    for head in range(heads_kv):
        pieces = []
        for g in range(groups):
            first = (head * groups + g) * width
            product = d_att[:, first : first + width] * r.att[:, first : first + width]
            pieces.append(jnp.sum(product.T, axis=0, keepdims=True))
        r.delta[head] = jnp.concatenate(pieces, axis=1)
    tick("gate")
    tick("up")
    hidden_sums = step_forward(hidden_sums)

    r.dq_acc[...] = jnp.zeros_like(r.dq_acc)

    def backward_step(head, i):
        head_queries = stacked(r.q_rot, head, groups, width)
        grads = stacked(r.d_attb, head, groups, width)
        base = 2 * head * width
        keys = chunk_of(i, base)
        values = chunk_of(i, base + width)
        scores = masked_scores(keys, head_queries, chunk_starts(i), q_pos, inv_root)
        probs = jnp.exp(scores - r.lse[head])
        d_prob = transposed_dot(values, grads)
        d_scores = (probs * (d_prob - r.delta[head])).astype(BF16)
        d_keys = dot(d_scores, head_queries) * inv_root
        d_values = dot(probs.astype(BF16), grads)
        where = (i // 4, lax.rem(i, 4), slice(None), slice(None))
        shape = (4, rows, width)
        r.dkv[where + (slice(base, base + width),)] = d_keys.astype(BF16).reshape(shape)
        r.dkv[where + (slice(base + width, base + 2 * width),)] = d_values.astype(BF16).reshape(shape)
        r.dq_acc[head] += first_dims_dot(keys, d_scores)

    def backward_range(head, begin, end):
        def body(i, carry):
            backward_step(head, i)
            return carry

        lax.fori_loop(begin, end, body, 0, unroll=4)

    def start_kv(head):
        flows = []
        columns = pl.ds(2 * head * width, 2 * width)
        for (order, first, count), buffers in zip(ROW_PARTS, r.kv_buffers[3 * head : 3 * head + 3]):
            part_rows = pl.ds(first, count)
            flows.append(
                scatter_flow(
                    copies, coords, tp, r.dkv.at[:, :, :, part_rows, columns],
                    r.dkv_own.at[part_rows, columns], buffers, order, 1,
                )
            )
        groups_of_flows["kv%d" % head] = step_forward(flows)

    backward_range(0, 0, 4)
    run_together(hidden_sums)
    tick("gate")
    backward_range(0, 4, 8)
    start_kv(0)
    tick("up", "gate")
    backward_range(1, 0, 4)
    tick("kv0", "up", "gate")
    backward_range(1, 4, 8)
    start_kv(1)
    tick("up")
    r.hidden_out[...] = r.xmid[...] + r.sum_out[2].astype(F32)

    def store(name):
        copy = pltpu.make_async_copy(
            getattr(r, name), getattr(r, name + "_hbm"), r.store_sem.at[r.output_names.index(name)]
        )
        copy.start()
        return copy

    stores = [store("hidden_out")]

    small_q = jnp.zeros((1, width), F32)
    for head in range(heads_kv):
        for g in range(groups):
            index = head * groups + g
            here = slice(index * width, (index + 1) * width)
            grad = rope_back(r.dq_acc[head, :, g * rows : (g + 1) * rows].T * inv_root, cosine, sine)
            hat = r.qhat[:, here]
            small_q = small_q + jnp.sum(grad * hat, axis=0, keepdims=True)
            r.dqb[:, here] = norm_backward(grad * r.query_gain[...], hat, r.rq[index]).astype(BF16)
    tokens_product(r.normed1, r.dqb[...], r.g_query)
    r.dn1[...] = transposed_dot(r.dqb[...], r.w_q[...])
    tick("kv0", "kv1")
    start("query")
    tick("kv0", "kv1")
    tokens_product(r.gob, r.hid[...], r.g_down)
    start("down")
    tick("query")
    tick("kv0", "kv1")
    tokens_product(r.dmidb, r.att[...].astype(BF16), r.g_out)
    start("out")
    tick("down", "query")
    tick("kv0", "kv1")

    small_k = jnp.zeros((1, width), F32)
    for head in range(heads_kv):
        here = slice(head * width, (head + 1) * width)
        base = 2 * head * width
        grad = rope_back(r.dkv_own[:, base : base + width], cosine, sine)
        hat = r.khat[:, here]
        small_k = small_k + jnp.sum(grad * hat, axis=0, keepdims=True)
        r.dvb[:, here] = r.dkv_own[:, base + width : base + 2 * width].astype(BF16)
        r.dkb[:, here] = norm_backward(grad * r.key_gain[...], hat, r.rk[head]).astype(BF16)
    dn1_part = (
        r.dn1[...] + transposed_dot(r.dkb[...], r.w_k[...]) + transposed_dot(r.dvb[...], r.w_v[...])
    )
    xhat1 = r.x[...] * r.r1[...]
    r.sum_in[3] = dn1_part.astype(BF16)
    sums = step_forward(sum_flows(3))
    r.small_in[0:1, 0:1024] = jnp.sum(dn1_part * xhat1, axis=0, keepdims=True)
    r.small_in[0:1, 1024:2048] = r.ffn_small[...]
    r.small_in[0:1, 2048:2176] = small_q
    r.small_in[0:1, 2176:2304] = small_k
    groups_of_flows["small"] = step_forward(
        [sum_everywhere_flow(copies, coords, tp, r.small_in, r.small_out, r.small_slots)]
    )
    tokens_product(r.normed1, r.dkb[...], r.g_key)
    start("key")
    sums = step_forward(sums)
    tokens_product(r.normed1, r.dvb[...], r.g_value)
    start("value")
    tick("small", "key", "value", "query", "down", "out")
    run_together(sums)
    flows = []
    dn1 = r.sum_out[3].astype(F32)
    r.input_gradient[...] = r.dmid[...] + norm_backward(
        dn1 * r.attention_gain[...], r.x[...] * r.r1[...], r.r1[...]
    )
    stores.append(store("input_gradient"))
    for name in ("small", "key", "value", "query", "down", "out", "up", "gate", "kv0", "kv1"):
        flows = flows + groups_of_flows.pop(name)
    assert not any(groups_of_flows.values())
    run_together(flows)
    stores += [store(name) for name in r.output_names if name not in ("hidden_out", "input_gradient")]
    copies.drain()
    assert (copies.sends, copies.count) == (SENDS, RECEIVES)
    for copy in stores:
        copy.wait()


SENDS, RECEIVES = 90, 262
WEIGHT_NAMES = ("w_k", "w_v", "w_q", "w_o", "w_gate", "w_up", "w_down")


def whole_layer(
    layer_input, cotangent, weights, gains, cosine, sine, positions, heads_kv, groups
):
    rows, features = layer_input.shape
    width = cosine.shape[1]
    heads_q = heads_kv * groups
    q_width, kv_width = heads_q * width, heads_kv * width
    hidden = weights["w_gate"].shape[1]
    hbm = pl.BlockSpec(memory_space=pl.ANY)
    inputs = {
        "x": layer_input, "cotangent": cotangent, "cosine": cosine, "sine": sine,
        "positions": positions, **gains,
    }
    columns = {
        "gate": hidden, "up": hidden, "down": hidden, "out": q_width,
        "query": q_width, "key": kv_width, "value": kv_width,
    }
    outputs = {
        "hidden_out": ((rows, features), F32),
        "input_gradient": ((rows, features), F32),
        "small_out": ((1, 2304), F32),
    }
    for name, count in columns.items():
        outputs["grad_" + name] = ((32, count), F32)
    scratch = {
        "send_sem": pltpu.SemaphoreType.DMA((SENDS,)),
        "recv_sem": pltpu.SemaphoreType.DMA((RECEIVES,)),
        "load_sem": pltpu.SemaphoreType.DMA((len(WEIGHT_NAMES) + len(inputs),)),
        "store_sem": pltpu.SemaphoreType.DMA((len(outputs),)),
    }
    for name in WEIGHT_NAMES:
        scratch[name] = pltpu.VMEM(weights[name].shape, BF16)
    for name, shape, kind in (
        ("normed1", (rows, features), BF16),
        ("normed2", (rows, features), BF16),
        ("gob", (rows, features), BF16),
        ("dmidb", (rows, features), BF16),
        ("r1", (rows, 1), F32),
        ("r2", (rows, 1), F32),
        ("rq", (heads_q, rows, 1), F32),
        ("rk", (heads_kv, rows, 1), F32),
        ("qhat", (rows, q_width), F32),
        ("khat", (rows, kv_width), F32),
        ("q_rot", (rows, q_width), BF16),
        ("kv_all", (2, 4, 4, rows, 2 * kv_width), BF16),
        ("pos_all", (2, 4, 4, 1, 256), jnp.int32),
        ("scores", (32 * rows, groups * rows), F32),
        ("lse", (heads_kv, 1, groups * rows), F32),
        ("delta", (heads_kv, 1, groups * rows), F32),
        ("att", (rows, q_width), F32),
        ("sum_in", (4, rows, features), BF16),
        ("sum_out", (4, rows, features), BF16),
        ("sum_landed", (4, rows // 2, features), BF16),
        ("sum_chip", (4, rows // 2, features), BF16),
        ("sum_far", (4, rows // 2, features), BF16),
        ("xmid", (rows, features), F32),
        ("dmid", (rows, features), F32),
        ("dn1", (rows, features), F32),
        ("dhid", (rows, hidden), F32),
        ("hid", (rows, hidden), BF16),
        ("d_gate", (rows, hidden), BF16),
        ("d_up", (rows, hidden), BF16),
        ("ffn_small", (1, features), F32),
        ("d_attb", (rows, q_width), BF16),
        ("dq_acc", (heads_kv, width, groups * rows), F32),
        ("dkv", (2, 4, 4, rows, 2 * kv_width), BF16),
        ("dkv_own", (rows, 2 * kv_width), F32),
        ("dqb", (rows, q_width), BF16),
        ("dkb", (rows, kv_width), BF16),
        ("dvb", (rows, kv_width), BF16),
        ("small_in", (1, 2304), F32),
    ):
        scratch[name] = pltpu.VMEM(shape, kind)
    for name, count in columns.items():
        scratch["g_" + name] = pltpu.VMEM((2, 4, 4, 32, count), BF16)
    lists = {"small_slots": sum_everywhere_scratch((1, 2304))}
    for name, count in columns.items():
        for i, (order, first, size) in enumerate(WEIGHT_PARTS[name]):
            lists["%s_%d" % (name, i)] = scatter_scratch((32, size), order, 0)
    for i, (order, first, count) in enumerate(ROW_PARTS):
        for head in range(heads_kv):
            lists["kv_%d_%d" % (head, i)] = scatter_scratch((count, 2 * width), order, 1)

    load_names = tuple(inputs) + WEIGHT_NAMES
    for name, value in inputs.items():
        scratch[name] = pltpu.VMEM(value.shape, value.dtype)
    for name, (shape, kind) in outputs.items():
        scratch[name] = pltpu.VMEM(shape, kind)
    input_names = [name + "_hbm" for name in load_names]
    flat_scratch = list(scratch.values())
    for buffers in lists.values():
        flat_scratch.extend(buffers)

    def kernel(*refs):
        r = types.SimpleNamespace()
        r.input_names = tuple(inputs)
        r.output_names = tuple(outputs)
        names = input_names + [name + "_hbm" for name in outputs] + list(scratch)
        for name, ref in zip(names, refs):
            setattr(r, name, ref)
        rest = list(refs[len(names) :])
        groups_of = {}
        for name, buffers in lists.items():
            groups_of[name], rest = rest[: len(buffers)], rest[len(buffers) :]
        r.small_slots = groups_of["small_slots"]
        r.weight_buffers = {
            name: [groups_of["%s_%d" % (name, i)] for i in range(len(WEIGHT_PARTS[name]))]
            for name in columns
        }
        r.kv_buffers = [
            groups_of["kv_%d_%d" % (head, i)]
            for head in range(heads_kv)
            for i in range(len(ROW_PARTS))
        ]
        layer_kernel(r, (heads_kv, groups, width))

    results = pl.pallas_call(
        kernel,
        out_shape=tuple(jax.ShapeDtypeStruct(shape, kind) for shape, kind in outputs.values()),
        in_specs=[hbm] * len(load_names),
        out_specs=(hbm,) * len(outputs),
        scratch_shapes=flat_scratch,
        compiler_params=pltpu.CompilerParams(
            collective_id=0, has_side_effects=True, vmem_limit_bytes=67043328
        ),
        name="whole_layer",
    )(*inputs.values(), *[weights[name] for name in WEIGHT_NAMES])
    return dict(zip(outputs, results))


def body(
    layer_input,
    positions,
    attention_norm_gain,
    w_query,
    key_projection,
    value_projection,
    query_norm,
    key_norm_gain,
    output_projection,
    feedforward_norm_gain,
    w_gate,
    w_up,
    w_down,
    output_cotangent,
):
    head_dim = query_norm.shape[0]
    heads_q = w_query.shape[1] // head_dim
    heads_kv = key_projection.shape[1] // head_dim
    groups = heads_q // heads_kv
    cosine, sine = rope_tables(positions, head_dim)
    out = whole_layer(
        layer_input,
        output_cotangent,
        {
            "w_q": w_query, "w_k": key_projection, "w_v": value_projection, "w_o": output_projection,
            "w_gate": w_gate, "w_up": w_up, "w_down": w_down,
        },
        {
            "attention_gain": attention_norm_gain.reshape(1, -1),
            "ffn_gain": feedforward_norm_gain.reshape(1, -1),
            "query_gain": query_norm.reshape(1, -1),
            "key_gain": key_norm_gain.reshape(1, -1),
        },
        cosine,
        sine,
        positions.reshape(1, -1),
        heads_kv,
        groups,
    )
    names = (
        "hidden_out", "input_gradient", "grad_query", "grad_key", "grad_value", "grad_out",
        "grad_gate", "grad_up", "grad_down", "small_out",
    )
    written = write_results([out[name] for name in names], (1024, 1024, 128, 128))
    done = dict(zip(names[:-1], written))
    small = [piece.reshape(-1) for piece in written[len(names) - 1 :]]
    return (
        done["hidden_out"],
        done["input_gradient"],
        small[0],
        done["grad_query"],
        done["grad_key"],
        done["grad_value"],
        small[2],
        small[3],
        done["grad_out"].T,
        small[1],
        done["grad_gate"],
        done["grad_up"],
        done["grad_down"].T,
    )


def solution(mesh):
    return jax.shard_map(
        body,
        mesh=mesh,
        in_specs=(
            P("ctx", None),
            P("ctx"),
            P(),
            P(None, "tp"),
            P(None, "tp"),
            P(None, "tp"),
            P(),
            P(),
            P("tp", None),
            P(),
            P(None, "tp"),
            P(None, "tp"),
            P("tp", None),
            P("ctx", None),
        ),
        out_specs=(
            P("ctx", None),
            P("ctx", None),
            P(),
            P("ctx", "tp"),
            P("ctx", "tp"),
            P("ctx", "tp"),
            P(),
            P(),
            P("tp", "ctx"),
            P(),
            P("ctx", "tp"),
            P("ctx", "tp"),
            P("tp", "ctx"),
        ),
        check_vma=False,
    )
```
